32 devices in a mesh: wide: 8 (over y, x, core), narrow: 4 (over z).
Axes of the slice: x: 2, y: 2, z: 4, core: 2. Of those that a mesh axis runs over, the one named last changes fastest.
Arguments:
- tokens: bfloat16 [64, 208, 768], P('wide'), may hold values from -6 to 6
- grid_shape: int32 [64, 2], P('wide'), may hold values from 8 to 24, as said below
- first_gain: bfloat16 [768], replicated, may hold values from 0.5 to 1.5
- first_shift: bfloat16 [768], replicated, may hold values from -1.1953125 to 1.1953125
- qkv_weight: bfloat16 [3, 768, 768], P(None, None, 'narrow'), may hold values from -0.21875 to 0.21875
- query_bias: bfloat16 [768], P('narrow'), may hold values from -1.796875 to 1.796875
- value_bias: bfloat16 [768], P('narrow'), may hold values from -0.59765625 to 0.59765625
- rel_table: bfloat16 [12, 2212], P('narrow'), may hold values from -5 to 5
- proj_weight: bfloat16 [768, 768], P('narrow'), may hold values from -1.25 to 1.25
- proj_bias: bfloat16 [768], replicated, may hold values from -1.796875 to 1.796875
- attn_scale: bfloat16 [768], replicated, may hold values from 0.25 to 1.75
- second_gain: bfloat16 [768], replicated, may hold values from 0.5 to 1.5
- second_shift: bfloat16 [768], replicated, may hold values from -1.1953125 to 1.1953125
- up_weight: bfloat16 [768, 3072], P(None, 'narrow'), may hold values from -0.21875 to 0.21875
- up_bias: bfloat16 [3072], P('narrow'), may hold values from -3 to 3
- down_weight: bfloat16 [3072, 768], P('narrow'), may hold values from -0.15625 to 0.15625
- down_bias: bfloat16 [768], replicated, may hold values from -1.796875 to 1.796875
- mlp_scale: bfloat16 [768], replicated, may hold values from 0.25 to 1.75
- cotangent: bfloat16 [64, 208, 768], P('wide'), may hold values from -6 to 6
Outputs:
- layer_out: bfloat16 [64, 208, 768], P('wide')
- tokens_grad: float32 [64, 208, 768], P('wide')
- first_gain_grad: float32 [768], replicated
- first_shift_grad: float32 [768], replicated
- qkv_weight_grad: float32 [3, 768, 768], P(None, None, 'narrow')
- query_bias_grad: float32 [768], P('narrow')
- value_bias_grad: float32 [768], P('narrow')
- rel_table_grad: float32 [12, 2212], P('narrow')
- proj_weight_grad: float32 [768, 768], P('narrow')
- proj_bias_grad: float32 [768], replicated
- attn_scale_grad: float32 [768], replicated
- second_gain_grad: float32 [768], replicated
- second_shift_grad: float32 [768], replicated
- up_weight_grad: float32 [768, 3072], P(None, 'narrow')
- up_bias_grad: float32 [3072], P('narrow')
- down_weight_grad: float32 [3072, 768], P('narrow')
- down_bias_grad: float32 [768], replicated
- mlp_scale_grad: float32 [768], replicated
The draws below stay inside these ranges and needn't reach their ends.
Inputs may be any that keep to these rules, and one draw needn't show every extreme that they name: `grid_shape`: each row is (height, width) of one image's patch grid, one of 14 x 14, 10 x 20, 20 x 10, 8 x 24, 24 x 8, 12 x 16, 16 x 12, 13 x 15; each of these occurs in every draw.
All inputs are finite; a program needn't handle non-finite values.
Results may differ from the reference program's by a relative error of at most 0.013.
Values sent between devices are 32-bit elements; how exact they have to be, the bound alone decides.
A program may use at most 384 MiB of HBM per device.

```python
import jax
import jax.numpy as jnp
from jax import lax

D = 768
H = 12
HD = 64
FF = 3072
SLOTS = 208
MAXG = 24
REL = 2212
IMAGES = 64


def draw_grid_shape(key, part):
    shape_table = jnp.array([[14, 14], [10, 20], [20, 10], [8, 24], [24, 8], [12, 16], [16, 12], [13, 15]], dtype=jnp.int32)
    shuffled = jax.random.permutation(key, IMAGES)
    return shape_table[shuffled % 8]


def block_scale(own_key, dims, split, low, largest):
    loudness, own = 1.0, jax.random.fold_in(own_key, 6)
    for axis_at, parts in split:
        steps = jnp.exp(jax.random.uniform(jax.random.fold_in(own, axis_at), (parts,), jnp.float32, low / len(split), largest / len(split)))
        loudness = loudness * jnp.repeat(steps, dims[axis_at] // parts).reshape([-1 if axis == axis_at else 1 for axis in range(len(dims))])
    return loudness


def scatter_about(key, extent, width, bound, cuts=(), held_as=jnp.bfloat16):
    result = jax.random.normal(key, extent, jnp.float32) * width
    if len(cuts) > 0:
        result = block_scale(key, extent, cuts, -0.22, 0.18) * result
    return jnp.clip(result, min=-bound, max=bound).astype(held_as)


def setup_inputs(seed: int = 0) -> dict:
    streams_of = jax.random.split(jax.random.key(seed), 20)
    return {
        "tokens": scatter_about(streams_of[0], (IMAGES, SLOTS, D), 1.0, 6.0, ((0, 8),)),
        "grid_shape": draw_grid_shape(jax.random.fold_in(streams_of[19], 71), 0),
        "first_gain": jnp.clip(1.0 + 0.1 * jax.random.normal(streams_of[2], (D,), jnp.float32), 0.5, 1.5).astype(jnp.bfloat16),
        "first_shift": scatter_about(streams_of[3], (D,), 0.2, 1.1953125),
        "qkv_weight": scatter_about(streams_of[4], (3, D, D), D ** -0.5, 0.21875, ((2, 4),)),
        "query_bias": scatter_about(streams_of[5], (D,), 0.3, 1.796875, ((0, 4),)),
        "value_bias": scatter_about(streams_of[6], (D,), 0.1, 0.59765625, ((0, 4),)),
        "rel_table": scatter_about(streams_of[7], (H, REL), 1.0, 5.0, ((0, 4),)),
        "proj_weight": scatter_about(streams_of[8], (D, D), (D // 32) ** -0.5, 1.25, ((0, 4),)),
        "proj_bias": scatter_about(streams_of[9], (D,), 0.3, 1.796875),
        "attn_scale": jnp.clip(1.0 + 0.15 * jax.random.normal(streams_of[10], (D,), jnp.float32), 0.25, 1.75).astype(jnp.bfloat16),
        "second_gain": jnp.clip(1.0 + 0.1 * jax.random.normal(streams_of[11], (D,), jnp.float32), 0.5, 1.5).astype(jnp.bfloat16),
        "second_shift": scatter_about(streams_of[12], (D,), 0.2, 1.1953125),
        "up_weight": scatter_about(streams_of[13], (D, FF), D ** -0.5, 0.21875, ((1, 4),)),
        "up_bias": scatter_about(streams_of[14], (FF,), 0.5, 3.0, ((0, 4),)),
        "down_weight": scatter_about(streams_of[15], (FF, D), (FF // 2) ** -0.5, 0.15625, ((0, 4),)),
        "down_bias": scatter_about(streams_of[16], (D,), 0.3, 1.796875),
        "mlp_scale": jnp.clip(1.0 + 0.15 * jax.random.normal(streams_of[17], (D,), jnp.float32), 0.25, 1.75).astype(jnp.bfloat16),
        "cotangent": scatter_about(streams_of[18], (IMAGES, SLOTS, D), 1.0, 6.0, ((0, 8),)),
    }


EPSILON = 1e-06
NEG_LARGE = -1000000000.0
HIGHEST = lax.Precision.HIGHEST

@jax.custom_vjp
def low(v):
    return lax.optimization_barrier(v.astype(jnp.bfloat16)).astype(jnp.float32)

@jax.custom_vjp
def low_back(v):
    return v

def low_keep(v):
    return (low(v), None)

def low_pass(kept, grad):
    return (grad,)

def back_keep(v):
    return (v, None)

def back_low(kept, grad):
    return (low(grad),)
low.defvjp(low_keep, low_pass)
low_back.defvjp(back_keep, back_low)

def slot_layout(grid_shape, slot_count):
    slot_ids = jnp.arange(slot_count, dtype=jnp.int32)
    patch_ids = slot_ids - 1
    grid_height = grid_shape[:, 0:1].astype(jnp.int32)
    grid_width = grid_shape[:, 1:2].astype(jnp.int32)
    is_valid = slot_ids[None, :] <= grid_height * grid_width
    row_place = jnp.floor_divide(patch_ids[None, :], grid_width)
    col_place = patch_ids[None, :] - row_place * grid_width
    span_size = 2 * MAXG - 1
    row_delta = row_place[:, :, None] - row_place[:, None, :] + (MAXG - 1)
    col_delta = col_place[:, :, None] - col_place[:, None, :] + (MAXG - 1)
    pair_index = row_delta * span_size + col_delta
    is_patch = jnp.logical_and(slot_ids[None, :] >= 1, is_valid)
    is_class = jnp.broadcast_to(slot_ids[None, :] == 0, is_patch.shape)
    both_patch = jnp.logical_and(is_patch[:, :, None], is_patch[:, None, :])
    class_query = jnp.logical_and(is_class[:, :, None], is_patch[:, None, :])
    class_key = jnp.logical_and(is_patch[:, :, None], is_class[:, None, :])
    last_entry = span_size * span_size
    pair_index = jnp.where(both_patch, pair_index, jnp.where(class_query, last_entry, jnp.where(class_key, last_entry + 1, last_entry + 2)))
    return (pair_index.astype(jnp.int32), is_valid)

def layer_norm(values, gain, shift):
    centre = lax.optimization_barrier(jnp.mean(values, axis=-1, keepdims=True))
    centred = values - centre
    spread = lax.optimization_barrier(jnp.mean(centred * centred, axis=-1, keepdims=True))
    return centred * lax.rsqrt(spread + EPSILON) * gain + shift

def matmul(left, right):
    return jnp.dot(left, right, precision=HIGHEST)

def one_layer(params, block_in, block_index, block_valid):
    first_gain, first_shift, qkv_weight, query_bias, value_bias, rel_table, proj_weight, proj_bias, attn_scale, second_gain, second_shift, up_weight, up_bias, down_weight, down_bias, mlp_scale = params
    count_images = block_in.shape[0]
    flat_in = block_in.reshape(count_images * SLOTS, D)
    first_in = low(layer_norm(flat_in, first_gain, first_shift))
    queries = low(low_back((matmul(first_in, qkv_weight[0]) + query_bias) * HD ** (-0.5)))
    keys_low = low(low_back(matmul(first_in, qkv_weight[1])))
    values_low = low(low_back(matmul(first_in, qkv_weight[2]) + value_bias))
    head_split = (count_images, SLOTS, H, HD)
    raw_scores = low_back(jnp.einsum('ishd,ithd->ihst', queries.reshape(head_split), keys_low.reshape(head_split), precision=HIGHEST))
    table_bias = jnp.transpose(jnp.take(rel_table, block_index, axis=1), (1, 0, 2, 3))
    scores = jnp.where(block_valid[:, None, None, :], raw_scores + table_bias, NEG_LARGE)
    probs_low = low(jax.nn.softmax(scores, axis=-1))
    attended = jnp.einsum('ihst,ithd->ishd', probs_low, values_low.reshape(head_split), precision=HIGHEST)
    attended = low(low_back(attended.reshape(count_images * SLOTS, D)))
    attn_branch = low_back(matmul(attended, proj_weight)) + proj_bias
    middle = flat_in + attn_scale * attn_branch
    second_in = low(layer_norm(middle, second_gain, second_shift))
    up_pre = low_back(matmul(second_in, up_weight) + up_bias)
    hidden = low(jax.nn.gelu(up_pre, approximate=False))
    mlp_branch = low_back(matmul(hidden, down_weight)) + down_bias
    return (middle + mlp_scale * mlp_branch).reshape(block_in.shape)

def reference(tokens, grid_shape, first_gain, first_shift, qkv_weight, query_bias, value_bias, rel_table, proj_weight, proj_bias, attn_scale, second_gain, second_shift, up_weight, up_bias, down_weight, down_bias, mlp_scale, cotangent):
    float_type = jnp.float32
    params = tuple((entry.astype(float_type) for entry in (first_gain, first_shift, qkv_weight, query_bias, value_bias, rel_table, proj_weight, proj_bias, attn_scale, second_gain, second_shift, up_weight, up_bias, down_weight, down_bias, mlp_scale)))
    pair_index, is_valid = slot_layout(grid_shape, SLOTS)
    group_count = IMAGES // 8
    x_groups = tokens.astype(float_type).reshape(group_count, 8, SLOTS, D)
    index_groups = pair_index.reshape(group_count, 8, SLOTS, SLOTS)
    valid_groups = is_valid.reshape(group_count, 8, SLOTS)

    def forward(inputs, weights):

        def group_step(packed):
            block_in, block_index, block_valid = packed
            return one_layer(weights, block_in, block_index, block_valid)
        return lax.map(jax.checkpoint(group_step), (inputs, index_groups, valid_groups))
    layer_out, pullback = jax.vjp(forward, x_groups, params)
    out_grad = cotangent.astype(float_type).reshape(group_count, 8, SLOTS, D) * valid_groups[..., None].astype(float_type)
    tokens_grad, param_grads = pullback(out_grad)
    first_gain_grad, first_shift_grad, qkv_weight_grad, query_bias_grad, value_bias_grad, rel_table_grad, proj_weight_grad, proj_bias_grad, attn_scale_grad, second_gain_grad, second_shift_grad, up_weight_grad, up_bias_grad, down_weight_grad, down_bias_grad, mlp_scale_grad = param_grads
    return (layer_out.reshape(IMAGES, SLOTS, D).astype(jnp.bfloat16), tokens_grad.reshape(IMAGES, SLOTS, D), first_gain_grad, first_shift_grad, qkv_weight_grad, query_bias_grad, value_bias_grad, rel_table_grad, proj_weight_grad, proj_bias_grad, attn_scale_grad, second_gain_grad, second_shift_grad, up_weight_grad, up_bias_grad, down_weight_grad, down_bias_grad, mlp_scale_grad)
```

```python
import functools

import jax
import jax.numpy as jnp
from jax import lax
from jax.experimental import pallas as pl
from jax.experimental.pallas import tpu as pltpu
from jax.sharding import PartitionSpec as P

HD = 64
MAXG = 24
SPAN = 2 * MAXG - 1
EPSILON = 1e-06
MASKED = -1e30
INV_ROOT_TWO = 0.7071067811865476
INV_ROOT_TWO_PI = 0.3989422804014327
GRIDS = ((14, 14), (10, 20), (20, 10), (8, 24), (24, 8), (12, 16), (16, 12), (13, 15))
DIAG = 512
F32 = jnp.float32
BF16 = jnp.bfloat16
VMEM_LIMIT = 60 * 1024 * 1024


def dot_nn(a, b):
    return lax.dot_general(a, b, (((1,), (0,)), ((), ())), preferred_element_type=F32)


def dot_nt(a, b):
    return lax.dot_general(a, b, (((1,), (1,)), ((), ())), preferred_element_type=F32)


def dot_tn(a, b):
    return lax.dot_general(a, b, (((0,), (0,)), ((), ())), preferred_element_type=F32)


def row_mean(v):
    return jnp.sum(v, axis=-1, keepdims=True) * (1.0 / v.shape[-1])


def norm_stats(v):
    centred = v - row_mean(v)
    inv = lax.rsqrt(row_mean(centred * centred) + EPSILON)
    return centred * inv, inv


def norm_back(incoming, normed, inv, gain):
    scaled = incoming * gain
    return inv * (scaled - row_mean(scaled) - normed * row_mean(scaled * normed))


def fold_rows(v):
    rows = v.shape[0]
    return jnp.sum(v.reshape(rows // 8, 8, v.shape[1]), axis=0)


def windows(shape_at):
    high, wide = GRIDS[shape_at]
    centre = MAXG - 1
    for m in range(-high, high):
        at = 207 + m * wide
        if m > -high:
            yield 0, centre + m, centre, at, wide
        if m < high - 1:
            yield 1, centre + 1 + m, centre + 1 - wide, at + 1, wide - 1


def diag_kernel(table_ref, out_ref):
    out_ref[...] = jnp.zeros_like(out_ref)
    for shape_at in range(len(GRIDS)):
        for which, row, col, at, size in windows(shape_at):
            out_ref[shape_at, which, :, at : at + size] = table_ref[row, :, col : col + size]


def undiag_kernel(diag_ref, out_ref):
    out_ref[...] = jnp.zeros_like(out_ref)
    for shape_at in range(len(GRIDS)):
        for which, row, col, at, size in windows(shape_at):
            out_ref[row, :, col : col + size] += diag_ref[shape_at, which, :, at : at + size]


def slot_masks(high, wide, reverse):
    rows = lax.broadcasted_iota(jnp.int32, (208, 1), 0)
    p = 207 - rows if reverse else rows
    s = lax.broadcasted_iota(jnp.int32, (1, 256), 1)
    limit = high * wide
    wide_f = wide.astype(F32)

    def column(slot):
        patch = (slot - 1).astype(F32)
        return patch - wide_f * jnp.floor((patch + 0.5) / wide_f)

    later = column(s) >= column(p)
    p_patch = (p >= 1) & (p <= limit)
    s_patch = (s >= 1) & (s <= limit)
    return p, s, limit, later, p_patch, s_patch


def load_pieces(pidx_ref, pieces, stage, sems, rows):
    copies = []
    for r, piece in enumerate(pieces):
        at = pl.multiple_of(pidx_ref[r] * rows, 8)
        copies.append(
            pltpu.make_async_copy(piece, stage.at[:, pl.ds(at, rows), :], sems.at[r])
        )
    for copy in copies:
        copy.start()
    return copies


def attention_forward(
    sid_ref, grid_ref, pidx_ref, tok_ref, gain_ref, shift_ref, qb_ref, vb_ref, pb_ref, own_ref, diag_ref, cls_ref,
    *rest,
):
    pieces = rest[:8]
    q_ref, k_ref, v_ref, prob_ref, att_ref, branch_ref, wa_ref = rest[8:15]
    stage, k_pad, v_pad, sems = rest[15:]
    image = pl.program_id(0)

    @pl.when(image == 0)
    def _():
        copies = load_pieces(pidx_ref, pieces, stage, sems, 96)
        k_pad[208:256, :] = jnp.zeros((48, 768), BF16)
        v_pad[208:256, :] = jnp.zeros((48, 768), BF16)
        for part in range(4):
            wa_ref[part, 0:192, :] = own_ref[part * 192 : (part + 1) * 192, :]
        for copy in copies:
            copy.wait()
        for slot in range(3):
            for part in range(4):
                wa_ref[part, (slot + 1) * 192 : (slot + 2) * 192, :] = stage[
                    slot, part * 192 : (part + 1) * 192, :
                ].astype(BF16)

    normed, _ = norm_stats(tok_ref[0].astype(F32))
    first_in = (normed * gain_ref[...] + shift_ref[...]).astype(BF16)
    q_ref[0] = ((dot_nt(first_in, wa_ref[0]) + qb_ref[...]) * (HD ** -0.5)).astype(BF16)
    keys = dot_nt(first_in, wa_ref[1]).astype(BF16)
    k_ref[0] = keys
    k_pad[0:208, :] = keys
    values = (dot_nt(first_in, wa_ref[2]) + vb_ref[...]).astype(BF16)
    v_ref[0] = values
    v_pad[0:208, :] = values

    p, s, limit, later, p_patch, s_patch = slot_masks(grid_ref[image, 0], grid_ref[image, 1], False)
    both = p_patch & s_patch
    open_key = s <= limit
    head_of = lax.broadcasted_iota(jnp.int32, (1, 256), 1) // HD

    @pl.loop(0, 3)
    def _(group):
        lanes = pl.ds(pl.multiple_of(group * 256, 256), 256)
        q_group = q_ref[0, :, lanes]
        k_group = k_pad[:, lanes]
        v_group = v_pad[:, lanes]
        stacked = jnp.concatenate(
            [jnp.where(head_of == h, q_group, jnp.zeros_like(q_group)) for h in range(4)], axis=0
        )
        raw = dot_nt(stacked, k_group)
        probs = []
        for h in range(4):
            head = group * 4 + h
            f0 = diag_ref[0, 0, pl.ds(head, 1), :]
            f1 = diag_ref[0, 1, pl.ds(head, 1), :]
            toep0 = pltpu.roll(jnp.broadcast_to(f0, (208, DIAG)), DIAG - 207, 1, stride=1, stride_axis=0)[:, :256]
            toep1 = pltpu.roll(jnp.broadcast_to(f1, (208, DIAG)), DIAG - 207, 1, stride=1, stride_axis=0)[:, :256]
            c0, c1, c2 = cls_ref[head, 0], cls_ref[head, 1], cls_ref[head, 2]
            outer = jnp.where((p == 0) & s_patch, c0, jnp.where(p_patch & (s == 0), c1, c2))
            bias = jnp.where(both, jnp.where(later, toep0, toep1), outer)
            scores = jnp.where(open_key, raw[h * 208 : (h + 1) * 208, :] + bias, MASKED)
            top = jnp.max(scores, axis=-1, keepdims=True)
            raised = jnp.exp(scores - top)
            prob = (raised * (1.0 / jnp.sum(raised, axis=-1, keepdims=True))).astype(BF16)
            prob_ref[0, head] = prob
            probs.append(prob)
        mixed = dot_nn(jnp.concatenate(probs, axis=0), v_group)
        out = mixed[0:208]
        for h in range(1, 4):
            out = jnp.where(head_of == h, mixed[h * 208 : (h + 1) * 208], out)
        att_ref[0, :, lanes] = out.astype(BF16)

    branch_ref[0] = dot_nn(att_ref[0], wa_ref[3]) + pb_ref[...]


def feed_forward(
    grid_ref, pidx_ref, tok_ref, branch_ref, cot_ref, vec_ref, ub_ref, ownb_ref, ownc_ref, *rest
):
    pieces_b, pieces_c = rest[:8], rest[8:16]
    out_ref, mg_ref, gb_ref, gc_ref, sums_ref = rest[16:21]
    stage, wb, wc, mlp_acc, second_acc, sems = rest[21:]
    image = pl.program_id(0)

    @pl.when(image == 0)
    def _():
        for own_ref, pieces, weights in ((ownb_ref, pieces_b, wb), (ownc_ref, pieces_c, wc)):
            copies = load_pieces(pidx_ref, pieces, stage, sems, 96)
            weights[0] = own_ref[...]
            for copy in copies:
                copy.wait()
            for slot in range(3):
                weights[slot + 1] = stage[slot].astype(BF16)
        gb_ref[...] = jnp.zeros_like(gb_ref)
        gc_ref[...] = jnp.zeros_like(gc_ref)
        sums_ref[...] = jnp.zeros_like(sums_ref)

    attn_scale, second_gain, second_shift, mlp_scale, down_bias = (vec_ref[i : i + 1, :] for i in range(5))
    branch = branch_ref[0]
    middle = tok_ref[0].astype(F32) + attn_scale * branch
    normed, inv = norm_stats(middle)
    second_in = (normed * second_gain + second_shift).astype(BF16)
    valid = lax.broadcasted_iota(jnp.int32, (208, 1), 0) <= grid_ref[image, 0] * grid_ref[image, 1]
    out_grad = jnp.where(valid, cot_ref[0].astype(F32), 0.0)
    branch_low = (out_grad * mlp_scale).astype(BF16)
    mlp_acc[...] = jnp.zeros_like(mlp_acc)
    second_acc[...] = jnp.zeros_like(second_acc)

    @pl.loop(0, 4)
    def _(slot):
        up_pre = dot_nn(second_in, wb[slot]) + ub_ref[pl.ds(slot, 1), :]
        cdf = 0.5 * (1.0 + lax.erf(up_pre * INV_ROOT_TWO))
        hidden = (up_pre * cdf).astype(BF16)
        slope = cdf + up_pre * jnp.exp(-0.5 * up_pre * up_pre) * INV_ROOT_TWO_PI
        mlp_acc[...] += dot_nn(hidden, wc[slot])
        pre_low = (dot_nt(branch_low, wc[slot]) * slope).astype(BF16)
        second_acc[...] += dot_nt(pre_low, wb[slot])

        @pl.when(slot == 0)
        def _():
            gc_ref[...] += dot_tn(hidden, branch_low)
            gb_ref[...] += dot_tn(second_in, pre_low)
            sums_ref[6] += fold_rows(pre_low.astype(F32))

    mlp_branch = mlp_acc[...] + down_bias
    out_ref[0] = (middle + mlp_scale * mlp_branch).astype(BF16)
    second_grad = second_acc[...]
    middle_grad = out_grad + norm_back(second_grad, normed, inv, second_gain)
    mg_ref[0] = middle_grad
    sums_ref[0] += fold_rows(out_grad * mlp_branch)
    sums_ref[1] += fold_rows(out_grad)
    sums_ref[2] += fold_rows(second_grad * normed)
    sums_ref[3] += fold_rows(second_grad)
    sums_ref[4] += fold_rows(middle_grad * branch)
    sums_ref[5] += fold_rows(middle_grad)


def attention_backward(
    sid_ref, grid_ref, tok_ref, mg_ref, att_ref, q_ref, k_ref, v_ref, prob_ref, vec_ref, wa_ref,
    tg_ref, ga_ref, sums_ref, diag_ref, cls_ref,
    k_pad, v_pad, dq, dk, dv,
):
    image = pl.program_id(0)

    @pl.when(image == 0)
    def _():
        k_pad[208:256, :] = jnp.zeros((48, 768), BF16)
        v_pad[208:256, :] = jnp.zeros((48, 768), BF16)
        ga_ref[...] = jnp.zeros_like(ga_ref)
        sums_ref[...] = jnp.zeros_like(sums_ref)
        diag_ref[...] = jnp.zeros_like(diag_ref)
        cls_ref[...] = jnp.zeros_like(cls_ref)

    k_pad[0:208, :] = k_ref[0]
    v_pad[0:208, :] = v_ref[0]
    attn_scale, first_gain, first_shift = (vec_ref[i : i + 1, :] for i in range(3))
    middle_grad = mg_ref[0]
    attn_low = (middle_grad * attn_scale).astype(BF16)
    attended_grad = dot_nt(attn_low, wa_ref[3]).astype(BF16)
    ga_ref[576:768, :] += dot_tn(att_ref[0], attn_low)[0:192, :]

    p, s, limit, later, p_patch, s_patch = slot_masks(grid_ref[image, 0], grid_ref[image, 1], True)
    both = p_patch & s_patch
    flip = (
        lax.broadcasted_iota(jnp.int32, (208, 208), 0) + lax.broadcasted_iota(jnp.int32, (208, 208), 1) == 207
    ).astype(BF16)
    head_of = lax.broadcasted_iota(jnp.int32, (1, 256), 1) // HD

    for group in range(3):
        lanes = slice(group * 256, group * 256 + 256)
        k_group, v_group = k_pad[:, lanes], v_pad[:, lanes]
        q_group = q_ref[0, :, lanes]
        g_group = attended_grad[:, lanes]
        q_stack = jnp.concatenate(
            [jnp.where(head_of == h, q_group, jnp.zeros_like(q_group)) for h in range(4)], axis=0
        )
        g_stack = jnp.concatenate(
            [jnp.where(head_of == h, g_group, jnp.zeros_like(g_group)) for h in range(4)], axis=0
        )
        prob_grads = dot_nt(g_stack, v_group)
        lows = []
        for h in range(4):
            prob = prob_ref[0, group * 4 + h].astype(F32)
            prob_grad = prob_grads[h * 208 : (h + 1) * 208]
            inner = jnp.sum(prob * prob_grad, axis=-1, keepdims=True)
            score_grad = prob * (prob_grad - inner)
            low = score_grad.astype(BF16)
            lows.append(low)
            if group == 0 and h < 3:
                rest = (score_grad - low.astype(F32)).astype(BF16)
                turned = dot_nn(flip, low) + dot_nn(flip, rest)
                patches = jnp.where(both, turned, 0.0)
                edge = turned - patches
                parts = [jnp.where(later, patches, 0.0), jnp.where(later, 0.0, patches)]
                for which in range(2):
                    wide = jnp.concatenate([parts[which], jnp.zeros((208, 256), F32)], axis=1)
                    lined = pltpu.roll(wide, 0, 1, stride=1, stride_axis=0)
                    diag_ref[pl.ds(sid_ref[image], 1), which, h] += fold_rows(lined)[None]
                class_query = jnp.where((p == 0) & s_patch, edge, 0.0)
                class_key = jnp.where(p_patch & (s == 0), edge, 0.0)
                cls_ref[0, h] += fold_rows(class_query)
                cls_ref[1, h] += fold_rows(class_key)
                cls_ref[2, h] += fold_rows(edge - class_query - class_key)
        low_stack = jnp.concatenate(lows, axis=0)
        mixed = dot_nn(low_stack, k_group)
        out = mixed[0:208]
        for h in range(1, 4):
            out = jnp.where(head_of == h, mixed[h * 208 : (h + 1) * 208], out)
        dq[:, lanes] = out.astype(BF16) * jnp.asarray(HD ** -0.5, BF16)
        dk[:, lanes] = dot_tn(low_stack, q_stack)[0:208].astype(BF16)
        prob_stack = jnp.concatenate([prob_ref[0, group * 4 + h] for h in range(4)], axis=0)
        dv[:, lanes] = dot_tn(prob_stack, g_stack)[0:208].astype(BF16)

    normed, inv = norm_stats(tok_ref[0].astype(F32))
    first_in = (normed * first_gain + first_shift).astype(BF16)
    for c, grad in enumerate((dq, dk, dv)):
        ga_ref[c * 192 : (c + 1) * 192, :] += dot_tn(grad[:, 0:256], first_in)[0:192, :]
    first_grad = dot_nn(dq[...], wa_ref[0]) + dot_nn(dk[...], wa_ref[1]) + dot_nn(dv[...], wa_ref[2])
    tg_ref[0] = middle_grad + norm_back(first_grad, normed, inv, first_gain)
    sums_ref[0] += fold_rows(first_grad * normed)
    sums_ref[1] += fold_rows(first_grad)
    sums_ref[2] += fold_rows(dq[...].astype(F32))
    sums_ref[3] += fold_rows(dv[...].astype(F32))


def make_body(wide_size, narrow_size):
    def shift(value, steps):
        return lax.ppermute(value, "narrow", [(i, (i - steps) % narrow_size) for i in range(narrow_size)])

    def swap(value, partner):
        return lax.ppermute(value, "wide", [(j, partner(j)) for j in range(wide_size)])

    def gather_rows(own, me):
        rows = own.shape[0] // wide_size
        mine = lax.dynamic_slice_in_dim(own, me * rows, rows, axis=0).astype(F32)
        across = jnp.stack([shift(mine, k) for k in range(1, narrow_size)])
        if wide_size != 8:
            full = lax.all_gather(across, "wide", axis=1, tiled=True)
            step = own.shape[0] // 8
            return [lax.dynamic_slice_in_dim(full, ((me % 8) ^ r) * step, step, axis=1) for r in range(8)]
        one = swap(across, lambda j: j ^ 2 if j % 2 == 0 else j ^ 4)
        two = swap(across, lambda j: j ^ 4 if j % 2 == 0 else j ^ 2)
        three = swap(one, lambda j: j ^ 4 if j % 2 == 0 else j ^ 2)
        held = [across, one, two, three]
        return held + [swap(value, lambda j: j ^ 1) for value in held]

    def piece_places(me):
        if wide_size != 8:
            return jnp.stack([(me % 8) ^ r for r in range(8)]).astype(jnp.int32)
        core = me % 2
        first, second = jnp.where(core == 0, 2, 4), jnp.where(core == 0, 4, 2)
        there = me ^ 1
        return jnp.stack(
            [me, me ^ first, me ^ second, me ^ 6, there, there ^ second, there ^ first, there ^ 6]
        ).astype(jnp.int32)

    def body(
        tokens, grid_shape, first_gain, first_shift, qkv_weight, query_bias, value_bias, rel_table, proj_weight,
        proj_bias, attn_scale, second_gain, second_shift, up_weight, up_bias, down_weight, down_bias, mlp_scale,
        cotangent,
    ):
        images, slots, width = tokens.shape
        heads, table_size = rel_table.shape
        local = heads * HD
        me = lax.axis_index("wide")
        places = piece_places(me)

        own_a = jnp.concatenate(
            [jnp.transpose(qkv_weight, (0, 2, 1)).reshape(3 * local, width), proj_weight], axis=0
        )
        small = jnp.concatenate(
            [rel_table.astype(F32).reshape(-1)] + [v.astype(F32) for v in (query_bias, value_bias, up_bias)]
        )
        count = small.shape[0]
        small = jnp.pad(small, (0, 8192 - count)).reshape(64, 128)
        smalls = jnp.stack([small] + [shift(small, k) for k in range(1, narrow_size)]).reshape(narrow_size, -1)
        table = smalls[:, : heads * table_size].reshape(narrow_size * heads, table_size)
        at = heads * table_size
        q_bias = smalls[:, at : at + local].reshape(1, width)
        v_bias = smalls[:, at + local : at + 2 * local].reshape(1, width)
        u_bias = smalls[:, at + 2 * local : count]

        pieces_a = gather_rows(own_a, me)
        pieces_b = gather_rows(up_weight, me)
        pieces_c = gather_rows(down_weight, me)

        all_heads = narrow_size * heads
        cls = table[:, SPAN * SPAN :]
        square = table[:, : SPAN * SPAN].reshape(all_heads, SPAN, SPAN)[:, ::-1, ::-1]
        square = jnp.pad(jnp.transpose(square, (1, 0, 2)), ((0, 0), (0, 16 - all_heads), (0, 128 - SPAN)))
        diag = pl.pallas_call(
            diag_kernel, out_shape=jax.ShapeDtypeStruct((len(GRIDS), 2, 16, DIAG), F32), name="diag"
        )(square)

        kinds = jnp.array(GRIDS, jnp.int32)
        sid = jnp.argmax(jnp.all(grid_shape[:, None, :] == kinds[None], axis=-1), axis=-1).astype(jnp.int32)

        def row(v):
            return v.astype(F32).reshape(1, -1)

        smem = pl.BlockSpec(memory_space=pltpu.SMEM)
        anyspace = pl.BlockSpec(memory_space=pl.ANY)

        def whole(*shape):
            return pl.BlockSpec(shape, lambda i, *_: (0,) * len(shape))

        def per_image(*shape):
            return pl.BlockSpec((1,) + shape, lambda i, *_: (i,) + (0,) * len(shape))

        def struct(*shape, dtype=F32):
            return jax.ShapeDtypeStruct(shape, dtype)

        params = pltpu.CompilerParams(vmem_limit_bytes=VMEM_LIMIT, dimension_semantics=("arbitrary",))
        queries, keys, values, probs, attended, branch, weights_a = pl.pallas_call(
            attention_forward,
            grid_spec=pltpu.PrefetchScalarGridSpec(
                num_scalar_prefetch=3,
                grid=(images,),
                in_specs=[per_image(slots, width)]
                + [whole(1, width)] * 5
                + [
                    whole(width, width),
                    pl.BlockSpec((1, 2, 16, DIAG), lambda i, sid_ref, *_: (sid_ref[i], 0, 0, 0)),
                    smem,
                ]
                + [anyspace] * 8,
                out_specs=[per_image(slots, width)] * 3
                + [per_image(all_heads, slots, 256), per_image(slots, width), per_image(slots, width)]
                + [whole(4, width, width)],
                scratch_shapes=[
                    pltpu.VMEM((3, width, width), F32),
                    pltpu.VMEM((256, width), BF16),
                    pltpu.VMEM((256, width), BF16),
                    pltpu.SemaphoreType.DMA((8,)),
                ],
            ),
            out_shape=[struct(images, slots, width, dtype=BF16)] * 3
            + [
                struct(images, all_heads, slots, 256, dtype=BF16),
                struct(images, slots, width, dtype=BF16),
                struct(images, slots, width),
                struct(4, width, width, dtype=BF16),
            ],
            compiler_params=params,
            name="attention_forward",
        )(
            sid, grid_shape, places, tokens, row(first_gain), row(first_shift), q_bias, v_bias, row(proj_bias),
            own_a, diag, cls, *pieces_a,
        )

        vec = jnp.concatenate([row(v) for v in (attn_scale, second_gain, second_shift, mlp_scale, down_bias)])
        layer_out, middle_grad, grad_b, grad_c, sums = pl.pallas_call(
            feed_forward,
            grid_spec=pltpu.PrefetchScalarGridSpec(
                num_scalar_prefetch=2,
                grid=(images,),
                in_specs=[per_image(slots, width)] * 3
                + [whole(5, width), whole(narrow_size, width), whole(width, width), whole(width, width)]
                + [anyspace] * 16,
                out_specs=[per_image(slots, width)] * 2
                + [whole(width, width), whole(width, width), whole(7, 8, width)],
                scratch_shapes=[
                    pltpu.VMEM((3, width, width), F32),
                    pltpu.VMEM((4, width, width), BF16),
                    pltpu.VMEM((4, width, width), BF16),
                    pltpu.VMEM((slots, width), F32),
                    pltpu.VMEM((slots, width), F32),
                    pltpu.SemaphoreType.DMA((8,)),
                ],
            ),
            out_shape=[
                struct(images, slots, width, dtype=BF16),
                struct(images, slots, width),
                struct(width, width),
                struct(width, width),
                struct(7, 8, width),
            ],
            compiler_params=params,
            name="feed_forward",
        )(
            grid_shape, places, tokens, branch, cotangent, vec, u_bias, up_weight, down_weight, *pieces_b, *pieces_c
        )

        grad_b, grad_c = lax.psum((grad_b, grad_c), "wide")

        vec = jnp.concatenate([row(v) for v in (attn_scale, first_gain, first_shift)])
        tokens_grad, grad_a, more, diag_grad, cls_grad = pl.pallas_call(
            attention_backward,
            grid_spec=pltpu.PrefetchScalarGridSpec(
                num_scalar_prefetch=2,
                grid=(images,),
                in_specs=[
                    per_image(slots, width),
                    per_image(slots, width),
                    pl.BlockSpec((1, slots, 256), lambda i, *_: (i, 0, 0)),
                    per_image(slots, width),
                    per_image(slots, width),
                    per_image(slots, width),
                    per_image(all_heads, slots, 256),
                    whole(3, width),
                    whole(4, width, width),
                ],
                out_specs=[
                    per_image(slots, width),
                    whole(width, width),
                    whole(4, 8, width),
                    whole(len(GRIDS), 2, 3, 8, DIAG),
                    whole(3, 3, 8, 256),
                ],
                scratch_shapes=[
                    pltpu.VMEM((256, width), BF16),
                    pltpu.VMEM((256, width), BF16),
                    pltpu.VMEM((slots, width), BF16),
                    pltpu.VMEM((slots, width), BF16),
                    pltpu.VMEM((slots, width), BF16),
                ],
            ),
            out_shape=[
                struct(images, slots, width),
                struct(width, width),
                struct(4, 8, width),
                struct(len(GRIDS), 2, 3, 8, DIAG),
                struct(3, 3, 8, 256),
            ],
            compiler_params=params,
            name="attention_backward",
        )(sid, grid_shape, tokens, middle_grad, attended, queries, keys, values, probs, vec, weights_a)

        diag_grad = jnp.pad(jnp.sum(diag_grad, axis=3), ((0, 0), (0, 0), (0, 8 - heads), (0, 0)))
        square_grad = pl.pallas_call(
            undiag_kernel, out_shape=struct(SPAN, 8, 128), name="undiag"
        )(diag_grad)
        square_grad = jnp.transpose(square_grad[:, :heads, :SPAN], (1, 0, 2))[:, ::-1, ::-1]
        table_grad = jnp.concatenate(
            [square_grad.reshape(heads, SPAN * SPAN), jnp.sum(cls_grad, axis=(2, 3)).T], axis=1
        )
        sums = jnp.sum(sums, axis=1)
        more = jnp.sum(more, axis=1)
        grad_a, table_grad, sums, more = lax.psum((grad_a, table_grad, sums, more), "wide")
        qkv_grad = jnp.transpose(grad_a[: 3 * local].reshape(3, local, width), (0, 2, 1))
        return (
            layer_out,
            tokens_grad,
            more[0],
            more[1],
            qkv_grad,
            more[2, :local],
            more[3, :local],
            table_grad,
            grad_a[3 * local :],
            sums[5] * attn_scale.astype(F32),
            sums[4],
            sums[2],
            sums[3],
            grad_b,
            sums[6],
            grad_c,
            sums[1] * mlp_scale.astype(F32),
            sums[0],
        )

    return body


def solution(mesh):
    rows = P("wide", None, None)
    return jax.shard_map(
        make_body(mesh.shape["wide"], mesh.shape["narrow"]),
        mesh=mesh,
        in_specs=(
            rows, P("wide", None), P(), P(), P(None, None, "narrow"), P("narrow"), P("narrow"), P("narrow", None),
            P("narrow", None), P(), P(), P(), P(), P(None, "narrow"), P("narrow"), P("narrow", None), P(), P(), rows,
        ),
        out_specs=(
            rows, rows, P(), P(), P(None, None, "narrow"), P("narrow"), P("narrow"), P("narrow", None),
            P("narrow", None), P(), P(), P(), P(), P(None, "narrow"), P("narrow"), P("narrow", None), P(), P(),
        ),
        check_vma=False,
    )
```

```python
import functools

import jax
import jax.numpy as jnp
from jax import lax
from jax.experimental import pallas as pl
from jax.experimental.pallas import tpu as pltpu
from jax.sharding import PartitionSpec as P

HD = 64
MAXG = 24
SPAN = 2 * MAXG - 1
EPSILON = 1e-06
MASKED = -1e30
INV_ROOT_TWO = 0.7071067811865476
INV_ROOT_TWO_PI = 0.3989422804014327
GRIDS = ((14, 14), (10, 20), (20, 10), (8, 24), (24, 8), (12, 16), (16, 12), (13, 15))
DIAG = 512
F32 = jnp.float32
BF16 = jnp.bfloat16
VMEM_LIMIT = 60 * 1024 * 1024


def dot_nn(a, b):
    return lax.dot_general(a, b, (((1,), (0,)), ((), ())), preferred_element_type=F32)


def dot_nt(a, b):
    return lax.dot_general(a, b, (((1,), (1,)), ((), ())), preferred_element_type=F32)


def dot_tn(a, b):
    return lax.dot_general(a, b, (((0,), (0,)), ((), ())), preferred_element_type=F32)


def row_mean(v):
    return jnp.sum(v, axis=-1, keepdims=True) * (1.0 / v.shape[-1])


def norm_stats(v):
    centred = v - row_mean(v)
    inv = lax.rsqrt(row_mean(centred * centred) + EPSILON)
    return centred * inv, inv


def norm_back(incoming, normed, inv, gain):
    scaled = incoming * gain
    return inv * (scaled - row_mean(scaled) - normed * row_mean(scaled * normed))


def fold_rows(v):
    rows = v.shape[0]
    return jnp.sum(v.reshape(rows // 8, 8, v.shape[1]), axis=0)


def windows(shape_at):
    high, wide = GRIDS[shape_at]
    centre = MAXG - 1
    for m in range(-high, high):
        at = 207 + m * wide
        if m > -high:
            yield 0, centre + m, centre, at, wide
        if m < high - 1:
            yield 1, centre + 1 + m, centre + 1 - wide, at + 1, wide - 1


def undiag_kernel(diag_ref, out_ref):
    out_ref[...] = jnp.zeros_like(out_ref)
    for shape_at in range(len(GRIDS)):
        for which, row, col, at, size in windows(shape_at):
            out_ref[row, :, col : col + size] += diag_ref[shape_at, which, :, at : at + size]


def slot_masks(high, wide, reverse):
    rows = lax.broadcasted_iota(jnp.int32, (208, 1), 0)
    p = 207 - rows if reverse else rows
    s = lax.broadcasted_iota(jnp.int32, (1, 256), 1)
    limit = high * wide
    wide_f = wide.astype(F32)

    def column(slot):
        patch = (slot - 1).astype(F32)
        return patch - wide_f * jnp.floor((patch + 0.5) / wide_f)

    later = column(s) >= column(p)
    p_patch = (p >= 1) & (p <= limit)
    s_patch = (s >= 1) & (s <= limit)
    return p, s, limit, later, p_patch, s_patch


MESH = pl.DeviceIdType.MESH
SLICES = 8
SLICE_ROWS = 96
PART_ROWS = 24
CHUNKS = tuple((group, at, 24) for group in range(3) for at in (0, 24, 48, 72))


class Gather:
    def __init__(self, narrow, slices, buffers, send, recv):
        self.narrow, self.slices, self.buffers, self.send, self.recv = narrow, slices, buffers, send, recv
        self.z = lax.axis_index("narrow")
        wide = lax.axis_index("wide")
        self.me = wide % SLICES
        self.base = wide - self.me
        core = self.me % 2
        over_x = self.me + 2 - 4 * ((self.me // 2) % 2)
        over_y = self.me + 4 - 8 * (self.me // 4)
        self.first = over_x * (1 - core) + over_y * core
        self.second = over_y * (1 - core) + over_x * core
        self.third = over_x + over_y - self.me
        self.twin = self.me + 1 - 2 * core
        self.per_chunk = narrow - 1 + 7
        self.started = []

    def copy(self, chunk, phase, piece):
        group, at, rows = CHUNKS[chunk]
        buffer = self.buffers[group]

        def part(owner):
            return buffer.at[:, pl.ds(pl.multiple_of(owner * SLICE_ROWS + at, 8), rows), :]

        place = chunk * self.per_chunk
        if phase == 0:
            place += piece - 1
            source = self.slices.at[group, pl.ds(at, rows), :]
            target = buffer.at[piece - 1, pl.ds(pl.multiple_of(self.me * SLICE_ROWS + at, 8), rows), :]
            device = {"narrow": (self.z + self.narrow - piece) % self.narrow}
        else:
            owners = (self.me, self.first, self.second, self.third)
            place += self.narrow - 1 + (0, 1, 3)[phase - 1] + piece
            source = target = part(owners[piece])
            device = {"wide": self.base + (self.first, self.second, self.twin)[phase - 1]}
        return pltpu.make_async_remote_copy(
            src_ref=source, dst_ref=target, send_sem=self.send.at[place], recv_sem=self.recv.at[place],
            device_id=device, device_id_type=MESH,
        )

    def pieces(self, phase):
        return (range(1, self.narrow), range(1), range(2), range(4))[phase]

    def start(self, chunk, phase):
        for piece in self.pieces(phase):
            self.copy(chunk, phase, piece).start()

    def arrive(self, chunk, phase):
        for piece in self.pieces(phase):
            self.copy(chunk, phase, piece).wait_recv()

    def run(self, steps):
        for chunk, phase in steps:
            if phase > 0:
                self.arrive(chunk, phase - 1)
            self.start(chunk, phase)

    def drain(self):
        for chunk in range(len(CHUNKS)):
            for phase in range(4):
                for piece in self.pieces(phase):
                    self.copy(chunk, phase, piece).wait_send()

    def barrier(self):
        sem = pltpu.get_barrier_semaphore()
        for k in range(1, self.narrow):
            pl.semaphore_signal(
                sem, inc=1, device_id={"narrow": (self.z + k) % self.narrow}, device_id_type=MESH
            )
        for other in (self.first, self.second, self.twin):
            pl.semaphore_signal(sem, inc=1, device_id={"wide": self.base + other}, device_id_type=MESH)
        pl.semaphore_wait(sem, self.narrow - 1 + 3)


def tick(t):
    steps = ((t, 1), (t + 2, 0), (t - 1, 2), (t - 2, 3))
    return tuple((chunk, phase) for chunk, phase in steps if 0 <= chunk < len(CHUNKS))


LATE = {3: 7, 11: 8, 20: 9}
LAST = range(10, len(CHUNKS) + 2)


def attention_forward(
    sid_ref, grid_ref, tok_ref, gain_ref, shift_ref, pb_ref, own_ref, slices, table_ref, small_ref,
    prob_ref, att_ref, branch_ref, wa_ref, small_out, q_out, k_out, v_out, gath_b, gath_c,
    stage, first_in, queries, k_pad, v_pad, bias, lined, diag, far, smalls, send, recv, extra_send, extra_recv, local,
    narrow,
):
    image = pl.program_id(0)
    images = pl.num_programs(0)
    gather = Gather(narrow, slices, (stage, gath_b, gath_c), send, recv)

    def extra(which, k):
        source = diag if which else small_ref.at[k]
        target = far.at[k - 1] if which else smalls.at[k]
        place = which * (narrow - 1) + k - 1
        return pltpu.make_async_remote_copy(
            src_ref=source, dst_ref=target, send_sem=extra_send.at[place], recv_sem=extra_recv.at[place],
            device_id={"narrow": (gather.z + narrow - k) % narrow}, device_id_type=MESH,
        )

    def keep(which):
        source, target = ((queries, q_out), (k_pad, k_out), (v_pad, v_out))[which]
        return pltpu.make_async_copy(source, target, local.at[which])

    @pl.when(image == 0)
    def _():
        def bias_of(slot, at, table):
            p, s, limit, later, p_patch, s_patch = slot_masks(grid_ref[at, 0], grid_ref[at, 1], False)
            both = p_patch & s_patch
            open_key = s <= limit
            for h in range(3):
                row = h * 16 + sid_ref[at] * 2
                toep = [
                    pltpu.roll(
                        jnp.broadcast_to(table(row + which), (208, DIAG)), DIAG - 207, 1, stride=1, stride_axis=0
                    )[:, :256]
                    for which in range(2)
                ]
                c0, c1, c2 = (smalls[slot, 3:4, h * 3 + c : h * 3 + c + 1] for c in range(3))
                outer = jnp.where((p == 0) & s_patch, c0, jnp.where(p_patch & (s == 0), c1, c2))
                value = jnp.where(both, jnp.where(later, toep[0], toep[1]), outer)
                bias[at, slot * 3 + h] = jnp.where(open_key, value, MASKED).astype(BF16)

        def far_bias(slot):
            @pl.loop(0, 8)
            def _(at):
                bias_of(slot, at, lambda row: far[slot - 1, pl.ds(row, 1), :])

        def weights_of(part):
            gather.arrive(part, 3)
            for slot in range(narrow - 1):
                for pair in range(4):
                    rows = [
                        stage[slot, pl.ds((2 * pair + i) * SLICE_ROWS + part * PART_ROWS, PART_ROWS), :]
                        for i in range(2)
                    ]
                    at = (slot + 1) * 192 + pair * 2 * PART_ROWS
                    wa_ref[part, at : at + 2 * PART_ROWS, :] = jnp.concatenate(rows, axis=0).astype(BF16)

        def project(part, target, finish):
            @pl.loop(0, 8)
            def _(at):
                target[at, 0:208, :] = finish(dot_nt(first_in[at], wa_ref[part])).astype(BF16)

            keep(part).start()

        lined[...] = jnp.zeros_like(lined)
        for shape_at in range(len(GRIDS)):
            for which, row, col, at, size in windows(shape_at):
                lined[shape_at * 2 + which, :, at : at + size] = table_ref[row, :, col : col + size]
        for h in range(3):
            for r in range(16):
                diag[h * 16 + r : h * 16 + r + 1, :] = lined[r, h : h + 1, :]
        gather.barrier()
        smalls[0] = small_ref[0]
        for k in range(1, narrow):
            extra(0, k).start()
            extra(1, k).start()
        gather.run(((0, 0), (1, 0)))
        k_pad[:, 208:256, :] = jnp.zeros((8, 48, 768), BF16)
        v_pad[:, 208:256, :] = jnp.zeros((8, 48, 768), BF16)
        for part in range(4):
            wa_ref[part, 0:192, :] = own_ref[part * 192 : (part + 1) * 192, :]

        @pl.loop(0, 8)
        def _(at):
            normed, _ = norm_stats(tok_ref[at].astype(F32))
            first_in[at] = (normed * gain_ref[...] + shift_ref[...]).astype(BF16)
            bias_of(0, at, lambda row: diag[pl.ds(row, 1), :])

        gather.run(tick(0))
        for k in range(1, narrow):
            extra(0, k).wait_recv()
            extra(1, k).wait_recv()
        far_bias(1)
        gather.run(tick(1))
        far_bias(2)
        gather.run(tick(2))
        far_bias(3)
        gather.run(tick(3))
        q_bias = sum(smalls[k, 0:1, :] for k in range(narrow))
        v_bias = sum(smalls[k, 1:2, :] for k in range(narrow))
        small_out[...] = smalls[...]
        weights_of(0)
        project(0, queries, lambda v: (v + q_bias) * (HD ** -0.5))
        gather.run(tick(4))
        weights_of(1)
        project(1, k_pad, lambda v: v)
        gather.run(tick(5))
        weights_of(2)
        project(2, v_pad, lambda v: v + v_bias)
        gather.run(tick(6))
        weights_of(3)

    head_of = lax.broadcasted_iota(jnp.int32, (1, 256), 1) // HD

    @pl.loop(0, 3)
    def _(group):
        for when, t in LATE.items():
            @pl.when(image * 3 + group == when)
            def _():
                gather.run(tick(t))

        lanes = pl.ds(pl.multiple_of(group * 256, 256), 256)
        q_group = queries[image, :, lanes]
        k_group = k_pad[image, :, lanes]
        v_group = v_pad[image, :, lanes]
        stacked = jnp.concatenate(
            [jnp.where(head_of == h, q_group, jnp.zeros_like(q_group)) for h in range(4)], axis=0
        )
        raw = dot_nt(stacked, k_group)
        probs = []
        for h in range(4):
            head = group * 4 + h
            scores = raw[h * 208 : (h + 1) * 208, :] + bias[image, head].astype(F32)
            top = jnp.max(scores, axis=-1, keepdims=True)
            raised = jnp.exp(scores - top)
            prob = (raised * (1.0 / jnp.sum(raised, axis=-1, keepdims=True))).astype(BF16)
            prob_ref[0, head] = prob
            probs.append(prob)
        mixed = dot_nn(jnp.concatenate(probs, axis=0), v_group)
        out = mixed[0:208]
        for h in range(1, 4):
            out = jnp.where(head_of == h, mixed[h * 208 : (h + 1) * 208], out)
        att_ref[0, :, lanes] = out.astype(BF16)

    branch_ref[0] = dot_nn(att_ref[0], wa_ref[3]) + pb_ref[...]

    @pl.when(image == images - 1)
    def _():
        for t in LAST:
            gather.run(tick(t))
        for chunk in range(4, len(CHUNKS)):
            gather.arrive(chunk, 3)
        gather.drain()
        for k in range(1, narrow):
            extra(0, k).wait_send()
            extra(1, k).wait_send()
        for which in range(3):
            keep(which).wait()


def feed_forward(
    grid_ref, tok_ref, branch_ref, cot_ref, vec_ref, small_ref, ownb_ref, ownc_ref, gath_b, gath_c,
    out_ref, mg_ref, gb_ref, gc_ref, sums_ref,
    stage, wb, wc, mlp_acc, second_acc, sems,
):
    image = pl.program_id(0)

    @pl.when(image == 0)
    def _():
        copies = [
            pltpu.make_async_copy(gath.at[slot], stage.at[which * 3 + slot], sems.at[which * 3 + slot])
            for which, gath in enumerate((gath_b, gath_c))
            for slot in range(3)
        ]
        for copy in copies:
            copy.start()
        wb[0] = ownb_ref[...]
        wc[0] = ownc_ref[...]
        for which, weights in enumerate((wb, wc)):
            for slot in range(3):
                copies[which * 3 + slot].wait()
                weights[slot + 1] = stage[which * 3 + slot].astype(BF16)
        gb_ref[...] = jnp.zeros_like(gb_ref)
        gc_ref[...] = jnp.zeros_like(gc_ref)
        sums_ref[...] = jnp.zeros_like(sums_ref)

    attn_scale, second_gain, second_shift, mlp_scale, down_bias = (vec_ref[i : i + 1, :] for i in range(5))
    branch = branch_ref[0]
    middle = tok_ref[0].astype(F32) + attn_scale * branch
    normed, inv = norm_stats(middle)
    second_in = (normed * second_gain + second_shift).astype(BF16)
    valid = lax.broadcasted_iota(jnp.int32, (208, 1), 0) <= grid_ref[image, 0] * grid_ref[image, 1]
    out_grad = jnp.where(valid, cot_ref[0].astype(F32), 0.0)
    branch_low = (out_grad * mlp_scale).astype(BF16)
    mlp_acc[...] = jnp.zeros_like(mlp_acc)
    second_acc[...] = jnp.zeros_like(second_acc)

    @pl.loop(0, 4)
    def _(slot):
        up_pre = dot_nn(second_in, wb[slot]) + small_ref[slot, 2:3, :]
        cdf = 0.5 * (1.0 + lax.erf(up_pre * INV_ROOT_TWO))
        hidden = (up_pre * cdf).astype(BF16)
        slope = cdf + up_pre * jnp.exp(-0.5 * up_pre * up_pre) * INV_ROOT_TWO_PI
        mlp_acc[...] += dot_nn(hidden, wc[slot])
        pre_low = (dot_nt(branch_low, wc[slot]) * slope).astype(BF16)
        second_acc[...] += dot_nt(pre_low, wb[slot])

        @pl.when(slot == 0)
        def _():
            gc_ref[...] += dot_tn(hidden, branch_low)
            gb_ref[...] += dot_tn(second_in, pre_low)
            sums_ref[6] += fold_rows(pre_low.astype(F32))

    mlp_branch = mlp_acc[...] + down_bias
    out_ref[0] = (middle + mlp_scale * mlp_branch).astype(BF16)
    second_grad = second_acc[...]
    middle_grad = out_grad + norm_back(second_grad, normed, inv, second_gain)
    mg_ref[0] = middle_grad
    sums_ref[0] += fold_rows(out_grad * mlp_branch)
    sums_ref[1] += fold_rows(out_grad)
    sums_ref[2] += fold_rows(second_grad * normed)
    sums_ref[3] += fold_rows(second_grad)
    sums_ref[4] += fold_rows(middle_grad * branch)
    sums_ref[5] += fold_rows(middle_grad)


def attention_backward(
    sid_ref, grid_ref, tok_ref, mg_ref, att_ref, q_ref, k_ref, v_ref, prob_ref, vec_ref, wa_ref,
    tg_ref, ga_ref, sums_ref, diag_ref, cls_ref,
    dq, dk, dv,
):
    image = pl.program_id(0)

    @pl.when(image == 0)
    def _():
        ga_ref[...] = jnp.zeros_like(ga_ref)
        sums_ref[...] = jnp.zeros_like(sums_ref)
        diag_ref[...] = jnp.zeros_like(diag_ref)
        cls_ref[...] = jnp.zeros_like(cls_ref)

    attn_scale, first_gain, first_shift = (vec_ref[i : i + 1, :] for i in range(3))
    middle_grad = mg_ref[0]
    attn_low = (middle_grad * attn_scale).astype(BF16)
    attended_grad = dot_nt(attn_low, wa_ref[3]).astype(BF16)
    ga_ref[576:768, :] += dot_tn(att_ref[0], attn_low)[0:192, :]

    p, s, limit, later, p_patch, s_patch = slot_masks(grid_ref[image, 0], grid_ref[image, 1], True)
    both = p_patch & s_patch
    flip = (
        lax.broadcasted_iota(jnp.int32, (208, 208), 0) + lax.broadcasted_iota(jnp.int32, (208, 208), 1) == 207
    ).astype(BF16)
    head_of = lax.broadcasted_iota(jnp.int32, (1, 256), 1) // HD

    for group in range(3):
        lanes = slice(group * 256, group * 256 + 256)
        k_group, v_group = k_ref[0, :, lanes], v_ref[0, :, lanes]
        q_group = q_ref[0, :, lanes]
        g_group = attended_grad[:, lanes]
        q_stack = jnp.concatenate(
            [jnp.where(head_of == h, q_group, jnp.zeros_like(q_group)) for h in range(4)], axis=0
        )
        g_stack = jnp.concatenate(
            [jnp.where(head_of == h, g_group, jnp.zeros_like(g_group)) for h in range(4)], axis=0
        )
        prob_grads = dot_nt(g_stack, v_group)
        lows = []
        for h in range(4):
            prob = prob_ref[0, group * 4 + h].astype(F32)
            prob_grad = prob_grads[h * 208 : (h + 1) * 208]
            inner = jnp.sum(prob * prob_grad, axis=-1, keepdims=True)
            score_grad = prob * (prob_grad - inner)
            low = score_grad.astype(BF16)
            lows.append(low)
            if group == 0 and h < 3:
                rest = (score_grad - low.astype(F32)).astype(BF16)
                turned = dot_nn(flip, low) + dot_nn(flip, rest)
                patches = jnp.where(both, turned, 0.0)
                edge = turned - patches
                parts = [jnp.where(later, patches, 0.0), jnp.where(later, 0.0, patches)]
                for which in range(2):
                    wide = jnp.concatenate([parts[which], jnp.zeros((208, 256), F32)], axis=1)
                    lined = pltpu.roll(wide, 0, 1, stride=1, stride_axis=0)
                    diag_ref[pl.ds(sid_ref[image], 1), which, h] += fold_rows(lined)[None]
                class_query = jnp.where((p == 0) & s_patch, edge, 0.0)
                class_key = jnp.where(p_patch & (s == 0), edge, 0.0)
                cls_ref[0, h] += fold_rows(class_query)
                cls_ref[1, h] += fold_rows(class_key)
                cls_ref[2, h] += fold_rows(edge - class_query - class_key)
        low_stack = jnp.concatenate(lows, axis=0)
        mixed = dot_nn(low_stack, k_group)
        out = mixed[0:208]
        for h in range(1, 4):
            out = jnp.where(head_of == h, mixed[h * 208 : (h + 1) * 208], out)
        dq[:, lanes] = out.astype(BF16) * jnp.asarray(HD ** -0.5, BF16)
        dk[:, lanes] = dot_tn(low_stack, q_stack)[0:208].astype(BF16)
        prob_stack = jnp.concatenate([prob_ref[0, group * 4 + h] for h in range(4)], axis=0)
        dv[:, lanes] = dot_tn(prob_stack, g_stack)[0:208].astype(BF16)

    normed, inv = norm_stats(tok_ref[0].astype(F32))
    first_in = (normed * first_gain + first_shift).astype(BF16)
    for c, grad in enumerate((dq, dk, dv)):
        ga_ref[c * 192 : (c + 1) * 192, :] += dot_tn(grad[:, 0:256], first_in)[0:192, :]
    first_grad = dot_nn(dq[...], wa_ref[0]) + dot_nn(dk[...], wa_ref[1]) + dot_nn(dv[...], wa_ref[2])
    tg_ref[0] = middle_grad + norm_back(first_grad, normed, inv, first_gain)
    sums_ref[0] += fold_rows(first_grad * normed)
    sums_ref[1] += fold_rows(first_grad)
    sums_ref[2] += fold_rows(dq[...].astype(F32))
    sums_ref[3] += fold_rows(dv[...].astype(F32))


def make_body(wide_size, narrow_size):
    def body(
        tokens, grid_shape, first_gain, first_shift, qkv_weight, query_bias, value_bias, rel_table, proj_weight,
        proj_bias, attn_scale, second_gain, second_shift, up_weight, up_bias, down_weight, down_bias, mlp_scale,
        cotangent,
    ):
        images, slots, width = tokens.shape
        heads, table_size = rel_table.shape
        local = heads * HD
        own_a = jnp.concatenate(
            [jnp.transpose(qkv_weight, (0, 2, 1)).reshape(3 * local, width), proj_weight], axis=0
        )
        table = rel_table.astype(F32)
        square = table[:, : SPAN * SPAN].reshape(heads, SPAN, SPAN)[:, ::-1, ::-1]
        square = jnp.pad(jnp.transpose(square, (1, 0, 2)), ((0, 0), (0, 8 - heads), (0, 128 - SPAN)))

        def small_for(k):
            def at(v, start):
                return jnp.pad(v.astype(F32).reshape(1, -1), ((0, 0), (start, width - start - v.size)))

            return jnp.concatenate(
                [
                    at(query_bias, k * local), at(value_bias, k * local), at(up_bias, 0),
                    at(table[:, SPAN * SPAN :].reshape(-1), 0), jnp.zeros((4, width), F32),
                ]
            )

        small = jnp.stack([small_for(k) for k in range(narrow_size)])
        all_heads = narrow_size * heads

        kinds = jnp.array(GRIDS, jnp.int32)
        sid = jnp.argmax(jnp.all(grid_shape[:, None, :] == kinds[None], axis=-1), axis=-1).astype(jnp.int32)

        def row(v):
            return v.astype(F32).reshape(1, -1)

        smem = pl.BlockSpec(memory_space=pltpu.SMEM)
        anyspace = pl.BlockSpec(memory_space=pl.ANY)
        vmem = pl.BlockSpec(memory_space=pltpu.VMEM)

        def whole(*shape):
            return pl.BlockSpec(shape, lambda i, *_: (0,) * len(shape))

        def per_image(*shape):
            return pl.BlockSpec((1,) + shape, lambda i, *_: (i,) + (0,) * len(shape))

        def struct(*shape, dtype=F32):
            return jax.ShapeDtypeStruct(shape, dtype)

        params = pltpu.CompilerParams(vmem_limit_bytes=VMEM_LIMIT, dimension_semantics=("arbitrary",))
        copies = len(CHUNKS) * (narrow_size - 1 + 7)
        copies = len(CHUNKS) * (narrow_size - 1 + 7)
        me = lax.axis_index("wide") % SLICES
        slices = jnp.stack(
            [lax.dynamic_slice_in_dim(own_a.reshape(4, local, width), me * PART_ROWS, PART_ROWS, 1).reshape(-1, width)]
            + [lax.dynamic_slice_in_dim(w, me * SLICE_ROWS, SLICE_ROWS, 0) for w in (up_weight, down_weight)]
        ).astype(F32)
        probs, attended, branch, weights_a, small, queries, keys, values, gath_b, gath_c = pl.pallas_call(
            functools.partial(attention_forward, narrow=narrow_size),
            grid=(images,),
            in_specs=[smem, smem, vmem] + [whole(1, width)] * 3 + [vmem] * 4,
            out_specs=[per_image(all_heads, slots, 256), per_image(slots, width), per_image(slots, width)]
            + [vmem, vmem] + [anyspace] * 5,
            scratch_shapes=[
                pltpu.VMEM((narrow_size - 1, width, width), F32),
                pltpu.VMEM((images, slots, width), BF16),
                pltpu.VMEM((images, slots, width), BF16),
                pltpu.VMEM((images, 256, width), BF16),
                pltpu.VMEM((images, 256, width), BF16),
                pltpu.VMEM((images, all_heads, slots, 256), BF16),
                pltpu.VMEM((16, 8, DIAG), F32),
                pltpu.VMEM((48, DIAG), F32),
                pltpu.VMEM((narrow_size - 1, 48, DIAG), F32),
                pltpu.VMEM((narrow_size, 8, width), F32),
                pltpu.SemaphoreType.DMA((copies,)),
                pltpu.SemaphoreType.DMA((copies,)),
                pltpu.SemaphoreType.DMA((2 * narrow_size - 2,)),
                pltpu.SemaphoreType.DMA((2 * narrow_size - 2,)),
                pltpu.SemaphoreType.DMA((3,)),
            ],
            out_shape=[
                struct(images, all_heads, slots, 256, dtype=BF16),
                struct(images, slots, width, dtype=BF16),
                struct(images, slots, width),
                struct(4, width, width, dtype=BF16),
                struct(narrow_size, 8, width),
                struct(images, slots, width, dtype=BF16),
                struct(images, 256, width, dtype=BF16),
                struct(images, 256, width, dtype=BF16),
                struct(narrow_size - 1, width, width),
                struct(narrow_size - 1, width, width),
            ],
            compiler_params=pltpu.CompilerParams(
                vmem_limit_bytes=VMEM_LIMIT, dimension_semantics=("arbitrary",), collective_id=0,
                has_side_effects=True,
            ),
            name="attention_forward",
        )(
            sid, grid_shape, tokens, row(first_gain), row(first_shift), row(proj_bias), own_a, slices, square, small,
        )

        vec = jnp.concatenate([row(v) for v in (attn_scale, second_gain, second_shift, mlp_scale, down_bias)])
        layer_out, middle_grad, grad_b, grad_c, sums = pl.pallas_call(
            feed_forward,
            grid_spec=pltpu.PrefetchScalarGridSpec(
                num_scalar_prefetch=1,
                grid=(images,),
                in_specs=[per_image(slots, width)] * 3
                + [whole(5, width), whole(narrow_size, 8, width), whole(width, width), whole(width, width)]
                + [anyspace] * 2,
                out_specs=[per_image(slots, width)] * 2
                + [whole(width, width), whole(width, width), whole(7, 8, width)],
                scratch_shapes=[
                    pltpu.VMEM((6, width, width), F32),
                    pltpu.VMEM((4, width, width), BF16),
                    pltpu.VMEM((4, width, width), BF16),
                    pltpu.VMEM((slots, width), F32),
                    pltpu.VMEM((slots, width), F32),
                    pltpu.SemaphoreType.DMA((6,)),
                ],
            ),
            out_shape=[
                struct(images, slots, width, dtype=BF16),
                struct(images, slots, width),
                struct(width, width),
                struct(width, width),
                struct(7, 8, width),
            ],
            compiler_params=params,
            name="feed_forward",
        )(
            grid_shape, tokens, branch, cotangent, vec, small, up_weight, down_weight, gath_b, gath_c
        )

        grad_b, grad_c = lax.psum((grad_b, grad_c), "wide")

        vec = jnp.concatenate([row(v) for v in (attn_scale, first_gain, first_shift)])
        tokens_grad, grad_a, more, diag_grad, cls_grad = pl.pallas_call(
            attention_backward,
            grid_spec=pltpu.PrefetchScalarGridSpec(
                num_scalar_prefetch=2,
                grid=(images,),
                in_specs=[
                    per_image(slots, width),
                    per_image(slots, width),
                    pl.BlockSpec((1, slots, 256), lambda i, *_: (i, 0, 0)),
                    per_image(slots, width),
                    per_image(256, width),
                    per_image(256, width),
                    per_image(all_heads, slots, 256),
                    whole(3, width),
                    whole(4, width, width),
                ],
                out_specs=[
                    per_image(slots, width),
                    whole(width, width),
                    whole(4, 8, width),
                    whole(len(GRIDS), 2, 3, 8, DIAG),
                    whole(3, 3, 8, 256),
                ],
                scratch_shapes=[
                    pltpu.VMEM((slots, width), BF16),
                    pltpu.VMEM((slots, width), BF16),
                    pltpu.VMEM((slots, width), BF16),
                ],
            ),
            out_shape=[
                struct(images, slots, width),
                struct(width, width),
                struct(4, 8, width),
                struct(len(GRIDS), 2, 3, 8, DIAG),
                struct(3, 3, 8, 256),
            ],
            compiler_params=params,
            name="attention_backward",
        )(sid, grid_shape, tokens, middle_grad, attended, queries, keys, values, probs, vec, weights_a)

        diag_grad = jnp.pad(jnp.sum(diag_grad, axis=3), ((0, 0), (0, 0), (0, 8 - heads), (0, 0)))
        square_grad = pl.pallas_call(
            undiag_kernel, out_shape=struct(SPAN, 8, 128), name="undiag"
        )(diag_grad)
        square_grad = jnp.transpose(square_grad[:, :heads, :SPAN], (1, 0, 2))[:, ::-1, ::-1]
        table_grad = jnp.concatenate(
            [square_grad.reshape(heads, SPAN * SPAN), jnp.sum(cls_grad, axis=(2, 3)).T], axis=1
        )
        sums = jnp.sum(sums, axis=1)
        more = jnp.sum(more, axis=1)
        grad_a, table_grad, sums, more = lax.psum((grad_a, table_grad, sums, more), "wide")
        qkv_grad = jnp.transpose(grad_a[: 3 * local].reshape(3, local, width), (0, 2, 1))
        return (
            layer_out,
            tokens_grad,
            more[0],
            more[1],
            qkv_grad,
            more[2, :local],
            more[3, :local],
            table_grad,
            grad_a[3 * local :],
            sums[5] * attn_scale.astype(F32),
            sums[4],
            sums[2],
            sums[3],
            grad_b,
            sums[6],
            grad_c,
            sums[1] * mlp_scale.astype(F32),
            sums[0],
        )

    return body


def solution(mesh):
    rows = P("wide", None, None)
    return jax.shard_map(
        make_body(mesh.shape["wide"], mesh.shape["narrow"]),
        mesh=mesh,
        in_specs=(
            rows, P("wide", None), P(), P(), P(None, None, "narrow"), P("narrow"), P("narrow"), P("narrow", None),
            P("narrow", None), P(), P(), P(), P(), P(None, "narrow"), P("narrow"), P("narrow", None), P(), P(), rows,
        ),
        out_specs=(
            rows, rows, P(), P(), P(None, None, "narrow"), P("narrow"), P("narrow"), P("narrow", None),
            P("narrow", None), P(), P(), P(), P(), P(None, "narrow"), P("narrow"), P("narrow", None), P(), P(),
        ),
        check_vma=False,
    )
```

```python
import functools

import jax
import jax.numpy as jnp
from jax import lax
from jax.experimental import pallas as pl
from jax.experimental.pallas import tpu as pltpu
from jax.sharding import PartitionSpec as P

HD = 64
MAXG = 24
SPAN = 2 * MAXG - 1
EPSILON = 1e-06
MASKED = -1e30
INV_ROOT_TWO = 0.7071067811865476
INV_ROOT_TWO_PI = 0.3989422804014327
GRIDS = ((14, 14), (10, 20), (20, 10), (8, 24), (24, 8), (12, 16), (16, 12), (13, 15))
DIAG = 512
F32 = jnp.float32
BF16 = jnp.bfloat16
VMEM_LIMIT = 60 * 1024 * 1024


def dot_nn(a, b):
    return lax.dot_general(a, b, (((1,), (0,)), ((), ())), preferred_element_type=F32)


def dot_nt(a, b):
    return lax.dot_general(a, b, (((1,), (1,)), ((), ())), preferred_element_type=F32)


def dot_tn(a, b):
    return lax.dot_general(a, b, (((0,), (0,)), ((), ())), preferred_element_type=F32)


def row_mean(v):
    return jnp.sum(v, axis=-1, keepdims=True) * (1.0 / v.shape[-1])


def norm_stats(v):
    centred = v - row_mean(v)
    inv = lax.rsqrt(row_mean(centred * centred) + EPSILON)
    return centred * inv, inv


def norm_back(incoming, normed, inv, gain):
    scaled = incoming * gain
    return inv * (scaled - row_mean(scaled) - normed * row_mean(scaled * normed))


def fold_rows(v):
    rows = v.shape[0]
    return jnp.sum(v.reshape(rows // 8, 8, v.shape[1]), axis=0)


def windows(shape_at):
    high, wide = GRIDS[shape_at]
    centre = MAXG - 1
    for m in range(-high, high):
        at = 207 + m * wide
        if m > -high:
            yield 0, centre + m, centre, at, wide
        if m < high - 1:
            yield 1, centre + 1 + m, centre + 1 - wide, at + 1, wide - 1


def undiag_kernel(diag_ref, out_ref):
    out_ref[...] = jnp.zeros_like(out_ref)
    for shape_at in range(len(GRIDS)):
        for which, row, col, at, size in windows(shape_at):
            out_ref[row, :, col : col + size] += diag_ref[shape_at, which, :, at : at + size]


def slot_masks(high, wide, reverse):
    rows = lax.broadcasted_iota(jnp.int32, (208, 1), 0)
    p = 207 - rows if reverse else rows
    s = lax.broadcasted_iota(jnp.int32, (1, 256), 1)
    limit = high * wide
    wide_f = wide.astype(F32)

    def column(slot):
        patch = (slot - 1).astype(F32)
        return patch - wide_f * jnp.floor((patch + 0.5) / wide_f)

    later = column(s) >= column(p)
    p_patch = (p >= 1) & (p <= limit)
    s_patch = (s >= 1) & (s <= limit)
    return p, s, limit, later, p_patch, s_patch


MESH = pl.DeviceIdType.MESH
SLICES = 8
SLICE_ROWS = 96
PART_ROWS = 24
CHUNKS = tuple((group, at, 24) for group in range(3) for at in (0, 24, 48, 72))


class Neighbours:
    def __init__(self):
        self.wide = lax.axis_index("wide")
        self.me = self.wide % SLICES
        self.base = self.wide - self.me
        self.core = core = self.me % 2
        x_bit, y_bit = (self.me // 2) % 2, self.me // 4
        over_x, over_y = self.me + 2 - 4 * x_bit, self.me + 4 - 8 * y_bit
        self.first = over_x * (1 - core) + over_y * core
        self.second = over_y * (1 - core) + over_x * core
        self.first_bit = x_bit * (1 - core) + y_bit * core
        self.second_bit = y_bit * (1 - core) + x_bit * core
        self.third = over_x + over_y - self.me
        self.twin = self.me + 1 - 2 * core

    def beyond(self, step):
        size = SLICES << step
        return self.wide + size - 2 * size * ((self.wide // size) % 2)


class Gather(Neighbours):
    def __init__(self, narrow, slices, buffers, send, recv):
        super().__init__()
        self.narrow, self.slices, self.buffers, self.send, self.recv = narrow, slices, buffers, send, recv
        self.z = lax.axis_index("narrow")
        self.per_chunk = narrow - 1 + 7

    def copy(self, chunk, phase, piece):
        group, at, rows = CHUNKS[chunk]
        buffer = self.buffers[group]

        def part(owner):
            return buffer.at[:, pl.ds(pl.multiple_of(owner * SLICE_ROWS + at, 8), rows), :]

        place = chunk * self.per_chunk
        if phase == 0:
            place += piece - 1
            source = self.slices.at[group, pl.ds(at, rows), :]
            target = buffer.at[piece - 1, pl.ds(pl.multiple_of(self.me * SLICE_ROWS + at, 8), rows), :]
            device = {"narrow": (self.z + self.narrow - piece) % self.narrow}
        else:
            owners = (self.me, self.first, self.second, self.third)
            place += self.narrow - 1 + (0, 1, 3)[phase - 1] + piece
            source = target = part(owners[piece])
            device = {"wide": self.base + (self.first, self.second, self.twin)[phase - 1]}
        return pltpu.make_async_remote_copy(
            src_ref=source, dst_ref=target, send_sem=self.send.at[place], recv_sem=self.recv.at[place],
            device_id=device, device_id_type=MESH,
        )

    def pieces(self, phase):
        return (range(1, self.narrow), range(1), range(2), range(4))[phase]

    def start(self, chunk, phase):
        for piece in self.pieces(phase):
            self.copy(chunk, phase, piece).start()

    def arrive(self, chunk, phase):
        for piece in self.pieces(phase):
            self.copy(chunk, phase, piece).wait_recv()

    def run(self, steps):
        for chunk, phase in steps:
            if phase > 0:
                self.arrive(chunk, phase - 1)
            self.start(chunk, phase)

    def drain(self):
        for chunk in range(len(CHUNKS)):
            for phase in range(4):
                for piece in self.pieces(phase):
                    self.copy(chunk, phase, piece).wait_send()

    def barrier(self):
        sem = pltpu.get_barrier_semaphore()
        for k in range(1, self.narrow):
            pl.semaphore_signal(
                sem, inc=1, device_id={"narrow": (self.z + k) % self.narrow}, device_id_type=MESH
            )
        for other in (self.first, self.second, self.twin):
            pl.semaphore_signal(sem, inc=1, device_id={"wide": self.base + other}, device_id_type=MESH)
        pl.semaphore_wait(sem, self.narrow - 1 + 3)


def tick(t):
    steps = ((t, 1), (t + 2, 0), (t - 1, 2), (t - 2, 3))
    return tuple((chunk, phase) for chunk, phase in steps if 0 <= chunk < len(CHUNKS))


LATE = {3: 7, 11: 8, 20: 9}
LAST = range(10, len(CHUNKS) + 2)


def attention_forward(
    sid_ref, grid_ref, tok_ref, gain_ref, shift_ref, pb_ref, own_ref, slices, table_ref, small_ref,
    prob_ref, att_ref, branch_ref, wa_ref, small_out, q_out, k_out, v_out, gath_b, gath_c,
    stage, first_in, queries, k_pad, v_pad, bias, lined, diag, far, smalls, send, recv, extra_send, extra_recv, local,
    narrow,
):
    image = pl.program_id(0)
    images = pl.num_programs(0)
    gather = Gather(narrow, slices, (stage, gath_b, gath_c), send, recv)

    def extra(which, k):
        source = diag if which else small_ref.at[k]
        target = far.at[k - 1] if which else smalls.at[k]
        place = which * (narrow - 1) + k - 1
        return pltpu.make_async_remote_copy(
            src_ref=source, dst_ref=target, send_sem=extra_send.at[place], recv_sem=extra_recv.at[place],
            device_id={"narrow": (gather.z + narrow - k) % narrow}, device_id_type=MESH,
        )

    def keep(which):
        source, target = ((queries, q_out), (k_pad, k_out), (v_pad, v_out))[which]
        return pltpu.make_async_copy(source, target, local.at[which])

    @pl.when(image == 0)
    def _():
        def bias_of(slot, at, table):
            p, s, limit, later, p_patch, s_patch = slot_masks(grid_ref[at, 0], grid_ref[at, 1], False)
            both = p_patch & s_patch
            open_key = s <= limit
            for h in range(3):
                row = h * 16 + sid_ref[at] * 2
                toep = [
                    pltpu.roll(
                        jnp.broadcast_to(table(row + which), (208, DIAG)), DIAG - 207, 1, stride=1, stride_axis=0
                    )[:, :256]
                    for which in range(2)
                ]
                c0, c1, c2 = (smalls[slot, 3:4, h * 3 + c : h * 3 + c + 1] for c in range(3))
                outer = jnp.where((p == 0) & s_patch, c0, jnp.where(p_patch & (s == 0), c1, c2))
                value = jnp.where(both, jnp.where(later, toep[0], toep[1]), outer)
                bias[at, slot * 3 + h] = jnp.where(open_key, value, MASKED).astype(BF16)

        def far_bias(slot):
            @pl.loop(0, 8)
            def _(at):
                bias_of(slot, at, lambda row: far[slot - 1, pl.ds(row, 1), :])

        def weights_of(part):
            gather.arrive(part, 3)
            for slot in range(narrow - 1):
                for pair in range(4):
                    rows = [
                        stage[slot, pl.ds((2 * pair + i) * SLICE_ROWS + part * PART_ROWS, PART_ROWS), :]
                        for i in range(2)
                    ]
                    at = (slot + 1) * 192 + pair * 2 * PART_ROWS
                    wa_ref[part, at : at + 2 * PART_ROWS, :] = jnp.concatenate(rows, axis=0).astype(BF16)

        def project(part, target, finish):
            @pl.loop(0, 8)
            def _(at):
                target[at, 0:208, :] = finish(dot_nt(first_in[at], wa_ref[part])).astype(BF16)

            keep(part).start()

        lined[...] = jnp.zeros_like(lined)
        for shape_at in range(len(GRIDS)):
            for which, row, col, at, size in windows(shape_at):
                lined[shape_at * 2 + which, :, at : at + size] = table_ref[row, :, col : col + size]
        for h in range(3):
            for r in range(16):
                diag[h * 16 + r : h * 16 + r + 1, :] = lined[r, h : h + 1, :]
        gather.barrier()
        smalls[0] = small_ref[0]
        for k in range(1, narrow):
            extra(0, k).start()
            extra(1, k).start()
        gather.run(((0, 0), (1, 0)))
        k_pad[:, 208:256, :] = jnp.zeros((8, 48, 768), BF16)
        v_pad[:, 208:256, :] = jnp.zeros((8, 48, 768), BF16)
        for part in range(4):
            wa_ref[part, 0:192, :] = own_ref[part * 192 : (part + 1) * 192, :]

        @pl.loop(0, 8)
        def _(at):
            normed, _ = norm_stats(tok_ref[at].astype(F32))
            first_in[at] = (normed * gain_ref[...] + shift_ref[...]).astype(BF16)
            bias_of(0, at, lambda row: diag[pl.ds(row, 1), :])

        gather.run(tick(0))
        for k in range(1, narrow):
            extra(0, k).wait_recv()
            extra(1, k).wait_recv()
        far_bias(1)
        gather.run(tick(1))
        far_bias(2)
        gather.run(tick(2))
        far_bias(3)
        gather.run(tick(3))
        q_bias = sum(smalls[k, 0:1, :] for k in range(narrow))
        v_bias = sum(smalls[k, 1:2, :] for k in range(narrow))
        small_out[...] = smalls[...]
        weights_of(0)
        project(0, queries, lambda v: (v + q_bias) * (HD ** -0.5))
        gather.run(tick(4))
        weights_of(1)
        project(1, k_pad, lambda v: v)
        gather.run(tick(5))
        weights_of(2)
        project(2, v_pad, lambda v: v + v_bias)
        gather.run(tick(6))
        weights_of(3)

    head_of = lax.broadcasted_iota(jnp.int32, (1, 256), 1) // HD

    @pl.loop(0, 3)
    def _(group):
        for when, t in LATE.items():
            @pl.when(image * 3 + group == when)
            def _():
                gather.run(tick(t))

        lanes = pl.ds(pl.multiple_of(group * 256, 256), 256)
        q_group = queries[image, :, lanes]
        k_group = k_pad[image, :, lanes]
        v_group = v_pad[image, :, lanes]
        stacked = jnp.concatenate(
            [jnp.where(head_of == h, q_group, jnp.zeros_like(q_group)) for h in range(4)], axis=0
        )
        raw = dot_nt(stacked, k_group)
        probs = []
        for h in range(4):
            head = group * 4 + h
            scores = raw[h * 208 : (h + 1) * 208, :] + bias[image, head].astype(F32)
            top = jnp.max(scores, axis=-1, keepdims=True)
            raised = jnp.exp(scores - top)
            prob = (raised * (1.0 / jnp.sum(raised, axis=-1, keepdims=True))).astype(BF16)
            prob_ref[0, head] = prob
            probs.append(prob)
        mixed = dot_nn(jnp.concatenate(probs, axis=0), v_group)
        out = mixed[0:208]
        for h in range(1, 4):
            out = jnp.where(head_of == h, mixed[h * 208 : (h + 1) * 208], out)
        att_ref[0, :, lanes] = out.astype(BF16)

    branch_ref[0] = dot_nn(att_ref[0], wa_ref[3]) + pb_ref[...]

    @pl.when(image == images - 1)
    def _():
        for t in LAST:
            gather.run(tick(t))
        for chunk in range(4, len(CHUNKS)):
            gather.arrive(chunk, 3)
        gather.drain()
        for k in range(1, narrow):
            extra(0, k).wait_send()
            extra(1, k).wait_send()
        for which in range(3):
            keep(which).wait()


class Reduce:
    STEPS = 7

    def __init__(self, near, beyond, source, half, quarter, eighth, between, total, send, recv, first_sem):
        self.near, self.beyond, self.source, self.total = near, beyond, source, total
        self.half, self.quarter, self.eighth, self.between = half, quarter, eighth, between
        self.send, self.recv, self.first_sem = send, recv, first_sem
        self.rows = eighth.shape[0]

    @staticmethod
    def scratch(rows, width, beyond):
        shapes = [(rows // 2, width), (rows // 4, width), (rows // 8, width), (2 * max(beyond, 1), rows // 8, width)]
        return [pltpu.VMEM(shape, F32) for shape in shapes]

    def span(self, ref, start, count):
        return ref.at[pl.ds(pl.multiple_of(start, 8), count), :]

    def value(self, ref, start, count):
        return ref[pl.ds(pl.multiple_of(start, 8), count), :]

    def copy(self, step):
        near, rows = self.near, self.rows
        half_at = near.core * 4 * rows
        quarter_at = half_at + near.first_bit * 2 * rows
        own_at = quarter_at + near.second_bit * rows
        if step == 0:
            source, target, to = self.span(self.source, (1 - near.core) * 4 * rows, 4 * rows), self.half, near.twin
        elif step == 1:
            source, target, to = (
                self.span(self.half, (1 - near.first_bit) * 2 * rows, 2 * rows), self.quarter, near.first
            )
        elif step == 2:
            source, target, to = self.span(self.quarter, (1 - near.second_bit) * rows, rows), self.eighth, near.second
        else:
            at, count, to = (
                (own_at, rows, near.second), (quarter_at, 2 * rows, near.first), (half_at, 4 * rows, near.twin)
            )[step - 3]
            source = target = self.span(self.total, at, count)
        return self.remote(source, target, step, near.base + to)

    def remote(self, source, target, place, to):
        place += self.first_sem
        return pltpu.make_async_remote_copy(
            src_ref=source, dst_ref=target, send_sem=self.send.at[place], recv_sem=self.recv.at[place],
            device_id={"wide": to}, device_id_type=MESH,
        )

    def run(self, step):
        near, rows = self.near, self.rows
        if step > 0:
            self.copy(step - 1).wait_recv()
        if step == 1:
            self.half[...] += self.value(self.source, near.core * 4 * rows, 4 * rows)
        if step == 2:
            self.quarter[...] += self.value(self.half, near.first_bit * 2 * rows, 2 * rows)
        if step == 3:
            summed = self.eighth[...] + self.value(self.quarter, near.second_bit * rows, rows)
            for i in range(self.beyond):
                self.between[2 * i] = summed
                copy = self.remote(self.between.at[2 * i], self.between.at[2 * i + 1], 6 + i, near.beyond(i))
                copy.start()
                copy.wait()
                summed = self.between[2 * i] + self.between[2 * i + 1]
            own_at = (near.core * 4 + near.first_bit * 2 + near.second_bit) * rows
            self.total[pl.ds(pl.multiple_of(own_at, 8), rows), :] = summed
        if step < 6:
            self.copy(step).start()

    def drain(self):
        for step in range(6):
            self.copy(step).wait_send()


def greet(near, beyond):
    sem = pltpu.get_barrier_semaphore()
    for k in range(1, SLICES):
        other = near.base + (near.me + k) % SLICES
        pl.semaphore_signal(sem, inc=1, device_id={"wide": other}, device_id_type=MESH)
    for i in range(beyond):
        pl.semaphore_signal(sem, inc=1, device_id={"wide": near.beyond(i)}, device_id_type=MESH)
    pl.semaphore_wait(sem, SLICES - 1 + beyond)


PAIR = 2
FF_TICKS = {
    4: ((0, 0), (1, 0)), 5: ((0, 1), (1, 1)), 7: ((0, 2),), 9: ((1, 2), (0, 3)), 10: ((0, 4), (1, 3)), 12: ((0, 5), (1, 4)),
    14: ((1, 5),), 15: ((0, 6),),
}


def feed_forward(
    grid_ref, tok_ref, branch_ref, cot_ref, vec_ref, small_ref, ownb_ref, ownc_ref, gath_b, gath_c,
    out_ref, mg_ref, out_b, out_c, sums_ref,
    total_b, total_c, stage, wb, wc, second_ins, branch_lows, mlp_acc, second_acc, grad_b, grad_c, *rest, beyond,
):
    loads, send, recv = rest[8:]
    slot, pair = pl.program_id(0), pl.program_id(1)
    slots, pairs = pl.num_programs(0), pl.num_programs(1)
    rows = PAIR * 208
    near = Neighbours()
    sums = [
        Reduce(near, beyond, grad, *rest[4 * i : 4 * i + 4], total, send, recv, i * (6 + beyond))
        for i, (grad, total) in enumerate(((grad_b, total_b), (grad_c, total_c)))
    ]

    def load(which, at):
        return pltpu.make_async_copy((gath_b, gath_c)[which].at[at], stage.at[which], loads.at[which])

    @pl.when((slot == 0) & (pair == 0))
    def _():
        greet(near, beyond)
        wb[0] = ownb_ref[...]
        wc[0] = ownc_ref[...]
        grad_b[...] = jnp.zeros_like(grad_b)
        grad_c[...] = jnp.zeros_like(grad_c)
        sums_ref[...] = jnp.zeros_like(sums_ref)

    @pl.when((pair == 0) & (slot < slots - 1))
    def _():
        load(0, slot).start()
        load(1, slot).start()

    for when, steps in FF_TICKS.items():
        @pl.when(slot * pairs + pair == when)
        def _():
            for chain, step in steps:
                sums[chain].run(step)

    attn_scale, second_gain, second_shift, mlp_scale, down_bias = (vec_ref[i : i + 1, :] for i in range(5))

    def residual():
        branch = branch_ref[...].reshape(rows, 768)
        return branch, tok_ref[...].reshape(rows, 768).astype(F32) + attn_scale * branch

    def masked_cotangent():
        at = lax.broadcasted_iota(jnp.int32, (rows, 1), 0)
        limit = jnp.zeros((rows, 1), jnp.int32)
        for i in range(PAIR):
            image = pair * PAIR + i
            inside = (at >= i * 208) & (at < (i + 1) * 208)
            limit = jnp.where(inside, grid_ref[image, 0] * grid_ref[image, 1] + i * 208, limit)
        return jnp.where(at <= limit, cot_ref[...].reshape(rows, 768).astype(F32), 0.0)

    @pl.when(slot == 0)
    def _():
        _, middle = residual()
        normed, _ = norm_stats(middle)
        second_ins[pair] = (normed * second_gain + second_shift).astype(BF16)
        branch_lows[pair] = (masked_cotangent() * mlp_scale).astype(BF16)
        mlp_acc[pair] = jnp.zeros((rows, 768), F32)
        second_acc[pair] = jnp.zeros((rows, 768), F32)

    second_in, branch_low = second_ins[pair], branch_lows[pair]
    up, down = wb[slot % 2], wc[slot % 2]
    up_pre = dot_nn(second_in, up) + small_ref[slot, 2:3, :]
    cdf = 0.5 * (1.0 + lax.erf(up_pre * INV_ROOT_TWO))
    hidden = (up_pre * cdf).astype(BF16)
    slope = cdf + up_pre * jnp.exp(-0.5 * up_pre * up_pre) * INV_ROOT_TWO_PI
    mlp_acc[pair] += dot_nn(hidden, down)
    pre_low = (dot_nt(branch_low, down) * slope).astype(BF16)
    second_acc[pair] += dot_nt(pre_low, up)

    @pl.when(slot == 0)
    def _():
        grad_c[...] += dot_tn(hidden, branch_low)
        grad_b[...] += dot_tn(second_in, pre_low)
        sums_ref[6] += fold_rows(pre_low.astype(F32))

    @pl.when((pair == pairs - 1) & (slot < slots - 1))
    def _():
        for which, weights in enumerate((wb, wc)):
            load(which, slot).wait()
            weights[(slot + 1) % 2] = stage[which].astype(BF16)

    @pl.when(slot == slots - 1)
    def _():
        branch, middle = residual()
        normed, inv = norm_stats(middle)
        out_grad = masked_cotangent()
        mlp_branch = mlp_acc[pair] + down_bias
        out_ref[...] = (middle + mlp_scale * mlp_branch).astype(BF16).reshape(PAIR, 208, 768)
        second_grad = second_acc[pair]
        middle_grad = out_grad + norm_back(second_grad, normed, inv, second_gain)
        mg_ref[...] = middle_grad.reshape(PAIR, 208, 768)
        sums_ref[0] += fold_rows(out_grad * mlp_branch)
        sums_ref[1] += fold_rows(out_grad)
        sums_ref[2] += fold_rows(second_grad * normed)
        sums_ref[3] += fold_rows(second_grad)
        sums_ref[4] += fold_rows(middle_grad * branch)
        sums_ref[5] += fold_rows(middle_grad)

    @pl.when((slot == slots - 1) & (pair == pairs - 1))
    def _():
        sums[1].run(6)
        copies = [
            pltpu.make_async_copy(chain.total, out, loads.at[i])
            for i, (chain, out) in enumerate(zip(sums, (out_b, out_c)))
        ]
        for copy in copies:
            copy.start()
        for copy in copies:
            copy.wait()
        for chain in sums:
            chain.drain()


SMALL_ROWS = 128
AB_TICKS = {8: (0,), 10: (1,), 13: (2,), 15: (3,)}
AB_LAST = (4, 5, 6)


def attention_backward(
    sid_ref, grid_ref, tok_ref, mg_ref, att_ref, q0_ref, k0_ref, v0_ref, p0_ref, q_ref, k_ref, v_ref, p1_ref, p2_ref,
    vec_ref, wa_ref, ff_sums_ref,
    tg_ref, total_out, late_total,
    total, grads, attn_lows, kept, dq, dk, dv, lines, edges, sums, late, late_in, late_between,
    half, quarter, eighth, between, send, recv, late_send, late_recv, local, beyond,
):
    step = pl.program_id(0)
    images = pl.num_programs(0) // 2
    near = Neighbours()
    reduction = Reduce(near, beyond, grads, half, quarter, eighth, between, total, send, recv, 0)
    attn_scale, first_gain, first_shift = (vec_ref[i : i + 1, :] for i in range(3))
    head_of = lax.broadcasted_iota(jnp.int32, (1, 256), 1) // HD

    def stack(group):
        return jnp.concatenate([jnp.where(head_of == h, group, jnp.zeros_like(group)) for h in range(4)], axis=0)

    def merge(mixed):
        out = mixed[0:208]
        for h in range(1, 4):
            out = jnp.where(head_of == h, mixed[h * 208 : (h + 1) * 208], out)
        return out

    def heads_back(q_group, k_group, v_group, g_group, prob_at, each):
        q_stack, g_stack = stack(q_group), stack(g_group)
        prob_grads = dot_nt(g_stack, v_group)
        lows = []
        for h in range(4):
            prob = prob_at(h).astype(F32)
            prob_grad = prob_grads[h * 208 : (h + 1) * 208]
            score_grad = prob * (prob_grad - jnp.sum(prob * prob_grad, axis=-1, keepdims=True))
            low = score_grad.astype(BF16)
            lows.append(low)
            each(h, score_grad, low)
        low_stack = jnp.concatenate(lows, axis=0)
        prob_stack = jnp.concatenate([prob_at(h) for h in range(4)], axis=0)
        return (
            merge(dot_nn(low_stack, k_group)).astype(BF16) * jnp.asarray(HD ** -0.5, BF16),
            dot_tn(low_stack, q_stack)[0:208].astype(BF16),
            dot_tn(prob_stack, g_stack)[0:208].astype(BF16),
        )

    @pl.when(step == 0)
    def _():
        greet(near, beyond)
        grads[...] = jnp.zeros_like(grads)
        sums[...] = jnp.zeros_like(sums)
        lines[...] = jnp.zeros_like(lines)
        edges[...] = jnp.zeros_like(edges)
        late[...] = jnp.zeros_like(late)

    normed, inv = norm_stats(tok_ref[0].astype(F32))

    @pl.when(step < images)
    def _():
        attn_low = (mg_ref[0] * attn_scale).astype(BF16)
        attn_lows[step] = attn_low
        g_group = dot_nt(attn_low, wa_ref[3, 0:256, :]).astype(BF16)
        grads[576:768, :] += dot_tn(att_ref[0], attn_low)[0:192, :]
        p, s, limit, later, p_patch, s_patch = slot_masks(grid_ref[step, 0], grid_ref[step, 1], True)
        both = p_patch & s_patch
        flip = (
            lax.broadcasted_iota(jnp.int32, (208, 208), 0) + lax.broadcasted_iota(jnp.int32, (208, 208), 1) == 207
        ).astype(BF16)
        kind = sid_ref[step]

        def table_grad(h, score_grad, low):
            if h == 3:
                return
            rest = (score_grad - low.astype(F32)).astype(BF16)
            turned = dot_nn(flip, low) + dot_nn(flip, rest)
            patches = jnp.where(both, turned, 0.0)
            edge = turned - patches
            for which, part in enumerate((jnp.where(later, patches, 0.0), jnp.where(later, 0.0, patches))):
                wide = jnp.concatenate([part, jnp.zeros((208, 256), F32)], axis=1)
                folded = jnp.sum(pltpu.roll(wide, 0, 1, stride=1, stride_axis=0), axis=0, keepdims=True)
                row = which * 3 + h
                for shape_at in range(len(GRIDS)):
                    lines[shape_at, row : row + 1, :] += jnp.where(kind == shape_at, folded, 0.0)
            class_query = jnp.where((p == 0) & s_patch, edge, 0.0)
            class_key = jnp.where(p_patch & (s == 0), edge, 0.0)
            for at, part in enumerate((class_query, class_key, edge - class_query - class_key)):
                edges[at * 3 + h] += fold_rows(part)

        own = heads_back(q0_ref[0], k0_ref[0], v0_ref[0], g_group, lambda h: p0_ref[0, h], table_grad)
        first_in = (normed * first_gain + first_shift).astype(BF16)
        for c, grad in enumerate(own):
            kept[c, step] = grad
            grads[c * 192 : (c + 1) * 192, :] += dot_tn(grad, first_in)[0:192, :]
        sums[0] += fold_rows(own[0].astype(F32))
        sums[1] += fold_rows(own[2].astype(F32))

    @pl.when(step == images)
    def _():
        grads[768 : 768 + SMALL_ROWS, :] = jnp.zeros((SMALL_ROWS, 768), F32)
        for shape_at in range(len(GRIDS)):
            grads[768 + shape_at * 8 : 776 + shape_at * 8, 0:DIAG] = lines[shape_at]
        for at in range(9):
            grads[832 + at : 833 + at, 0:256] = jnp.sum(edges[at], axis=0, keepdims=True)
        for at in range(2):
            grads[848 + at : 849 + at, 0:256] = jnp.sum(sums[at], axis=0, keepdims=True)
        for at in range(7):
            grads[856 + at : 857 + at, :] = jnp.sum(ff_sums_ref[at], axis=0, keepdims=True)

    for when, steps in AB_TICKS.items():
        @pl.when(step == when)
        def _():
            for at in steps:
                reduction.run(at)

    @pl.when(step >= images)
    def _():
        image = step - images
        attn_low = attn_lows[image]
        for c, ref in enumerate((dq, dk, dv)):
            ref[:, 0:256] = kept[c, image]
        for group in (1, 2):
            lanes = slice(group * 256, group * 256 + 256)
            g_group = dot_nt(attn_low, wa_ref[3, lanes, :]).astype(BF16)
            probs = (p1_ref, p2_ref)[group - 1]
            parts = heads_back(
                q_ref[0, :, lanes], k_ref[0, :, lanes], v_ref[0, :, lanes], g_group,
                lambda h: probs[0, h], lambda *_: None,
            )
            for ref, part in zip((dq, dk, dv), parts):
                ref[:, lanes] = part
        first_grad = dot_nn(dq[...], wa_ref[0]) + dot_nn(dk[...], wa_ref[1]) + dot_nn(dv[...], wa_ref[2])
        tg_ref[0] = mg_ref[0] + norm_back(first_grad, normed, inv, first_gain)
        late[0:8, :] += fold_rows(first_grad * normed)
        late[8:16, :] += fold_rows(first_grad)

    @pl.when(step == 2 * images - 1)
    def _():
        copies = [
            pltpu.make_async_remote_copy(
                src_ref=late, dst_ref=late_in.at[k - 1], send_sem=late_send.at[k - 1], recv_sem=late_recv.at[k - 1],
                device_id={"wide": near.base + (near.me + k) % SLICES}, device_id_type=MESH,
            )
            for k in range(1, SLICES)
        ]
        for copy in copies:
            copy.start()
        for at in AB_LAST:
            reduction.run(at)
        for copy in copies:
            copy.wait()
        summed = late[...]
        for k in range(SLICES - 1):
            summed = summed + late_in[k]
        for i in range(beyond):
            late_between[2 * i] = summed
            copy = pltpu.make_async_remote_copy(
                src_ref=late_between.at[2 * i], dst_ref=late_between.at[2 * i + 1],
                send_sem=late_send.at[SLICES - 1 + i], recv_sem=late_recv.at[SLICES - 1 + i],
                device_id={"wide": near.beyond(i)}, device_id_type=MESH,
            )
            copy.start()
            copy.wait()
            summed = late_between[2 * i] + late_between[2 * i + 1]
        late_total[...] = summed
        copy = pltpu.make_async_copy(total, total_out, local.at[0])
        copy.start()
        copy.wait()
        reduction.drain()


def make_body(wide_size, narrow_size):
    def body(
        tokens, grid_shape, first_gain, first_shift, qkv_weight, query_bias, value_bias, rel_table, proj_weight,
        proj_bias, attn_scale, second_gain, second_shift, up_weight, up_bias, down_weight, down_bias, mlp_scale,
        cotangent,
    ):
        images, slots, width = tokens.shape
        heads, table_size = rel_table.shape
        local = heads * HD
        own_a = jnp.concatenate(
            [jnp.transpose(qkv_weight, (0, 2, 1)).reshape(3 * local, width), proj_weight], axis=0
        )
        table = rel_table.astype(F32)
        square = table[:, : SPAN * SPAN].reshape(heads, SPAN, SPAN)[:, ::-1, ::-1]
        square = jnp.pad(jnp.transpose(square, (1, 0, 2)), ((0, 0), (0, 8 - heads), (0, 128 - SPAN)))

        def small_for(k):
            def at(v, start):
                return jnp.pad(v.astype(F32).reshape(1, -1), ((0, 0), (start, width - start - v.size)))

            return jnp.concatenate(
                [
                    at(query_bias, k * local), at(value_bias, k * local), at(up_bias, 0),
                    at(table[:, SPAN * SPAN :].reshape(-1), 0), jnp.zeros((4, width), F32),
                ]
            )

        small = jnp.stack([small_for(k) for k in range(narrow_size)])
        all_heads = narrow_size * heads

        kinds = jnp.array(GRIDS, jnp.int32)
        sid = jnp.argmax(jnp.all(grid_shape[:, None, :] == kinds[None], axis=-1), axis=-1).astype(jnp.int32)

        def row(v):
            return v.astype(F32).reshape(1, -1)

        smem = pl.BlockSpec(memory_space=pltpu.SMEM)
        anyspace = pl.BlockSpec(memory_space=pl.ANY)
        vmem = pl.BlockSpec(memory_space=pltpu.VMEM)

        def whole(*shape):
            return pl.BlockSpec(shape, lambda i, *_: (0,) * len(shape))

        def per_image(*shape):
            return pl.BlockSpec((1,) + shape, lambda i, *_: (i,) + (0,) * len(shape))

        def struct(*shape, dtype=F32):
            return jax.ShapeDtypeStruct(shape, dtype)

        params = pltpu.CompilerParams(vmem_limit_bytes=VMEM_LIMIT, dimension_semantics=("arbitrary",))
        copies = len(CHUNKS) * (narrow_size - 1 + 7)
        copies = len(CHUNKS) * (narrow_size - 1 + 7)
        me = lax.axis_index("wide") % SLICES
        slices = jnp.stack(
            [lax.dynamic_slice_in_dim(own_a.reshape(4, local, width), me * PART_ROWS, PART_ROWS, 1).reshape(-1, width)]
            + [lax.dynamic_slice_in_dim(w, me * SLICE_ROWS, SLICE_ROWS, 0) for w in (up_weight, down_weight)]
        ).astype(F32)
        probs, attended, branch, weights_a, small, queries, keys, values, gath_b, gath_c = pl.pallas_call(
            functools.partial(attention_forward, narrow=narrow_size),
            grid=(images,),
            in_specs=[smem, smem, vmem] + [whole(1, width)] * 3 + [vmem] * 4,
            out_specs=[per_image(all_heads, slots, 256), per_image(slots, width), per_image(slots, width)]
            + [vmem, vmem] + [anyspace] * 5,
            scratch_shapes=[
                pltpu.VMEM((narrow_size - 1, width, width), F32),
                pltpu.VMEM((images, slots, width), BF16),
                pltpu.VMEM((images, slots, width), BF16),
                pltpu.VMEM((images, 256, width), BF16),
                pltpu.VMEM((images, 256, width), BF16),
                pltpu.VMEM((images, all_heads, slots, 256), BF16),
                pltpu.VMEM((16, 8, DIAG), F32),
                pltpu.VMEM((48, DIAG), F32),
                pltpu.VMEM((narrow_size - 1, 48, DIAG), F32),
                pltpu.VMEM((narrow_size, 8, width), F32),
                pltpu.SemaphoreType.DMA((copies,)),
                pltpu.SemaphoreType.DMA((copies,)),
                pltpu.SemaphoreType.DMA((2 * narrow_size - 2,)),
                pltpu.SemaphoreType.DMA((2 * narrow_size - 2,)),
                pltpu.SemaphoreType.DMA((3,)),
            ],
            out_shape=[
                struct(images, all_heads, slots, 256, dtype=BF16),
                struct(images, slots, width, dtype=BF16),
                struct(images, slots, width),
                struct(4, width, width, dtype=BF16),
                struct(narrow_size, 8, width),
                struct(images, slots, width, dtype=BF16),
                struct(images, 256, width, dtype=BF16),
                struct(images, 256, width, dtype=BF16),
                struct(narrow_size - 1, width, width),
                struct(narrow_size - 1, width, width),
            ],
            compiler_params=pltpu.CompilerParams(
                vmem_limit_bytes=VMEM_LIMIT, dimension_semantics=("arbitrary",), collective_id=0,
                has_side_effects=True,
            ),
            name="attention_forward",
        )(
            sid, grid_shape, tokens, row(first_gain), row(first_shift), row(proj_bias), own_a, slices, square, small,
        )

        vec = jnp.concatenate([row(v) for v in (attn_scale, second_gain, second_shift, mlp_scale, down_bias)])
        beyond = (wide_size // SLICES).bit_length() - 1
        rows = PAIR * slots
        pairs = images // PAIR
        last = narrow_size - 1

        def remote_params(at):
            return pltpu.CompilerParams(
                vmem_limit_bytes=VMEM_LIMIT, collective_id=at, has_side_effects=True,
            )

        ends = pl.BlockSpec((PAIR, slots, width), lambda s, i: (jnp.where((s > 0) & (s < last), pairs - 1, i), 0, 0))
        outs = pl.BlockSpec((PAIR, slots, width), lambda s, i: (jnp.where(s < last, 0, i), 0, 0))
        layer_out, middle_grad, grad_b, grad_c, sums = pl.pallas_call(
            functools.partial(feed_forward, beyond=beyond),
            grid=(narrow_size, pairs),
            in_specs=[smem] + [ends] * 3 + [vmem] * 4 + [anyspace] * 2,
            out_specs=[outs] * 2 + [anyspace] * 2 + [vmem],
            scratch_shapes=[
                pltpu.VMEM((width, width), F32),
                pltpu.VMEM((width, width), F32),
                pltpu.VMEM((2, width, width), F32),
                pltpu.VMEM((2, width, width), BF16),
                pltpu.VMEM((2, width, width), BF16),
                pltpu.VMEM((pairs, rows, width), BF16),
                pltpu.VMEM((pairs, rows, width), BF16),
                pltpu.VMEM((pairs, rows, width), F32),
                pltpu.VMEM((pairs, rows, width), F32),
                pltpu.VMEM((width, width), F32),
                pltpu.VMEM((width, width), F32),
            ]
            + Reduce.scratch(width, width, beyond) * 2
            + [
                pltpu.SemaphoreType.DMA((2,)),
                pltpu.SemaphoreType.DMA((2 * (6 + beyond),)),
                pltpu.SemaphoreType.DMA((2 * (6 + beyond),)),
            ],
            out_shape=[
                struct(images, slots, width, dtype=BF16),
                struct(images, slots, width),
                struct(width, width),
                struct(width, width),
                struct(7, 8, width),
            ],
            compiler_params=remote_params(1),
            name="feed_forward",
        )(grid_shape, tokens, branch, cotangent, vec, small, up_weight, down_weight, gath_b, gath_c)

        def first_pass(*shape):
            return pl.BlockSpec((1,) + shape, lambda i: (jnp.minimum(i, images - 1),) + (0,) * len(shape))

        def second_pass(*shape, at=0):
            return pl.BlockSpec((1,) + shape, lambda i: (jnp.maximum(i - images, 0), at) + (0,) * (len(shape) - 1))

        both_passes = pl.BlockSpec((1, slots, width), lambda i: (i % images, 0, 0))
        total_rows = width + SMALL_ROWS
        vec = jnp.concatenate([row(v) for v in (attn_scale, first_gain, first_shift)])
        tokens_grad, total, late = pl.pallas_call(
            functools.partial(attention_backward, beyond=beyond),
            grid=(2 * images,),
            in_specs=[smem, smem, both_passes, both_passes]
            + [first_pass(slots, 256)] * 2
            + [first_pass(256, 256)] * 2
            + [first_pass(4, slots, 256)]
            + [second_pass(slots, width), second_pass(256, width), second_pass(256, width)]
            + [second_pass(4, slots, 256, at=1), second_pass(4, slots, 256, at=2)]
            + [vmem] * 3,
            out_specs=[second_pass(slots, width), anyspace, vmem],
            scratch_shapes=[
                pltpu.VMEM((total_rows, width), F32),
                pltpu.VMEM((total_rows, width), F32),
                pltpu.VMEM((images, slots, width), BF16),
                pltpu.VMEM((3, images, slots, 256), BF16),
                pltpu.VMEM((slots, width), BF16),
                pltpu.VMEM((slots, width), BF16),
                pltpu.VMEM((slots, width), BF16),
                pltpu.VMEM((len(GRIDS), 8, DIAG), F32),
                pltpu.VMEM((9, 8, 256), F32),
                pltpu.VMEM((2, 8, 256), F32),
                pltpu.VMEM((16, width), F32),
                pltpu.VMEM((SLICES - 1, 16, width), F32),
                pltpu.VMEM((2 * max(beyond, 1), 16, width), F32),
            ]
            + Reduce.scratch(total_rows, width, beyond)
            + [
                pltpu.SemaphoreType.DMA((6 + beyond,)),
                pltpu.SemaphoreType.DMA((6 + beyond,)),
                pltpu.SemaphoreType.DMA((SLICES - 1 + beyond,)),
                pltpu.SemaphoreType.DMA((SLICES - 1 + beyond,)),
                pltpu.SemaphoreType.DMA((1,)),
            ],
            out_shape=[struct(images, slots, width), struct(total_rows, width), struct(16, width)],
            compiler_params=remote_params(2),
            name="attention_backward",
        )(
            sid, grid_shape, tokens, middle_grad, attended, queries, keys, values, probs, queries, keys, values, probs,
            probs, vec, weights_a, sums,
        )

        grad_a = total[:width]
        lines = total[width : width + 64, :DIAG].reshape(len(GRIDS), 8, DIAG)[:, : 2 * heads]
        lines = jnp.pad(lines.reshape(len(GRIDS), 2, heads, DIAG), ((0, 0), (0, 0), (0, 8 - heads), (0, 0)))
        square_grad = pl.pallas_call(
            undiag_kernel, out_shape=struct(SPAN, 8, 128), name="undiag"
        )(lines)
        square_grad = jnp.transpose(square_grad[:, :heads, :SPAN], (1, 0, 2))[:, ::-1, ::-1]
        edges = jnp.sum(total[width + 64 : width + 73, :256], axis=1).reshape(3, heads).T
        table_grad = jnp.concatenate([square_grad.reshape(heads, SPAN * SPAN), edges], axis=1)
        more = total[width + 80 : width + 82, :local]
        sums = total[width + 88 : width + 95]
        late = jnp.sum(late.reshape(2, 8, width), axis=1)
        qkv_grad = jnp.transpose(grad_a[: 3 * local].reshape(3, local, width), (0, 2, 1))
        return (
            layer_out,
            tokens_grad,
            late[0],
            late[1],
            qkv_grad,
            more[0],
            more[1],
            table_grad,
            grad_a[3 * local :],
            sums[5] * attn_scale.astype(F32),
            sums[4],
            sums[2],
            sums[3],
            grad_b,
            sums[6],
            grad_c,
            sums[1] * mlp_scale.astype(F32),
            sums[0],
        )

    return body


def solution(mesh):
    rows = P("wide", None, None)
    return jax.shard_map(
        make_body(mesh.shape["wide"], mesh.shape["narrow"]),
        mesh=mesh,
        in_specs=(
            rows, P("wide", None), P(), P(), P(None, None, "narrow"), P("narrow"), P("narrow"), P("narrow", None),
            P("narrow", None), P(), P(), P(), P(), P(None, "narrow"), P("narrow"), P("narrow", None), P(), P(), rows,
        ),
        out_specs=(
            rows, rows, P(), P(), P(None, None, "narrow"), P("narrow"), P("narrow"), P("narrow", None),
            P("narrow", None), P(), P(), P(), P(), P(None, "narrow"), P("narrow"), P("narrow", None), P(), P(),
        ),
        check_vma=False,
    )
```

```python
import functools

import jax
import jax.numpy as jnp
from jax import lax
from jax.experimental import pallas as pl
from jax.experimental.pallas import tpu as pltpu
from jax.sharding import PartitionSpec as P

HD = 64
MAXG = 24
SPAN = 2 * MAXG - 1
EPSILON = 1e-06
MASKED = -1e30
INV_ROOT_TWO = 0.7071067811865476
INV_ROOT_TWO_PI = 0.3989422804014327
GRIDS = ((14, 14), (10, 20), (20, 10), (8, 24), (24, 8), (12, 16), (16, 12), (13, 15))
DIAG = 512
F32 = jnp.float32
BF16 = jnp.bfloat16
VMEM_LIMIT = 60 * 1024 * 1024


def dot_nn(a, b):
    return lax.dot_general(a, b, (((1,), (0,)), ((), ())), preferred_element_type=F32)


def dot_nt(a, b):
    return lax.dot_general(a, b, (((1,), (1,)), ((), ())), preferred_element_type=F32)


def dot_tn(a, b):
    return lax.dot_general(a, b, (((0,), (0,)), ((), ())), preferred_element_type=F32)


def row_mean(v):
    return jnp.sum(v, axis=-1, keepdims=True) * (1.0 / v.shape[-1])


def norm_stats(v):
    centred = v - row_mean(v)
    inv = lax.rsqrt(row_mean(centred * centred) + EPSILON)
    return centred * inv, inv


def norm_back(incoming, normed, inv, gain):
    scaled = incoming * gain
    return inv * (scaled - row_mean(scaled) - normed * row_mean(scaled * normed))


def fold_rows(v):
    rows = v.shape[0]
    return jnp.sum(v.reshape(rows // 8, 8, v.shape[1]), axis=0)


def windows(shape_at):
    high, wide = GRIDS[shape_at]
    centre = MAXG - 1
    for m in range(-high, high):
        at = 207 + m * wide
        if m > -high:
            yield 0, centre + m, centre, at, wide
        if m < high - 1:
            yield 1, centre + 1 + m, centre + 1 - wide, at + 1, wide - 1


def undiag_kernel(diag_ref, out_ref):
    out_ref[...] = jnp.zeros_like(out_ref)
    for shape_at in range(len(GRIDS)):
        for which, row, col, at, size in windows(shape_at):
            out_ref[row, :, col : col + size] += diag_ref[shape_at, which, :, at : at + size]


def slot_masks(high, wide, reverse):
    rows = lax.broadcasted_iota(jnp.int32, (208, 1), 0)
    p = 207 - rows if reverse else rows
    s = lax.broadcasted_iota(jnp.int32, (1, 256), 1)
    limit = high * wide
    wide_f = wide.astype(F32)

    def column(slot):
        patch = (slot - 1).astype(F32)
        return patch - wide_f * jnp.floor((patch + 0.5) / wide_f)

    later = column(s) >= column(p)
    p_patch = (p >= 1) & (p <= limit)
    s_patch = (s >= 1) & (s <= limit)
    return p, s, limit, later, p_patch, s_patch


MESH = pl.DeviceIdType.MESH
SLICES = 8
SLICE_ROWS = 96
PART_ROWS = 24


def chunks_of(narrow):
    all_shards = tuple(range(1, narrow))
    rows = [(group, at, 24, all_shards) for group in range(2) for at in (0, 24, 48, 72)]
    return tuple(rows) + tuple((2, 0, SLICE_ROWS, (k,)) for k in all_shards)


ROW_CHUNKS = 8


class Neighbours:
    def __init__(self):
        self.wide = lax.axis_index("wide")
        self.me = self.wide % SLICES
        self.base = self.wide - self.me
        self.core = core = self.me % 2
        x_bit, y_bit = (self.me // 2) % 2, self.me // 4
        over_x, over_y = self.me + 2 - 4 * x_bit, self.me + 4 - 8 * y_bit
        self.first = over_x * (1 - core) + over_y * core
        self.second = over_y * (1 - core) + over_x * core
        self.first_bit = x_bit * (1 - core) + y_bit * core
        self.second_bit = y_bit * (1 - core) + x_bit * core
        self.third = over_x + over_y - self.me
        self.twin = self.me + 1 - 2 * core

    def beyond(self, step):
        size = SLICES << step
        return self.wide + size - 2 * size * ((self.wide // size) % 2)


class Gather(Neighbours):
    def __init__(self, narrow, slices, buffers, send, recv, done=()):
        super().__init__()
        self.done = done
        self.narrow, self.slices, self.buffers, self.send, self.recv = narrow, slices, buffers, send, recv
        self.z = lax.axis_index("narrow")
        self.chunks = chunks_of(narrow)
        self.per_chunk = narrow - 1 + 7
        self.started = []

    def copy(self, chunk, phase, piece):
        group, at, rows, shards = self.chunks[chunk]
        buffer = self.buffers[group]

        def part(owner):
            return buffer.at[
                pl.ds(shards[0] - 1, len(shards)), pl.ds(pl.multiple_of(owner * SLICE_ROWS + at, 8), rows), :
            ]

        place = chunk * self.per_chunk
        if phase == 0:
            place += piece - 1
            source = self.slices.at[group, pl.ds(at, rows), :]
            target = buffer.at[piece - 1, pl.ds(pl.multiple_of(self.me * SLICE_ROWS + at, 8), rows), :]
            device = {"narrow": (self.z + self.narrow - piece) % self.narrow}
        else:
            owners = (self.me, self.first, self.second, self.third)
            place += self.narrow - 1 + (0, 1, 3)[phase - 1] + piece
            source = target = part(owners[piece])
            device = {"wide": self.base + (self.first, self.second, self.twin)[phase - 1]}
        return pltpu.make_async_remote_copy(
            src_ref=source, dst_ref=target, send_sem=self.send.at[place], recv_sem=self.recv.at[place],
            device_id=device, device_id_type=MESH,
        )

    def pieces(self, chunk, phase):
        return (self.chunks[chunk][3], range(1), range(2), range(4))[phase]

    def start(self, chunk, phase):
        self.started.append((chunk, phase))
        for piece in self.pieces(chunk, phase):
            self.copy(chunk, phase, piece).start()

    def arrive(self, chunk, phase):
        for piece in self.pieces(chunk, phase):
            self.copy(chunk, phase, piece).wait_recv()

    def run(self, steps):
        for chunk, phase in steps:
            if phase > 0 and (chunk, phase - 1) not in self.done:
                self.arrive(chunk, phase - 1)
            self.start(chunk, phase)

    def drain(self):
        for chunk, phase in self.started:
            for piece in self.pieces(chunk, phase):
                self.copy(chunk, phase, piece).wait_send()

    def barrier(self):
        sem = pltpu.get_barrier_semaphore()
        for k in range(1, self.narrow):
            pl.semaphore_signal(
                sem, inc=1, device_id={"narrow": (self.z + k) % self.narrow}, device_id_type=MESH
            )
        for other in (self.first, self.second, self.twin):
            pl.semaphore_signal(sem, inc=1, device_id={"wide": self.base + other}, device_id_type=MESH)
        pl.semaphore_wait(sem, self.narrow - 1 + 3)


def tick(t):
    steps = ((t, 1), (t + 2, 0), (t - 1, 2), (t - 2, 3))
    return tuple((chunk, phase) for chunk, phase in steps if 0 <= chunk < ROW_CHUNKS + 3 * (phase == 0))


LATE = {4: 7, 14: 8, 23: 9}
LAST = ()


def attention_forward(
    sid_ref, grid_ref, tok_ref, gain_ref, shift_ref, pb_ref, own_ref, slices, table_ref, small_ref,
    prob_ref, att_ref, branch_ref, wa_ref, small_out, q_out, k_out, v_out, gath_b, gath_c,
    stage, first_in, queries, k_pad, v_pad, bias, lined, diag, far, smalls, send, recv, extra_send, extra_recv, local,
    narrow,
):
    image = pl.program_id(0)
    images = pl.num_programs(0)
    gather = Gather(narrow, slices, (stage, gath_b, gath_c), send, recv)

    def extra(which, k):
        source = diag if which else small_ref.at[k]
        target = far.at[k - 1] if which else smalls.at[k]
        place = which * (narrow - 1) + k - 1
        return pltpu.make_async_remote_copy(
            src_ref=source, dst_ref=target, send_sem=extra_send.at[place], recv_sem=extra_recv.at[place],
            device_id={"narrow": (gather.z + narrow - k) % narrow}, device_id_type=MESH,
        )

    def keep(which):
        source, target = ((queries, q_out), (k_pad, k_out), (v_pad, v_out))[which]
        return pltpu.make_async_copy(source, target, local.at[which])

    @pl.when(image == 0)
    def _():
        def bias_of(slot, at, table):
            p, s, limit, later, p_patch, s_patch = slot_masks(grid_ref[at, 0], grid_ref[at, 1], False)
            both = p_patch & s_patch
            open_key = s <= limit
            for h in range(3):
                row = h * 16 + sid_ref[at] * 2
                toep = [
                    pltpu.roll(
                        jnp.broadcast_to(table(row + which), (208, DIAG)), DIAG - 207, 1, stride=1, stride_axis=0
                    )[:, :256]
                    for which in range(2)
                ]
                c0, c1, c2 = (smalls[slot, 3:4, h * 3 + c : h * 3 + c + 1] for c in range(3))
                outer = jnp.where((p == 0) & s_patch, c0, jnp.where(p_patch & (s == 0), c1, c2))
                value = jnp.where(both, jnp.where(later, toep[0], toep[1]), outer)
                bias[at, slot * 3 + h] = jnp.where(open_key, value, MASKED).astype(BF16)

        def far_bias(slot):
            @pl.loop(0, 8)
            def _(at):
                bias_of(slot, at, lambda row: far[slot - 1, pl.ds(row, 1), :])

        def weights_of(part):
            gather.arrive(part, 3)
            for slot in range(narrow - 1):
                for pair in range(4):
                    rows = [
                        stage[slot, pl.ds((2 * pair + i) * SLICE_ROWS + part * PART_ROWS, PART_ROWS), :]
                        for i in range(2)
                    ]
                    at = (slot + 1) * 192 + pair * 2 * PART_ROWS
                    wa_ref[part, at : at + 2 * PART_ROWS, :] = jnp.concatenate(rows, axis=0).astype(BF16)

        def project(part, target, finish):
            @pl.loop(0, 8)
            def _(at):
                target[at, 0:208, :] = finish(dot_nt(first_in[at], wa_ref[part])).astype(BF16)

            keep(part).start()

        lined[...] = jnp.zeros_like(lined)
        for shape_at in range(len(GRIDS)):
            for which, row, col, at, size in windows(shape_at):
                lined[shape_at * 2 + which, :, at : at + size] = table_ref[row, :, col : col + size]
        for h in range(3):
            for r in range(16):
                diag[h * 16 + r : h * 16 + r + 1, :] = lined[r, h : h + 1, :]
        gather.barrier()
        smalls[0] = small_ref[0]
        gather.run(((0, 0), (1, 0)))
        for k in range(1, narrow):
            extra(0, k).start()
            extra(1, k).start()
        k_pad[:, 208:256, :] = jnp.zeros((8, 48, 768), BF16)
        v_pad[:, 208:256, :] = jnp.zeros((8, 48, 768), BF16)
        for part in range(4):
            wa_ref[part, 0:192, :] = own_ref[part * 192 : (part + 1) * 192, :]

        @pl.loop(0, 8)
        def _(at):
            normed, _ = norm_stats(tok_ref[at].astype(F32))
            first_in[at] = (normed * gain_ref[...] + shift_ref[...]).astype(BF16)
            bias_of(0, at, lambda row: diag[pl.ds(row, 1), :])

        gather.run(tick(0))
        gather.run(tick(1))
        for k in range(1, narrow):
            extra(0, k).wait_recv()
            extra(1, k).wait_recv()
        far_bias(1)
        gather.run(tick(2))
        for k in range(2, narrow):
            far_bias(k)
        gather.run(tick(3))
        q_bias = sum(smalls[k, 0:1, :] for k in range(narrow))
        v_bias = sum(smalls[k, 1:2, :] for k in range(narrow))
        small_out[...] = smalls[...]
        weights_of(0)
        project(0, queries, lambda v: (v + q_bias) * (HD ** -0.5))
        gather.run(tick(4))
        weights_of(1)
        project(1, k_pad, lambda v: v)
        gather.run(tick(5))
        weights_of(2)
        project(2, v_pad, lambda v: v + v_bias)
        gather.run(tick(6))
        weights_of(3)

    head_of = lax.broadcasted_iota(jnp.int32, (1, 256), 1) // HD

    @pl.loop(0, 3)
    def _(group):
        for when, t in LATE.items():
            @pl.when(image * 3 + group == when)
            def _():
                gather.run(tick(t))

        lanes = pl.ds(pl.multiple_of(group * 256, 256), 256)
        q_group = queries[image, :, lanes]
        k_group = k_pad[image, :, lanes]
        v_group = v_pad[image, :, lanes]
        stacked = jnp.concatenate(
            [jnp.where(head_of == h, q_group, jnp.zeros_like(q_group)) for h in range(4)], axis=0
        )
        raw = dot_nt(stacked, k_group)
        probs = []
        for h in range(4):
            head = group * 4 + h
            scores = raw[h * 208 : (h + 1) * 208, :] + bias[image, head].astype(F32)
            top = jnp.max(scores, axis=-1, keepdims=True)
            raised = jnp.exp(scores - top)
            prob = (raised * (1.0 / jnp.sum(raised, axis=-1, keepdims=True))).astype(BF16)
            prob_ref[0, head] = prob
            probs.append(prob)
        mixed = dot_nn(jnp.concatenate(probs, axis=0), v_group)
        out = mixed[0:208]
        for h in range(1, 4):
            out = jnp.where(head_of == h, mixed[h * 208 : (h + 1) * 208], out)
        att_ref[0, :, lanes] = out.astype(BF16)

    branch_ref[0] = dot_nn(att_ref[0], wa_ref[3]) + pb_ref[...]

    @pl.when(image == images - 1)
    def _():
        for t in LAST:
            gather.run(tick(t))
        for chunk in range(4, ROW_CHUNKS):
            gather.arrive(chunk, 3)
        for chunk in range(ROW_CHUNKS, len(gather.chunks)):
            gather.arrive(chunk, 0)
        gather.drain()
        for k in range(1, narrow):
            extra(0, k).wait_send()
            extra(1, k).wait_send()
        for which in range(3):
            keep(which).wait()


class Reduce:
    STEPS = 7

    def __init__(self, near, beyond, source, half, quarter, eighth, between, total, send, recv, first_sem):
        self.near, self.beyond, self.source, self.total = near, beyond, source, total
        self.half, self.quarter, self.eighth, self.between = half, quarter, eighth, between
        self.send, self.recv, self.first_sem = send, recv, first_sem
        self.rows = eighth.shape[0]

    @staticmethod
    def scratch(rows, width, beyond):
        shapes = [(rows // 2, width), (rows // 4, width), (rows // 8, width), (2 * max(beyond, 1), rows // 8, width)]
        return [pltpu.VMEM(shape, F32) for shape in shapes]

    def span(self, ref, start, count):
        return ref.at[pl.ds(pl.multiple_of(start, 8), count), :]

    def value(self, ref, start, count):
        return ref[pl.ds(pl.multiple_of(start, 8), count), :]

    def copy(self, step):
        near, rows = self.near, self.rows
        half_at = near.core * 4 * rows
        quarter_at = half_at + near.first_bit * 2 * rows
        own_at = quarter_at + near.second_bit * rows
        if step == 0:
            source, target, to = self.span(self.source, (1 - near.core) * 4 * rows, 4 * rows), self.half, near.twin
        elif step == 1:
            source, target, to = (
                self.span(self.half, (1 - near.first_bit) * 2 * rows, 2 * rows), self.quarter, near.first
            )
        elif step == 2:
            source, target, to = self.span(self.quarter, (1 - near.second_bit) * rows, rows), self.eighth, near.second
        else:
            at, count, to = (
                (own_at, rows, near.second), (quarter_at, 2 * rows, near.first), (half_at, 4 * rows, near.twin)
            )[step - 3]
            source = target = self.span(self.total, at, count)
        return self.remote(source, target, step, near.base + to)

    def remote(self, source, target, place, to):
        place += self.first_sem
        return pltpu.make_async_remote_copy(
            src_ref=source, dst_ref=target, send_sem=self.send.at[place], recv_sem=self.recv.at[place],
            device_id={"wide": to}, device_id_type=MESH,
        )

    def run(self, step):
        near, rows = self.near, self.rows
        if step > 0:
            self.copy(step - 1).wait_recv()
        if step == 1:
            self.half[...] += self.value(self.source, near.core * 4 * rows, 4 * rows)
        if step == 2:
            self.quarter[...] += self.value(self.half, near.first_bit * 2 * rows, 2 * rows)
        if step == 3:
            summed = self.eighth[...] + self.value(self.quarter, near.second_bit * rows, rows)
            for i in range(self.beyond):
                self.between[2 * i] = summed
                copy = self.remote(self.between.at[2 * i], self.between.at[2 * i + 1], 6 + i, near.beyond(i))
                copy.start()
                copy.wait()
                summed = self.between[2 * i] + self.between[2 * i + 1]
            own_at = (near.core * 4 + near.first_bit * 2 + near.second_bit) * rows
            self.total[pl.ds(pl.multiple_of(own_at, 8), rows), :] = summed
        if step < 6:
            self.copy(step).start()

    def drain(self):
        for step in range(6):
            self.copy(step).wait_send()


def greet(near, beyond, narrow=1):
    sem = pltpu.get_barrier_semaphore()
    for k in range(1, narrow):
        pl.semaphore_signal(sem, inc=1, device_id={"narrow": (near.z + k) % narrow}, device_id_type=MESH)
    for k in range(1, SLICES):
        other = near.base + (near.me + k) % SLICES
        pl.semaphore_signal(sem, inc=1, device_id={"wide": other}, device_id_type=MESH)
    for i in range(beyond):
        pl.semaphore_signal(sem, inc=1, device_id={"wide": near.beyond(i)}, device_id_type=MESH)
    pl.semaphore_wait(sem, narrow - 1 + SLICES - 1 + beyond)


PAIR = 2
FF_GATHER = {0: ((8, 1),), 1: ((8, 2), (9, 1)), 3: ((8, 3), (9, 2), (10, 1)), 5: ((9, 3), (10, 2)), 8: ((10, 3),)}

FF_SUM = {4: 0, 7: 1, 10: 2, 11: 3, 13: 4, 15: 5}


def feed_forward(
    grid_ref, tok_ref, branch_ref, cot_ref, vec_ref, small_ref, ownb_ref, ownc_ref, slices, gath_b, _,
    out_ref, mg_ref, out_b, grad_c, sums_ref, gath_c,
    total_b, stage, wb, wc, second_ins, branch_lows, mlp_acc, second_acc, grad_b, half, quarter, eighth, between,
    loads, send, recv, gather_send, gather_recv, narrow, beyond,
):
    slot, pair = pl.program_id(0), pl.program_id(1)
    slots, pairs = pl.num_programs(0), pl.num_programs(1)
    rows = PAIR * 208
    gather = Gather(narrow, slices, (None, None, gath_c), gather_send, gather_recv, done=tuple((ROW_CHUNKS + k, 0) for k in range(3)))
    reduction = Reduce(gather, beyond, grad_b, half, quarter, eighth, between, total_b, send, recv, 0)

    def load(which, at):
        return pltpu.make_async_copy((gath_b, gath_c)[which].at[at], stage.at[which], loads.at[which])

    @pl.when((slot == 0) & (pair == 0))
    def _():
        greet(gather, beyond, narrow)
        wb[0] = ownb_ref[...]
        wc[0] = ownc_ref[...]
        grad_b[...] = jnp.zeros_like(grad_b)
        grad_c[...] = jnp.zeros_like(grad_c)
        sums_ref[...] = jnp.zeros_like(sums_ref)

    for when, steps in FF_GATHER.items():
        @pl.when(slot * pairs + pair == when)
        def _():
            gather.run(steps)

    for when, step in FF_SUM.items():
        @pl.when(slot * pairs + pair == when)
        def _():
            reduction.run(step)

    for k in range(1, narrow):
        @pl.when((pair == pairs - 1) & (slot == k - 1))
        def _():
            load(0, k - 1).start()
            if k > 1:
                gather.arrive(ROW_CHUNKS + k - 1, 3)
                load(1, k - 1).start()

    attn_scale, second_gain, second_shift, mlp_scale, down_bias = (vec_ref[i : i + 1, :] for i in range(5))

    def residual():
        branch = branch_ref[...].reshape(rows, 768)
        return branch, tok_ref[...].reshape(rows, 768).astype(F32) + attn_scale * branch

    def masked_cotangent():
        at = lax.broadcasted_iota(jnp.int32, (rows, 1), 0)
        limit = jnp.zeros((rows, 1), jnp.int32)
        for i in range(PAIR):
            image = pair * PAIR + i
            inside = (at >= i * 208) & (at < (i + 1) * 208)
            limit = jnp.where(inside, grid_ref[image, 0] * grid_ref[image, 1] + i * 208, limit)
        return jnp.where(at <= limit, cot_ref[...].reshape(rows, 768).astype(F32), 0.0)

    @pl.when(slot == 0)
    def _():
        _, middle = residual()
        normed, _ = norm_stats(middle)
        second_ins[pair] = (normed * second_gain + second_shift).astype(BF16)
        branch_lows[pair] = (masked_cotangent() * mlp_scale).astype(BF16)
        mlp_acc[pair] = jnp.zeros((rows, 768), F32)
        second_acc[pair] = jnp.zeros((rows, 768), F32)

    second_in, branch_low = second_ins[pair], branch_lows[pair]
    up, down = wb[slot % 2], wc[slot % 2]
    up_pre = dot_nn(second_in, up) + small_ref[slot, 2:3, :]
    cdf = 0.5 * (1.0 + lax.erf(up_pre * INV_ROOT_TWO))
    hidden = (up_pre * cdf).astype(BF16)
    slope = cdf + up_pre * jnp.exp(-0.5 * up_pre * up_pre) * INV_ROOT_TWO_PI
    mlp_acc[pair] += dot_nn(hidden, down)
    pre_low = (dot_nt(branch_low, down) * slope).astype(BF16)
    second_acc[pair] += dot_nt(pre_low, up)

    @pl.when(slot == 0)
    def _():
        grad_c[...] += dot_tn(hidden, branch_low)
        grad_b[...] += dot_tn(second_in, pre_low)
        sums_ref[6] += fold_rows(pre_low.astype(F32))

    @pl.when((pair == pairs - 1) & (slot == 0))
    def _():
        gather.arrive(ROW_CHUNKS, 3)
        load(1, 0).start()

    @pl.when((pair == pairs - 1) & (slot < slots - 1))
    def _():
        for which, weights in enumerate((wb, wc)):
            load(which, slot).wait()
            weights[(slot + 1) % 2] = stage[which].astype(BF16)

    @pl.when(slot == slots - 1)
    def _():
        branch, middle = residual()
        normed, inv = norm_stats(middle)
        out_grad = masked_cotangent()
        mlp_branch = mlp_acc[pair] + down_bias
        out_ref[...] = (middle + mlp_scale * mlp_branch).astype(BF16).reshape(PAIR, 208, 768)
        second_grad = second_acc[pair]
        middle_grad = out_grad + norm_back(second_grad, normed, inv, second_gain)
        mg_ref[...] = middle_grad.reshape(PAIR, 208, 768)
        sums_ref[0] += fold_rows(out_grad * mlp_branch)
        sums_ref[1] += fold_rows(out_grad)
        sums_ref[2] += fold_rows(second_grad * normed)
        sums_ref[3] += fold_rows(second_grad)
        sums_ref[4] += fold_rows(middle_grad * branch)
        sums_ref[5] += fold_rows(middle_grad)

    @pl.when((slot == slots - 1) & (pair == pairs - 1))
    def _():
        reduction.run(6)
        copy = pltpu.make_async_copy(total_b, out_b, loads.at[0])
        copy.start()
        copy.wait()
        reduction.drain()
        gather.drain()


SMALL_ROWS = 128
AB_TICKS = {0: ((0, 0),), 2: ((0, 1),), 5: ((0, 2),), 7: ((0, 3),), 8: ((1, 0),), 9: ((1, 1),), 12: ((1, 2),), 14: ((1, 3),), 15: ((0, 4),)}

AB_LAST = ((1, 4), (0, 5), (1, 5), (0, 6), (1, 6))


def attention_backward(
    sid_ref, grid_ref, tok_ref, mg_ref, att_ref, q0_ref, k0_ref, v0_ref, p0_ref, q_ref, k_ref, v_ref, p1_ref, p2_ref,
    vec_ref, wa_ref, ff_sums_ref, grad_c,
    tg_ref, total_out, out_c, late_total,
    total, total_c, grads, attn_lows, kept, dq, dk, dv, lines, edges, sums, late, late_in, late_between,
    *rest, beyond,
):
    step = pl.program_id(0)
    half = pl.num_programs(0) // 2
    rows = PAIR * 208
    near = Neighbours()
    send, recv, late_send, late_recv, local = rest[8:]
    chains = (
        Reduce(near, beyond, grad_c, *rest[0:4], total_c, send, recv, 0),
        Reduce(near, beyond, grads, *rest[4:8], total, send, recv, 6 + beyond),
    )
    attn_scale, first_gain, first_shift = (vec_ref[i : i + 1, :] for i in range(3))
    head_of = lax.broadcasted_iota(jnp.int32, (1, 256), 1) // HD

    def advance(i):
        for when, steps in AB_TICKS.items():
            if when % PAIR == i:
                @pl.when(step == when // PAIR)
                def _():
                    for chain, at in steps:
                        chains[chain].run(at)

    def stack(group):
        return jnp.concatenate([jnp.where(head_of == h, group, jnp.zeros_like(group)) for h in range(4)], axis=0)

    def merge(mixed):
        out = mixed[0:208]
        for h in range(1, 4):
            out = jnp.where(head_of == h, mixed[h * 208 : (h + 1) * 208], out)
        return out

    def heads_back(q_group, k_group, v_group, g_group, prob_at, each):
        q_stack, g_stack = stack(q_group), stack(g_group)
        prob_grads = dot_nt(g_stack, v_group)
        lows = []
        for h in range(4):
            prob = prob_at(h).astype(F32)
            prob_grad = prob_grads[h * 208 : (h + 1) * 208]
            score_grad = prob * (prob_grad - jnp.sum(prob * prob_grad, axis=-1, keepdims=True))
            low = score_grad.astype(BF16)
            lows.append(low)
            each(h, score_grad, low)
        low_stack = jnp.concatenate(lows, axis=0)
        prob_stack = jnp.concatenate([prob_at(h) for h in range(4)], axis=0)
        return (
            merge(dot_nn(low_stack, k_group)).astype(BF16) * jnp.asarray(HD ** -0.5, BF16),
            dot_tn(low_stack, q_stack)[0:208].astype(BF16),
            dot_tn(prob_stack, g_stack)[0:208].astype(BF16),
        )

    @pl.when(step == 0)
    def _():
        greet(near, beyond)
        grads[...] = jnp.zeros_like(grads)
        sums[...] = jnp.zeros_like(sums)
        lines[...] = jnp.zeros_like(lines)
        edges[...] = jnp.zeros_like(edges)
        late[...] = jnp.zeros_like(late)

    normed, inv = norm_stats(tok_ref[...].reshape(rows, 768).astype(F32))
    middle_grad = mg_ref[...].reshape(rows, 768)

    @pl.when(step < half)
    def _():
        attn_low = (middle_grad * attn_scale).astype(BF16)
        attn_lows[step] = attn_low
        attended_grad = dot_nt(attn_low, wa_ref[3, 0:256, :]).astype(BF16)
        grads[576:768, :] += dot_tn(att_ref[...].reshape(rows, 256), attn_low)[0:192, :]
        flip = (
            lax.broadcasted_iota(jnp.int32, (208, 208), 0) + lax.broadcasted_iota(jnp.int32, (208, 208), 1) == 207
        ).astype(BF16)

        for i in range(PAIR):
            advance(i)
            image = step * PAIR + i
            p, s, limit, later, p_patch, s_patch = slot_masks(grid_ref[image, 0], grid_ref[image, 1], True)
            both = p_patch & s_patch
            kind = sid_ref[image]

            def table_grad(h, score_grad, low):
                if h == 3:
                    return
                low_rest = (score_grad - low.astype(F32)).astype(BF16)
                turned = dot_nn(flip, low) + dot_nn(flip, low_rest)
                patches = jnp.where(both, turned, 0.0)
                edge = turned - patches
                for which, part in enumerate((jnp.where(later, patches, 0.0), jnp.where(later, 0.0, patches))):
                    wide = jnp.concatenate([part, jnp.zeros((208, 256), F32)], axis=1)
                    folded = jnp.sum(pltpu.roll(wide, 0, 1, stride=1, stride_axis=0), axis=0, keepdims=True)
                    row = which * 3 + h
                    for shape_at in range(len(GRIDS)):
                        lines[shape_at, row : row + 1, :] += jnp.where(kind == shape_at, folded, 0.0)
                class_query = jnp.where((p == 0) & s_patch, edge, 0.0)
                class_key = jnp.where(p_patch & (s == 0), edge, 0.0)
                for at, part in enumerate((class_query, class_key, edge - class_query - class_key)):
                    edges[at * 3 + h] += fold_rows(part)

            here = slice(i * 208, (i + 1) * 208)
            own = heads_back(
                q0_ref[i], k0_ref[i], v0_ref[i], attended_grad[here], lambda h: p0_ref[i, h], table_grad
            )
            for c, grad in enumerate(own):
                kept[c, step, here, :] = grad
            sums[0] += fold_rows(own[0].astype(F32))
            sums[1] += fold_rows(own[2].astype(F32))

        first_in = (normed * first_gain + first_shift).astype(BF16)
        for c in range(3):
            grads[c * 192 : (c + 1) * 192, :] += dot_tn(kept[c, step], first_in)[0:192, :]

    @pl.when(step == half)
    def _():
        grads[768 : 768 + SMALL_ROWS, :] = jnp.zeros((SMALL_ROWS, 768), F32)
        for shape_at in range(len(GRIDS)):
            grads[768 + shape_at * 8 : 776 + shape_at * 8, 0:DIAG] = lines[shape_at]
        for at in range(9):
            grads[832 + at : 833 + at, 0:256] = jnp.sum(edges[at], axis=0, keepdims=True)
        for at in range(2):
            grads[848 + at : 849 + at, 0:256] = jnp.sum(sums[at], axis=0, keepdims=True)
        for at in range(7):
            grads[856 + at : 857 + at, :] = jnp.sum(ff_sums_ref[at], axis=0, keepdims=True)

    @pl.when(step >= half)
    def _():
        at = step - half
        attended_grad = dot_nt(attn_lows[at], wa_ref[3, 256:768, :]).astype(BF16)
        for c, ref in enumerate((dq, dk, dv)):
            ref[:, 0:256] = kept[c, at]
        for i in range(PAIR):
            advance(i)
            here = slice(i * 208, (i + 1) * 208)
            for group in (1, 2):
                lanes = slice(group * 256, group * 256 + 256)
                probs = (p1_ref, p2_ref)[group - 1]
                parts = heads_back(
                    q_ref[i, :, lanes], k_ref[i, :, lanes], v_ref[i, :, lanes],
                    attended_grad[here, (group - 1) * 256 : group * 256], lambda h: probs[i, h], lambda *_: None,
                )
                for ref, part in zip((dq, dk, dv), parts):
                    ref[here, lanes] = part
        first_grad = dot_nn(dq[...], wa_ref[0]) + dot_nn(dk[...], wa_ref[1]) + dot_nn(dv[...], wa_ref[2])
        tg_ref[...] = (middle_grad + norm_back(first_grad, normed, inv, first_gain)).reshape(PAIR, 208, 768)
        late[0:8, :] += fold_rows(first_grad * normed)
        late[8:16, :] += fold_rows(first_grad)

    @pl.when(step == 2 * half - 1)
    def _():
        copies = [
            pltpu.make_async_remote_copy(
                src_ref=late, dst_ref=late_in.at[k - 1], send_sem=late_send.at[k - 1], recv_sem=late_recv.at[k - 1],
                device_id={"wide": near.base + (near.me + k) % SLICES}, device_id_type=MESH,
            )
            for k in range(1, SLICES)
        ]
        for copy in copies:
            copy.start()
        outs = [
            pltpu.make_async_copy(source, target, local.at[i])
            for i, (source, target) in enumerate(((total_c, out_c), (total, total_out)))
        ]
        for chain, at in AB_LAST:
            chains[chain].run(at)
        for copy in outs:
            copy.start()
        for copy in copies:
            copy.wait()
        summed = late[...]
        for k in range(SLICES - 1):
            summed = summed + late_in[k]
        for i in range(beyond):
            late_between[2 * i] = summed
            copy = pltpu.make_async_remote_copy(
                src_ref=late_between.at[2 * i], dst_ref=late_between.at[2 * i + 1],
                send_sem=late_send.at[SLICES - 1 + i], recv_sem=late_recv.at[SLICES - 1 + i],
                device_id={"wide": near.beyond(i)}, device_id_type=MESH,
            )
            copy.start()
            copy.wait()
            summed = late_between[2 * i] + late_between[2 * i + 1]
        late_total[...] = summed
        for copy in outs:
            copy.wait()
        for chain in chains:
            chain.drain()


def make_body(wide_size, narrow_size):
    def body(
        tokens, grid_shape, first_gain, first_shift, qkv_weight, query_bias, value_bias, rel_table, proj_weight,
        proj_bias, attn_scale, second_gain, second_shift, up_weight, up_bias, down_weight, down_bias, mlp_scale,
        cotangent,
    ):
        images, slots, width = tokens.shape
        heads, table_size = rel_table.shape
        local = heads * HD
        own_a = jnp.concatenate(
            [jnp.transpose(qkv_weight, (0, 2, 1)).reshape(3 * local, width), proj_weight], axis=0
        )
        table = rel_table.astype(F32)
        square = table[:, : SPAN * SPAN].reshape(heads, SPAN, SPAN)[:, ::-1, ::-1]
        square = jnp.pad(jnp.transpose(square, (1, 0, 2)), ((0, 0), (0, 8 - heads), (0, 128 - SPAN)))

        def small_for(k):
            def at(v, start):
                return jnp.pad(v.astype(F32).reshape(1, -1), ((0, 0), (start, width - start - v.size)))

            return jnp.concatenate(
                [
                    at(query_bias, k * local), at(value_bias, k * local), at(up_bias, 0),
                    at(table[:, SPAN * SPAN :].reshape(-1), 0), jnp.zeros((4, width), F32),
                ]
            )

        small = jnp.stack([small_for(k) for k in range(narrow_size)])
        all_heads = narrow_size * heads

        kinds = jnp.array(GRIDS, jnp.int32)
        sid = jnp.argmax(jnp.all(grid_shape[:, None, :] == kinds[None], axis=-1), axis=-1).astype(jnp.int32)

        def row(v):
            return v.astype(F32).reshape(1, -1)

        smem = pl.BlockSpec(memory_space=pltpu.SMEM)
        anyspace = pl.BlockSpec(memory_space=pl.ANY)
        vmem = pl.BlockSpec(memory_space=pltpu.VMEM)

        def whole(*shape):
            return pl.BlockSpec(shape, lambda i, *_: (0,) * len(shape))

        def per_image(*shape):
            return pl.BlockSpec((1,) + shape, lambda i, *_: (i,) + (0,) * len(shape))

        def struct(*shape, dtype=F32):
            return jax.ShapeDtypeStruct(shape, dtype)

        params = pltpu.CompilerParams(vmem_limit_bytes=VMEM_LIMIT, dimension_semantics=("arbitrary",))
        copies = len(chunks_of(narrow_size)) * (narrow_size - 1 + 7)
        copies = len(chunks_of(narrow_size)) * (narrow_size - 1 + 7)
        me = lax.axis_index("wide") % SLICES
        slices = jnp.stack(
            [lax.dynamic_slice_in_dim(own_a.reshape(4, local, width), me * PART_ROWS, PART_ROWS, 1).reshape(-1, width)]
            + [lax.dynamic_slice_in_dim(w, me * SLICE_ROWS, SLICE_ROWS, 0) for w in (up_weight, down_weight)]
        ).astype(F32)
        probs, attended, branch, weights_a, small, queries, keys, values, gath_b, gath_c = pl.pallas_call(
            functools.partial(attention_forward, narrow=narrow_size),
            grid=(images,),
            in_specs=[smem, smem, vmem] + [whole(1, width)] * 3 + [vmem] * 4,
            out_specs=[per_image(all_heads, slots, 256), per_image(slots, width), per_image(slots, width)]
            + [vmem, vmem] + [anyspace] * 5,
            scratch_shapes=[
                pltpu.VMEM((narrow_size - 1, width, width), F32),
                pltpu.VMEM((images, slots, width), BF16),
                pltpu.VMEM((images, slots, width), BF16),
                pltpu.VMEM((images, 256, width), BF16),
                pltpu.VMEM((images, 256, width), BF16),
                pltpu.VMEM((images, all_heads, slots, 256), BF16),
                pltpu.VMEM((16, 8, DIAG), F32),
                pltpu.VMEM((48, DIAG), F32),
                pltpu.VMEM((narrow_size - 1, 48, DIAG), F32),
                pltpu.VMEM((narrow_size, 8, width), F32),
                pltpu.SemaphoreType.DMA((copies,)),
                pltpu.SemaphoreType.DMA((copies,)),
                pltpu.SemaphoreType.DMA((2 * narrow_size - 2,)),
                pltpu.SemaphoreType.DMA((2 * narrow_size - 2,)),
                pltpu.SemaphoreType.DMA((3,)),
            ],
            out_shape=[
                struct(images, all_heads, slots, 256, dtype=BF16),
                struct(images, slots, width, dtype=BF16),
                struct(images, slots, width),
                struct(4, width, width, dtype=BF16),
                struct(narrow_size, 8, width),
                struct(images, slots, width, dtype=BF16),
                struct(images, 256, width, dtype=BF16),
                struct(images, 256, width, dtype=BF16),
                struct(narrow_size - 1, width, width),
                struct(narrow_size - 1, width, width),
            ],
            compiler_params=pltpu.CompilerParams(
                vmem_limit_bytes=VMEM_LIMIT, dimension_semantics=("arbitrary",), collective_id=0,
                has_side_effects=True,
            ),
            name="attention_forward",
        )(
            sid, grid_shape, tokens, row(first_gain), row(first_shift), row(proj_bias), own_a, slices, square, small,
        )

        vec = jnp.concatenate([row(v) for v in (attn_scale, second_gain, second_shift, mlp_scale, down_bias)])
        beyond = (wide_size // SLICES).bit_length() - 1
        rows = PAIR * slots
        pairs = images // PAIR
        last = narrow_size - 1

        def remote_params(at):
            return pltpu.CompilerParams(
                vmem_limit_bytes=VMEM_LIMIT, collective_id=at, has_side_effects=True,
            )

        ends = pl.BlockSpec((PAIR, slots, width), lambda s, i: (jnp.where((s > 0) & (s < last), pairs - 1, i), 0, 0))
        outs = pl.BlockSpec((PAIR, slots, width), lambda s, i: (jnp.where(s < last, 0, i), 0, 0))
        layer_out, middle_grad, grad_b, grad_c, sums, _ = pl.pallas_call(
            functools.partial(feed_forward, narrow=narrow_size, beyond=beyond),
            grid=(narrow_size, pairs),
            in_specs=[smem] + [ends] * 3 + [vmem] * 5 + [anyspace] * 2,
            out_specs=[outs] * 2 + [anyspace, vmem, vmem, anyspace],
            input_output_aliases={10: 5},
            scratch_shapes=[
                pltpu.VMEM((width, width), F32),
                pltpu.VMEM((2, width, width), F32),
                pltpu.VMEM((2, width, width), BF16),
                pltpu.VMEM((2, width, width), BF16),
                pltpu.VMEM((pairs, rows, width), BF16),
                pltpu.VMEM((pairs, rows, width), BF16),
                pltpu.VMEM((pairs, rows, width), F32),
                pltpu.VMEM((pairs, rows, width), F32),
                pltpu.VMEM((width, width), F32),
            ]
            + Reduce.scratch(width, width, beyond)
            + [
                pltpu.SemaphoreType.DMA((2,)),
                pltpu.SemaphoreType.DMA((6 + beyond,)),
                pltpu.SemaphoreType.DMA((6 + beyond,)),
                pltpu.SemaphoreType.DMA((copies,)),
                pltpu.SemaphoreType.DMA((copies,)),
            ],
            out_shape=[
                struct(images, slots, width, dtype=BF16),
                struct(images, slots, width),
                struct(width, width),
                struct(width, width),
                struct(7, 8, width),
                struct(narrow_size - 1, width, width),
            ],
            compiler_params=remote_params(1),
            name="feed_forward",
        )(grid_shape, tokens, branch, cotangent, vec, small, up_weight, down_weight, slices, gath_b, gath_c)

        def first_pass(*shape):
            return pl.BlockSpec((PAIR,) + shape, lambda i: (jnp.minimum(i, pairs - 1),) + (0,) * len(shape))

        def second_pass(*shape, at=0):
            return pl.BlockSpec((PAIR,) + shape, lambda i: (jnp.maximum(i - pairs, 0), at) + (0,) * (len(shape) - 1))

        both_passes = pl.BlockSpec((PAIR, slots, width), lambda i: (i % pairs, 0, 0))
        total_rows = width + SMALL_ROWS
        vec = jnp.concatenate([row(v) for v in (attn_scale, first_gain, first_shift)])
        tokens_grad, total, grad_c, late = pl.pallas_call(
            functools.partial(attention_backward, beyond=beyond),
            grid=(2 * pairs,),
            in_specs=[smem, smem, both_passes, both_passes]
            + [first_pass(slots, 256)] * 2
            + [first_pass(256, 256)] * 2
            + [first_pass(4, slots, 256)]
            + [second_pass(slots, width), second_pass(256, width), second_pass(256, width)]
            + [second_pass(4, slots, 256, at=1), second_pass(4, slots, 256, at=2)]
            + [vmem] * 4,
            out_specs=[second_pass(slots, width), anyspace, anyspace, vmem],
            scratch_shapes=[
                pltpu.VMEM((total_rows, width), F32),
                pltpu.VMEM((width, width), F32),
                pltpu.VMEM((total_rows, width), F32),
                pltpu.VMEM((pairs, rows, width), BF16),
                pltpu.VMEM((3, pairs, rows, 256), BF16),
                pltpu.VMEM((rows, width), BF16),
                pltpu.VMEM((rows, width), BF16),
                pltpu.VMEM((rows, width), BF16),
                pltpu.VMEM((len(GRIDS), 8, DIAG), F32),
                pltpu.VMEM((9, 8, 256), F32),
                pltpu.VMEM((2, 8, 256), F32),
                pltpu.VMEM((16, width), F32),
                pltpu.VMEM((SLICES - 1, 16, width), F32),
                pltpu.VMEM((2 * max(beyond, 1), 16, width), F32),
            ]
            + Reduce.scratch(width, width, beyond)
            + Reduce.scratch(total_rows, width, beyond)
            + [
                pltpu.SemaphoreType.DMA((2 * (6 + beyond),)),
                pltpu.SemaphoreType.DMA((2 * (6 + beyond),)),
                pltpu.SemaphoreType.DMA((SLICES - 1 + beyond,)),
                pltpu.SemaphoreType.DMA((SLICES - 1 + beyond,)),
                pltpu.SemaphoreType.DMA((2,)),
            ],
            out_shape=[
                struct(images, slots, width), struct(total_rows, width), struct(width, width), struct(16, width),
            ],
            compiler_params=remote_params(2),
            name="attention_backward",
        )(
            sid, grid_shape, tokens, middle_grad, attended, queries, keys, values, probs, queries, keys, values, probs,
            probs, vec, weights_a, sums, grad_c,
        )

        grad_a = total[:width]
        lines = total[width : width + 64, :DIAG].reshape(len(GRIDS), 8, DIAG)[:, : 2 * heads]
        lines = jnp.pad(lines.reshape(len(GRIDS), 2, heads, DIAG), ((0, 0), (0, 0), (0, 8 - heads), (0, 0)))
        square_grad = pl.pallas_call(
            undiag_kernel, out_shape=struct(SPAN, 8, 128), name="undiag"
        )(lines)
        square_grad = jnp.transpose(square_grad[:, :heads, :SPAN], (1, 0, 2))[:, ::-1, ::-1]
        edges = jnp.sum(total[width + 64 : width + 73, :256], axis=1).reshape(3, heads).T
        table_grad = jnp.concatenate([square_grad.reshape(heads, SPAN * SPAN), edges], axis=1)
        more = total[width + 80 : width + 82, :local]
        sums = total[width + 88 : width + 95]
        late = jnp.sum(late.reshape(2, 8, width), axis=1)
        qkv_grad = jnp.transpose(grad_a[: 3 * local].reshape(3, local, width), (0, 2, 1))
        return (
            layer_out,
            tokens_grad,
            late[0],
            late[1],
            qkv_grad,
            more[0],
            more[1],
            table_grad,
            grad_a[3 * local :],
            sums[5] * attn_scale.astype(F32),
            sums[4],
            sums[2],
            sums[3],
            grad_b,
            sums[6],
            grad_c,
            sums[1] * mlp_scale.astype(F32),
            sums[0],
        )

    return body


def solution(mesh):
    rows = P("wide", None, None)
    return jax.shard_map(
        make_body(mesh.shape["wide"], mesh.shape["narrow"]),
        mesh=mesh,
        in_specs=(
            rows, P("wide", None), P(), P(), P(None, None, "narrow"), P("narrow"), P("narrow"), P("narrow", None),
            P("narrow", None), P(), P(), P(), P(), P(None, "narrow"), P("narrow"), P("narrow", None), P(), P(), rows,
        ),
        out_specs=(
            rows, rows, P(), P(), P(None, None, "narrow"), P("narrow"), P("narrow"), P("narrow", None),
            P("narrow", None), P(), P(), P(), P(), P(None, "narrow"), P("narrow"), P("narrow", None), P(), P(),
        ),
        check_vma=False,
    )
```

```python
import functools

import jax
import jax.numpy as jnp
from jax import lax
from jax.experimental import pallas as pl
from jax.experimental.pallas import tpu as pltpu
from jax.sharding import PartitionSpec as P

HD = 64
MAXG = 24
SPAN = 2 * MAXG - 1
EPSILON = 1e-06
MASKED = -1e30
INV_ROOT_TWO = 0.7071067811865476
INV_ROOT_TWO_PI = 0.3989422804014327
GRIDS = ((14, 14), (10, 20), (20, 10), (8, 24), (24, 8), (12, 16), (16, 12), (13, 15))
DIAG = 512
F32 = jnp.float32
BF16 = jnp.bfloat16
VMEM_LIMIT = 60 * 1024 * 1024


def dot_nn(a, b):
    return lax.dot_general(a, b, (((1,), (0,)), ((), ())), preferred_element_type=F32)


def dot_nt(a, b):
    return lax.dot_general(a, b, (((1,), (1,)), ((), ())), preferred_element_type=F32)


def dot_tn(a, b):
    return lax.dot_general(a, b, (((0,), (0,)), ((), ())), preferred_element_type=F32)


def row_mean(v):
    return jnp.sum(v, axis=-1, keepdims=True) * (1.0 / v.shape[-1])


def norm_stats(v):
    centred = v - row_mean(v)
    inv = lax.rsqrt(row_mean(centred * centred) + EPSILON)
    return centred * inv, inv


def norm_back(incoming, normed, inv, gain):
    scaled = incoming * gain
    return inv * (scaled - row_mean(scaled) - normed * row_mean(scaled * normed))


def fold_rows(v):
    rows = v.shape[0]
    return jnp.sum(v.reshape(rows // 8, 8, v.shape[1]), axis=0)


def windows(shape_at):
    high, wide = GRIDS[shape_at]
    centre = MAXG - 1
    for m in range(-high, high):
        at = 207 + m * wide
        if m > -high:
            yield 0, centre + m, centre, at, wide
        if m < high - 1:
            yield 1, centre + 1 + m, centre + 1 - wide, at + 1, wide - 1


def slot_masks(high, wide, reverse):
    rows = lax.broadcasted_iota(jnp.int32, (208, 1), 0)
    p = 207 - rows if reverse else rows
    s = lax.broadcasted_iota(jnp.int32, (1, 256), 1)
    limit = high * wide
    wide_f = wide.astype(F32)

    def column(slot):
        patch = (slot - 1).astype(F32)
        return patch - wide_f * jnp.floor((patch + 0.5) / wide_f)

    later = column(s) >= column(p)
    p_patch = (p >= 1) & (p <= limit)
    s_patch = (s >= 1) & (s <= limit)
    return p, s, limit, later, p_patch, s_patch


MESH = pl.DeviceIdType.MESH
SLICES = 8
SLICE_ROWS = 96
PART_ROWS = 24


def chunks_of(narrow):
    all_shards = tuple(range(1, narrow))
    rows = [(group, at, 24, all_shards) for group in range(2) for at in (0, 24, 48, 72)]
    return tuple(rows) + tuple((2, 0, SLICE_ROWS, (k,)) for k in all_shards)


ROW_CHUNKS = 8


class Neighbours:
    def __init__(self):
        self.wide = lax.axis_index("wide")
        self.me = self.wide % SLICES
        self.base = self.wide - self.me
        self.core = core = self.me % 2
        x_bit, y_bit = (self.me // 2) % 2, self.me // 4
        over_x, over_y = self.me + 2 - 4 * x_bit, self.me + 4 - 8 * y_bit
        self.first = over_x * (1 - core) + over_y * core
        self.second = over_y * (1 - core) + over_x * core
        self.first_bit = x_bit * (1 - core) + y_bit * core
        self.second_bit = y_bit * (1 - core) + x_bit * core
        self.third = over_x + over_y - self.me
        self.twin = self.me + 1 - 2 * core

    def beyond(self, step):
        size = SLICES << step
        return self.wide + size - 2 * size * ((self.wide // size) % 2)


class Gather(Neighbours):
    def __init__(self, narrow, slices, buffers, send, recv, done=()):
        super().__init__()
        self.done = done
        self.narrow, self.slices, self.buffers, self.send, self.recv = narrow, slices, buffers, send, recv
        self.z = lax.axis_index("narrow")
        self.chunks = chunks_of(narrow)
        self.per_chunk = narrow - 1 + 7
        self.started = []

    def copy(self, chunk, phase, piece):
        group, at, rows, shards = self.chunks[chunk]
        buffer = self.buffers[group]

        def part(owner):
            return buffer.at[
                pl.ds(shards[0] - 1, len(shards)), pl.ds(pl.multiple_of(owner * SLICE_ROWS + at, 8), rows), :
            ]

        place = chunk * self.per_chunk
        if phase == 0:
            place += piece - 1
            source = self.slices.at[group, pl.ds(at, rows), :]
            target = buffer.at[piece - 1, pl.ds(pl.multiple_of(self.me * SLICE_ROWS + at, 8), rows), :]
            device = {"narrow": (self.z + self.narrow - piece) % self.narrow}
        else:
            owners = (self.me, self.first, self.second, self.third)
            place += self.narrow - 1 + (0, 1, 3)[phase - 1] + piece
            source = target = part(owners[piece])
            device = {"wide": self.base + (self.first, self.second, self.twin)[phase - 1]}
        return pltpu.make_async_remote_copy(
            src_ref=source, dst_ref=target, send_sem=self.send.at[place], recv_sem=self.recv.at[place],
            device_id=device, device_id_type=MESH,
        )

    def pieces(self, chunk, phase):
        return (self.chunks[chunk][3], range(1), range(2), range(4))[phase]

    def start(self, chunk, phase):
        self.started.append((chunk, phase))
        for piece in self.pieces(chunk, phase):
            self.copy(chunk, phase, piece).start()

    def arrive(self, chunk, phase):
        for piece in self.pieces(chunk, phase):
            self.copy(chunk, phase, piece).wait_recv()

    def run(self, steps):
        for chunk, phase in steps:
            if phase > 0 and (chunk, phase - 1) not in self.done:
                self.arrive(chunk, phase - 1)
            self.start(chunk, phase)

    def drain(self):
        for chunk, phase in self.started:
            for piece in self.pieces(chunk, phase):
                self.copy(chunk, phase, piece).wait_send()

    def barrier(self):
        sem = pltpu.get_barrier_semaphore()
        for k in range(1, self.narrow):
            pl.semaphore_signal(
                sem, inc=1, device_id={"narrow": (self.z + k) % self.narrow}, device_id_type=MESH
            )
        for other in (self.first, self.second, self.twin):
            pl.semaphore_signal(sem, inc=1, device_id={"wide": self.base + other}, device_id_type=MESH)
        pl.semaphore_wait(sem, self.narrow - 1 + 3)


def tick(t):
    steps = ((t, 1), (t + 2, 0), (t - 1, 2), (t - 2, 3))
    return tuple((chunk, phase) for chunk, phase in steps if 0 <= chunk < ROW_CHUNKS + 3 * (phase == 0))


LATE = {6: 7, 17: 8}
LAST = (9,)


def attention_forward(
    sid_ref, grid_ref, tok_ref, gain_ref, shift_ref, pb_ref, own_ref, slices, table_ref, small_ref,
    prob_ref, att_ref, branch_ref, wa_ref, small_out, q_out, k_out, v_out, gath_b, gath_c,
    stage, first_in, queries, k_pad, v_pad, bias, lined, diag, far, smalls, send, recv, extra_send, extra_recv, local,
    narrow,
):
    image = pl.program_id(0)
    images = pl.num_programs(0)
    gather = Gather(narrow, slices, (stage, gath_b, gath_c), send, recv)

    def extra(which, k):
        source = diag if which else small_ref.at[k]
        target = far.at[k - 1] if which else smalls.at[k]
        place = which * (narrow - 1) + k - 1
        return pltpu.make_async_remote_copy(
            src_ref=source, dst_ref=target, send_sem=extra_send.at[place], recv_sem=extra_recv.at[place],
            device_id={"narrow": (gather.z + narrow - k) % narrow}, device_id_type=MESH,
        )

    def keep(which):
        source, target = ((queries, q_out), (k_pad, k_out), (v_pad, v_out))[which]
        return pltpu.make_async_copy(source, target, local.at[which])

    @pl.when(image == 0)
    def _():
        def bias_of(slot, at, table):
            p, s, limit, later, p_patch, s_patch = slot_masks(grid_ref[at, 0], grid_ref[at, 1], False)
            both = p_patch & s_patch
            open_key = s <= limit
            for h in range(3):
                row = h * 16 + sid_ref[at] * 2
                toep = [
                    pltpu.roll(
                        jnp.broadcast_to(table(row + which), (208, DIAG)), DIAG - 207, 1, stride=1, stride_axis=0
                    )[:, :256]
                    for which in range(2)
                ]
                c0, c1, c2 = (smalls[slot, 3:4, h * 3 + c : h * 3 + c + 1] for c in range(3))
                outer = jnp.where((p == 0) & s_patch, c0, jnp.where(p_patch & (s == 0), c1, c2))
                value = jnp.where(both, jnp.where(later, toep[0], toep[1]), outer)
                bias[at, slot * 3 + h] = jnp.where(open_key, value, MASKED).astype(BF16)

        def far_bias(slot):
            @pl.loop(0, 8)
            def _(at):
                bias_of(slot, at, lambda row: far[slot - 1, pl.ds(row, 1), :])

        def weights_of(part):
            gather.arrive(part, 3)
            for slot in range(narrow - 1):
                for pair in range(4):
                    rows = [
                        stage[slot, pl.ds((2 * pair + i) * SLICE_ROWS + part * PART_ROWS, PART_ROWS), :]
                        for i in range(2)
                    ]
                    at = (slot + 1) * 192 + pair * 2 * PART_ROWS
                    wa_ref[part, at : at + 2 * PART_ROWS, :] = jnp.concatenate(rows, axis=0).astype(BF16)

        def project(part, target, finish):
            @pl.loop(0, 8)
            def _(at):
                target[at, 0:208, :] = finish(dot_nt(first_in[at], wa_ref[part])).astype(BF16)

            keep(part).start()

        lined[...] = jnp.zeros_like(lined)
        for shape_at in range(len(GRIDS)):
            for which, row, col, at, size in windows(shape_at):
                lined[shape_at * 2 + which, :, at : at + size] = table_ref[row, :, col : col + size]
        for h in range(3):
            for r in range(16):
                diag[h * 16 + r : h * 16 + r + 1, :] = lined[r, h : h + 1, :]
        gather.barrier()
        smalls[0] = small_ref[0]
        gather.run(((0, 0), (1, 0)))
        for k in range(1, narrow):
            extra(0, k).start()
            extra(1, k).start()
        k_pad[:, 208:256, :] = jnp.zeros((8, 48, 768), BF16)
        v_pad[:, 208:256, :] = jnp.zeros((8, 48, 768), BF16)
        for part in range(4):
            wa_ref[part, 0:192, :] = own_ref[part * 192 : (part + 1) * 192, :]

        @pl.loop(0, 8)
        def _(at):
            normed, _ = norm_stats(tok_ref[at].astype(F32))
            first_in[at] = (normed * gain_ref[...] + shift_ref[...]).astype(BF16)
            bias_of(0, at, lambda row: diag[pl.ds(row, 1), :])

        gather.run(tick(0))
        gather.run(tick(1))
        for k in range(1, narrow):
            extra(0, k).wait_recv()
            extra(1, k).wait_recv()
        far_bias(1)
        gather.run(tick(2))
        for k in range(2, narrow):
            far_bias(k)
        gather.run(tick(3))
        q_bias = sum(smalls[k, 0:1, :] for k in range(narrow))
        v_bias = sum(smalls[k, 1:2, :] for k in range(narrow))
        small_out[...] = smalls[...]
        weights_of(0)
        project(0, queries, lambda v: (v + q_bias) * (HD ** -0.5))
        gather.run(tick(4))
        weights_of(1)
        project(1, k_pad, lambda v: v)
        gather.run(tick(5))
        weights_of(2)
        project(2, v_pad, lambda v: v + v_bias)
        gather.run(tick(6))
        weights_of(3)

    head_of = lax.broadcasted_iota(jnp.int32, (1, 256), 1) // HD

    @pl.loop(0, 3)
    def _(group):
        for when, t in LATE.items():
            @pl.when(image * 3 + group == when)
            def _():
                gather.run(tick(t))

        lanes = pl.ds(pl.multiple_of(group * 256, 256), 256)
        q_group = queries[image, :, lanes]
        k_group = k_pad[image, :, lanes]
        v_group = v_pad[image, :, lanes]
        stacked = jnp.concatenate(
            [jnp.where(head_of == h, q_group, jnp.zeros_like(q_group)) for h in range(4)], axis=0
        )
        raw = dot_nt(stacked, k_group)
        probs = []
        for h in range(4):
            head = group * 4 + h
            scores = raw[h * 208 : (h + 1) * 208, :] + bias[image, head].astype(F32)
            top = jnp.max(scores, axis=-1, keepdims=True)
            raised = jnp.exp(scores - top)
            prob = (raised * (1.0 / jnp.sum(raised, axis=-1, keepdims=True))).astype(BF16)
            prob_ref[0, head] = prob
            probs.append(prob)
        mixed = dot_nn(jnp.concatenate(probs, axis=0), v_group)
        out = mixed[0:208]
        for h in range(1, 4):
            out = jnp.where(head_of == h, mixed[h * 208 : (h + 1) * 208], out)
        att_ref[0, :, lanes] = out.astype(BF16)

    branch_ref[0] = dot_nn(att_ref[0], wa_ref[3]) + pb_ref[...]

    @pl.when(image == images - 1)
    def _():
        for t in LAST:
            gather.run(tick(t))
        for chunk in range(4, ROW_CHUNKS):
            gather.arrive(chunk, 3)
        for chunk in range(ROW_CHUNKS, len(gather.chunks)):
            gather.arrive(chunk, 0)
        gather.drain()
        for k in range(1, narrow):
            extra(0, k).wait_send()
            extra(1, k).wait_send()
        for which in range(3):
            keep(which).wait()


class Reduce:
    STEPS = 7

    def __init__(self, near, beyond, source, half, quarter, eighth, between, total, send, recv, first_sem):
        self.near, self.beyond, self.source, self.total = near, beyond, source, total
        self.half, self.quarter, self.eighth, self.between = half, quarter, eighth, between
        self.send, self.recv, self.first_sem = send, recv, first_sem
        self.rows = eighth.shape[0]

    @staticmethod
    def scratch(rows, width, beyond):
        shapes = [(rows // 2, width), (rows // 4, width), (rows // 8, width), (2 * max(beyond, 1), rows // 8, width)]
        return [pltpu.VMEM(shape, F32) for shape in shapes]

    def span(self, ref, start, count):
        return ref.at[pl.ds(pl.multiple_of(start, 8), count), :]

    def value(self, ref, start, count):
        return ref[pl.ds(pl.multiple_of(start, 8), count), :]

    def copy(self, step):
        near, rows = self.near, self.rows
        half_at = near.core * 4 * rows
        quarter_at = half_at + near.first_bit * 2 * rows
        own_at = quarter_at + near.second_bit * rows
        if step == 0:
            source, target, to = self.span(self.source, (1 - near.core) * 4 * rows, 4 * rows), self.half, near.twin
        elif step == 1:
            source, target, to = (
                self.span(self.half, (1 - near.first_bit) * 2 * rows, 2 * rows), self.quarter, near.first
            )
        elif step == 2:
            source, target, to = self.span(self.quarter, (1 - near.second_bit) * rows, rows), self.eighth, near.second
        else:
            at, count, to = (
                (own_at, rows, near.second), (quarter_at, 2 * rows, near.first), (half_at, 4 * rows, near.twin)
            )[step - 3]
            source = target = self.span(self.total, at, count)
        return self.remote(source, target, step, near.base + to)

    def remote(self, source, target, place, to):
        place += self.first_sem
        return pltpu.make_async_remote_copy(
            src_ref=source, dst_ref=target, send_sem=self.send.at[place], recv_sem=self.recv.at[place],
            device_id={"wide": to}, device_id_type=MESH,
        )

    def run(self, step):
        near, rows = self.near, self.rows
        if step > 0:
            self.copy(step - 1).wait_recv()
        if step == 1:
            self.half[...] += self.value(self.source, near.core * 4 * rows, 4 * rows)
        if step == 2:
            self.quarter[...] += self.value(self.half, near.first_bit * 2 * rows, 2 * rows)
        if step == 3:
            summed = self.eighth[...] + self.value(self.quarter, near.second_bit * rows, rows)
            for i in range(self.beyond):
                self.between[2 * i] = summed
                copy = self.remote(self.between.at[2 * i], self.between.at[2 * i + 1], 6 + i, near.beyond(i))
                copy.start()
                copy.wait()
                summed = self.between[2 * i] + self.between[2 * i + 1]
            own_at = (near.core * 4 + near.first_bit * 2 + near.second_bit) * rows
            self.total[pl.ds(pl.multiple_of(own_at, 8), rows), :] = summed
        if step < 6:
            self.copy(step).start()

    def drain(self):
        for step in range(6):
            self.copy(step).wait_send()


def greet(near, beyond, narrow=1):
    sem = pltpu.get_barrier_semaphore()
    for k in range(1, narrow):
        pl.semaphore_signal(sem, inc=1, device_id={"narrow": (near.z + k) % narrow}, device_id_type=MESH)
    for k in range(1, SLICES):
        other = near.base + (near.me + k) % SLICES
        pl.semaphore_signal(sem, inc=1, device_id={"wide": other}, device_id_type=MESH)
    for i in range(beyond):
        pl.semaphore_signal(sem, inc=1, device_id={"wide": near.beyond(i)}, device_id_type=MESH)
    pl.semaphore_wait(sem, narrow - 1 + SLICES - 1 + beyond)


PAIR = 2
FF_GATHER = {0: ((8, 1),), 1: ((8, 2), (9, 1)), 3: ((8, 3), (9, 2), (10, 1)), 5: ((9, 3), (10, 2)), 8: ((10, 3),)}

FF_SUM = {4: 0, 7: 1, 10: 2, 11: 3, 13: 4, 15: 5}


def feed_forward(
    grid_ref, tok_ref, branch_ref, cot_ref, vec_ref, small_ref, ownb_ref, ownc_ref, slices, gath_b, _,
    out_ref, mg_ref, out_b, grad_c, sums_ref, gath_c,
    total_b, stage, wb, wc, second_ins, branch_lows, mlp_acc, second_acc, grad_b, half, quarter, eighth, between,
    loads, send, recv, gather_send, gather_recv, narrow, beyond,
):
    slot, pair = pl.program_id(0), pl.program_id(1)
    slots, pairs = pl.num_programs(0), pl.num_programs(1)
    rows = PAIR * 208
    gather = Gather(narrow, slices, (None, None, gath_c), gather_send, gather_recv, done=tuple((ROW_CHUNKS + k, 0) for k in range(3)))
    reduction = Reduce(gather, beyond, grad_b, half, quarter, eighth, between, total_b, send, recv, 0)

    def load(which, at):
        return pltpu.make_async_copy((gath_b, gath_c)[which].at[at], stage.at[which], loads.at[which])

    @pl.when((slot == 0) & (pair == 0))
    def _():
        greet(gather, beyond, narrow)
        wb[0] = ownb_ref[...]
        wc[0] = ownc_ref[...]
        grad_b[...] = jnp.zeros_like(grad_b)
        grad_c[...] = jnp.zeros_like(grad_c)
        sums_ref[...] = jnp.zeros_like(sums_ref)

    for when, steps in FF_GATHER.items():
        @pl.when(slot * pairs + pair == when)
        def _():
            gather.run(steps)

    for when, step in FF_SUM.items():
        @pl.when(slot * pairs + pair == when)
        def _():
            reduction.run(step)

    for k in range(1, narrow):
        @pl.when((pair == pairs - 1) & (slot == k - 1))
        def _():
            load(0, k - 1).start()
            if k > 1:
                gather.arrive(ROW_CHUNKS + k - 1, 3)
                load(1, k - 1).start()

    attn_scale, second_gain, second_shift, mlp_scale, down_bias = (vec_ref[i : i + 1, :] for i in range(5))

    def residual():
        branch = branch_ref[...].reshape(rows, 768)
        return branch, tok_ref[...].reshape(rows, 768).astype(F32) + attn_scale * branch

    def masked_cotangent():
        at = lax.broadcasted_iota(jnp.int32, (rows, 1), 0)
        limit = jnp.zeros((rows, 1), jnp.int32)
        for i in range(PAIR):
            image = pair * PAIR + i
            inside = (at >= i * 208) & (at < (i + 1) * 208)
            limit = jnp.where(inside, grid_ref[image, 0] * grid_ref[image, 1] + i * 208, limit)
        return jnp.where(at <= limit, cot_ref[...].reshape(rows, 768).astype(F32), 0.0)

    @pl.when(slot == 0)
    def _():
        _, middle = residual()
        normed, _ = norm_stats(middle)
        second_ins[pair] = (normed * second_gain + second_shift).astype(BF16)
        branch_lows[pair] = (masked_cotangent() * mlp_scale).astype(BF16)
        mlp_acc[pair] = jnp.zeros((rows, 768), F32)
        second_acc[pair] = jnp.zeros((rows, 768), F32)

    second_in, branch_low = second_ins[pair], branch_lows[pair]
    up, down = wb[slot % 2], wc[slot % 2]
    up_pre = dot_nn(second_in, up) + small_ref[slot, 2:3, :]
    cdf = 0.5 * (1.0 + lax.erf(up_pre * INV_ROOT_TWO))
    hidden = (up_pre * cdf).astype(BF16)
    slope = cdf + up_pre * jnp.exp(-0.5 * up_pre * up_pre) * INV_ROOT_TWO_PI
    mlp_acc[pair] += dot_nn(hidden, down)
    pre_low = (dot_nt(branch_low, down) * slope).astype(BF16)
    second_acc[pair] += dot_nt(pre_low, up)

    @pl.when(slot == 0)
    def _():
        grad_c[...] += dot_tn(hidden, branch_low)
        grad_b[...] += dot_tn(second_in, pre_low)
        sums_ref[6] += fold_rows(pre_low.astype(F32))

    @pl.when((pair == pairs - 1) & (slot == 0))
    def _():
        gather.arrive(ROW_CHUNKS, 3)
        load(1, 0).start()

    @pl.when((pair == pairs - 1) & (slot < slots - 1))
    def _():
        for which, weights in enumerate((wb, wc)):
            load(which, slot).wait()
            weights[(slot + 1) % 2] = stage[which].astype(BF16)

    @pl.when(slot == slots - 1)
    def _():
        branch, middle = residual()
        normed, inv = norm_stats(middle)
        out_grad = masked_cotangent()
        mlp_branch = mlp_acc[pair] + down_bias
        out_ref[...] = (middle + mlp_scale * mlp_branch).astype(BF16).reshape(PAIR, 208, 768)
        second_grad = second_acc[pair]
        middle_grad = out_grad + norm_back(second_grad, normed, inv, second_gain)
        mg_ref[...] = middle_grad.reshape(PAIR, 208, 768)
        sums_ref[0] += fold_rows(out_grad * mlp_branch)
        sums_ref[1] += fold_rows(out_grad)
        sums_ref[2] += fold_rows(second_grad * normed)
        sums_ref[3] += fold_rows(second_grad)
        sums_ref[4] += fold_rows(middle_grad * branch)
        sums_ref[5] += fold_rows(middle_grad)

    @pl.when((slot == slots - 1) & (pair == pairs - 1))
    def _():
        reduction.run(6)
        copy = pltpu.make_async_copy(total_b, out_b, loads.at[0])
        copy.start()
        copy.wait()
        reduction.drain()
        gather.drain()


SMALL_ROWS = 128
AB_TICKS = {0: ((0, 0),), 1: ((0, 1),), 4: ((0, 2),), 6: ((0, 3),)}
AB_LATE = {0: ((1, 0), (0, 4)), 3: ((1, 1),), 7: ((0, 5),), 9: ((1, 2),), 12: ((1, 3),), 15: ((1, 4),)}
AB_LAST = ((0, 6), (1, 5), (1, 6))


def attention_backward(
    sid_ref, grid_ref, tok_ref, mg_ref, att_ref, q0_ref, k0_ref, v0_ref, p0_ref, q_ref, k_ref, v_ref, p1_ref, p2_ref,
    vec_ref, wa_ref, ff_sums_ref, grad_c,
    tg_ref, total_out, out_c, late_total,
    total, total_c, grads, attn_lows, kept, dq, dk, dv, lines, edges, sums, late, late_in, late_between,
    *rest, beyond,
):
    step = pl.program_id(0)
    half = pl.num_programs(0) // 2
    rows = PAIR * 208
    near = Neighbours()
    send, recv, late_send, late_recv, local = rest[8:]
    chains = (
        Reduce(near, beyond, grad_c, *rest[0:4], total_c, send, recv, 0),
        Reduce(near, beyond, grads, *rest[4:8], total, send, recv, 6 + beyond),
    )
    attn_scale, first_gain, first_shift = (vec_ref[i : i + 1, :] for i in range(3))
    head_of = lax.broadcasted_iota(jnp.int32, (1, 256), 1) // HD

    def advance(i):
        table = [(when % PAIR, when // PAIR, steps) for when, steps in AB_TICKS.items()]
        table += [(8 + when % 4, half + when // 4, steps) for when, steps in AB_LATE.items()]
        for part, when, steps in table:
            if part == i:
                @pl.when(step == when)
                def _():
                    for chain, at in steps:
                        chains[chain].run(at)

    def stack(group):
        return jnp.concatenate([jnp.where(head_of == h, group, jnp.zeros_like(group)) for h in range(4)], axis=0)

    def merge(mixed):
        out = mixed[0:208]
        for h in range(1, 4):
            out = jnp.where(head_of == h, mixed[h * 208 : (h + 1) * 208], out)
        return out

    def heads_back(q_group, k_group, v_group, g_group, prob_at, each):
        q_stack, g_stack = stack(q_group), stack(g_group)
        prob_grads = dot_nt(g_stack, v_group)
        lows = []
        for h in range(4):
            prob = prob_at(h).astype(F32)
            prob_grad = prob_grads[h * 208 : (h + 1) * 208]
            score_grad = prob * (prob_grad - jnp.sum(prob * prob_grad, axis=-1, keepdims=True))
            low = score_grad.astype(BF16)
            lows.append(low)
            each(h, score_grad, low)
        low_stack = jnp.concatenate(lows, axis=0)
        prob_stack = jnp.concatenate([prob_at(h) for h in range(4)], axis=0)
        return (
            merge(dot_nn(low_stack, k_group)).astype(BF16) * jnp.asarray(HD ** -0.5, BF16),
            dot_tn(low_stack, q_stack)[0:208].astype(BF16),
            dot_tn(prob_stack, g_stack)[0:208].astype(BF16),
        )

    @pl.when(step == 0)
    def _():
        greet(near, beyond)
        grads[...] = jnp.zeros_like(grads)
        sums[...] = jnp.zeros_like(sums)
        lines[...] = jnp.zeros_like(lines)
        edges[...] = jnp.zeros_like(edges)
        late[...] = jnp.zeros_like(late)

    normed, inv = norm_stats(tok_ref[...].reshape(rows, 768).astype(F32))
    middle_grad = mg_ref[...].reshape(rows, 768)

    @pl.when(step < half)
    def _():
        attn_low = (middle_grad * attn_scale).astype(BF16)
        attn_lows[step] = attn_low
        attended_grad = dot_nt(attn_low, wa_ref[3, 0:256, :]).astype(BF16)
        grads[576:768, :] += dot_tn(att_ref[...].reshape(rows, 256), attn_low)[0:192, :]
        flip = (
            lax.broadcasted_iota(jnp.int32, (208, 208), 0) + lax.broadcasted_iota(jnp.int32, (208, 208), 1) == 207
        ).astype(BF16)

        for i in range(PAIR):
            advance(i)
            image = step * PAIR + i
            p, s, limit, later, p_patch, s_patch = slot_masks(grid_ref[image, 0], grid_ref[image, 1], True)
            both = p_patch & s_patch
            kind = sid_ref[image]

            def table_grad(h, score_grad, low):
                if h == 3:
                    return
                low_rest = (score_grad - low.astype(F32)).astype(BF16)
                turned = dot_nn(flip, low) + dot_nn(flip, low_rest)
                patches = jnp.where(both, turned, 0.0)
                edge = turned - patches
                for which, part in enumerate((jnp.where(later, patches, 0.0), jnp.where(later, 0.0, patches))):
                    wide = jnp.concatenate([part, jnp.zeros((208, 256), F32)], axis=1)
                    folded = jnp.sum(pltpu.roll(wide, 0, 1, stride=1, stride_axis=0), axis=0, keepdims=True)
                    row = which * 3 + h
                    for shape_at in range(len(GRIDS)):
                        lines[shape_at, row : row + 1, :] += jnp.where(kind == shape_at, folded, 0.0)
                class_query = jnp.where((p == 0) & s_patch, edge, 0.0)
                class_key = jnp.where(p_patch & (s == 0), edge, 0.0)
                for at, part in enumerate((class_query, class_key, edge - class_query - class_key)):
                    edges[at * 3 + h] += fold_rows(part)

            here = slice(i * 208, (i + 1) * 208)
            own = heads_back(
                q0_ref[i], k0_ref[i], v0_ref[i], attended_grad[here], lambda h: p0_ref[i, h], table_grad
            )
            for c, grad in enumerate(own):
                kept[c, step, here, :] = grad
            sums[0] += fold_rows(own[0].astype(F32))
            sums[1] += fold_rows(own[2].astype(F32))

        first_in = (normed * first_gain + first_shift).astype(BF16)
        for c in range(3):
            grads[c * 192 : (c + 1) * 192, :] += dot_tn(kept[c, step], first_in)[0:192, :]

    @pl.when(step == half)
    def _():
        grads[768 : 768 + SMALL_ROWS, :] = jnp.zeros((SMALL_ROWS, 768), F32)
        for shape_at in range(len(GRIDS)):
            grads[768 + shape_at * 8 : 776 + shape_at * 8, 0:DIAG] = lines[shape_at]
        for at in range(9):
            grads[832 + at : 833 + at, 0:256] = jnp.sum(edges[at], axis=0, keepdims=True)
        for at in range(2):
            grads[848 + at : 849 + at, 0:256] = jnp.sum(sums[at], axis=0, keepdims=True)
        for at in range(7):
            grads[856 + at : 857 + at, :] = jnp.sum(ff_sums_ref[at], axis=0, keepdims=True)

    @pl.when(step >= half)
    def _():
        at = step - half
        attended_grad = dot_nt(attn_lows[at], wa_ref[3, 256:768, :]).astype(BF16)
        for c, ref in enumerate((dq, dk, dv)):
            ref[:, 0:256] = kept[c, at]
        for i in range(PAIR):
            here = slice(i * 208, (i + 1) * 208)
            for group in (1, 2):
                advance(8 + i * 2 + group - 1)
                lanes = slice(group * 256, group * 256 + 256)
                probs = (p1_ref, p2_ref)[group - 1]
                parts = heads_back(
                    q_ref[i, :, lanes], k_ref[i, :, lanes], v_ref[i, :, lanes],
                    attended_grad[here, (group - 1) * 256 : group * 256], lambda h: probs[i, h], lambda *_: None,
                )
                for ref, part in zip((dq, dk, dv), parts):
                    ref[here, lanes] = part
        first_grad = dot_nn(dq[...], wa_ref[0]) + dot_nn(dk[...], wa_ref[1]) + dot_nn(dv[...], wa_ref[2])
        tg_ref[...] = (middle_grad + norm_back(first_grad, normed, inv, first_gain)).reshape(PAIR, 208, 768)
        late[0:8, :] += fold_rows(first_grad * normed)
        late[8:16, :] += fold_rows(first_grad)

    @pl.when(step == 2 * half - 1)
    def _():
        copies = [
            pltpu.make_async_remote_copy(
                src_ref=late, dst_ref=late_in.at[k - 1], send_sem=late_send.at[k - 1], recv_sem=late_recv.at[k - 1],
                device_id={"wide": near.base + (near.me + k) % SLICES}, device_id_type=MESH,
            )
            for k in range(1, SLICES)
        ]
        for copy in copies:
            copy.start()
        outs = [
            pltpu.make_async_copy(source, target, local.at[i])
            for i, (source, target) in enumerate(((total_c, out_c), (total, total_out)))
        ]
        for chain, at in AB_LAST:
            chains[chain].run(at)
        for copy in outs:
            copy.start()
        for copy in copies:
            copy.wait()
        summed = late[...]
        for k in range(SLICES - 1):
            summed = summed + late_in[k]
        for i in range(beyond):
            late_between[2 * i] = summed
            copy = pltpu.make_async_remote_copy(
                src_ref=late_between.at[2 * i], dst_ref=late_between.at[2 * i + 1],
                send_sem=late_send.at[SLICES - 1 + i], recv_sem=late_recv.at[SLICES - 1 + i],
                device_id={"wide": near.beyond(i)}, device_id_type=MESH,
            )
            copy.start()
            copy.wait()
            summed = late_between[2 * i] + late_between[2 * i + 1]
        late_total[...] = summed
        for copy in outs:
            copy.wait()
        for chain in chains:
            chain.drain()


def finish(tg_in, out_in, b_in, c_in, total_ref, tg_ref, out_ref, b_ref, c_ref, qkv_ref, proj_ref, table_ref):
    tg_ref[...] = tg_in[...]
    out_ref[...] = out_in[...]
    b_ref[...] = b_in[...]
    c_ref[...] = c_in[...]

    step, steps = pl.program_id(0), pl.num_programs(0)
    rows = qkv_ref.shape[0]
    qkv_ref[...] = total_ref[pl.ds(pl.multiple_of(step * rows, 8), rows), :]
    rows = proj_ref.shape[0]
    proj_ref[...] = total_ref[pl.ds(pl.multiple_of(576 + step * rows, 8), rows), :]

    @pl.when(step == 0)
    def _():
        table_ref[...] = jnp.zeros_like(table_ref)

    for shape_at in range(len(GRIDS)):
        @pl.when(step == shape_at)
        def _():
            for which, row, col, at, size in windows(shape_at):
                first = 768 + shape_at * 8 + which * 3
                table_ref[row, 0:3, col : col + size] += total_ref[first : first + 3, at : at + size]


def make_body(wide_size, narrow_size):
    def body(
        tokens, grid_shape, first_gain, first_shift, qkv_weight, query_bias, value_bias, rel_table, proj_weight,
        proj_bias, attn_scale, second_gain, second_shift, up_weight, up_bias, down_weight, down_bias, mlp_scale,
        cotangent,
    ):
        images, slots, width = tokens.shape
        heads, table_size = rel_table.shape
        local = heads * HD
        own_a = jnp.concatenate(
            [jnp.transpose(qkv_weight, (0, 2, 1)).reshape(3 * local, width), proj_weight], axis=0
        )
        table = rel_table.astype(F32)
        square = table[:, : SPAN * SPAN].reshape(heads, SPAN, SPAN)[:, ::-1, ::-1]
        square = jnp.pad(jnp.transpose(square, (1, 0, 2)), ((0, 0), (0, 8 - heads), (0, 128 - SPAN)))

        def small_for(k):
            def at(v, start):
                return jnp.pad(v.astype(F32).reshape(1, -1), ((0, 0), (start, width - start - v.size)))

            return jnp.concatenate(
                [
                    at(query_bias, k * local), at(value_bias, k * local), at(up_bias, 0),
                    at(table[:, SPAN * SPAN :].reshape(-1), 0), jnp.zeros((4, width), F32),
                ]
            )

        small = jnp.stack([small_for(k) for k in range(narrow_size)])
        all_heads = narrow_size * heads

        kinds = jnp.array(GRIDS, jnp.int32)
        sid = jnp.argmax(jnp.all(grid_shape[:, None, :] == kinds[None], axis=-1), axis=-1).astype(jnp.int32)

        def row(v):
            return v.astype(F32).reshape(1, -1)

        smem = pl.BlockSpec(memory_space=pltpu.SMEM)
        anyspace = pl.BlockSpec(memory_space=pl.ANY)
        vmem = pl.BlockSpec(memory_space=pltpu.VMEM)

        def whole(*shape):
            return pl.BlockSpec(shape, lambda i, *_: (0,) * len(shape))

        def per_image(*shape):
            return pl.BlockSpec((1,) + shape, lambda i, *_: (i,) + (0,) * len(shape))

        def struct(*shape, dtype=F32):
            return jax.ShapeDtypeStruct(shape, dtype)

        params = pltpu.CompilerParams(vmem_limit_bytes=VMEM_LIMIT, dimension_semantics=("arbitrary",))
        copies = len(chunks_of(narrow_size)) * (narrow_size - 1 + 7)
        copies = len(chunks_of(narrow_size)) * (narrow_size - 1 + 7)
        me = lax.axis_index("wide") % SLICES
        slices = jnp.stack(
            [lax.dynamic_slice_in_dim(own_a.reshape(4, local, width), me * PART_ROWS, PART_ROWS, 1).reshape(-1, width)]
            + [lax.dynamic_slice_in_dim(w, me * SLICE_ROWS, SLICE_ROWS, 0) for w in (up_weight, down_weight)]
        ).astype(F32)
        probs, attended, branch, weights_a, small, queries, keys, values, gath_b, gath_c = pl.pallas_call(
            functools.partial(attention_forward, narrow=narrow_size),
            grid=(images,),
            in_specs=[smem, smem, vmem] + [whole(1, width)] * 3 + [vmem] * 4,
            out_specs=[per_image(all_heads, slots, 256), per_image(slots, width), per_image(slots, width)]
            + [vmem, vmem] + [anyspace] * 5,
            scratch_shapes=[
                pltpu.VMEM((narrow_size - 1, width, width), F32),
                pltpu.VMEM((images, slots, width), BF16),
                pltpu.VMEM((images, slots, width), BF16),
                pltpu.VMEM((images, 256, width), BF16),
                pltpu.VMEM((images, 256, width), BF16),
                pltpu.VMEM((images, all_heads, slots, 256), BF16),
                pltpu.VMEM((16, 8, DIAG), F32),
                pltpu.VMEM((48, DIAG), F32),
                pltpu.VMEM((narrow_size - 1, 48, DIAG), F32),
                pltpu.VMEM((narrow_size, 8, width), F32),
                pltpu.SemaphoreType.DMA((copies,)),
                pltpu.SemaphoreType.DMA((copies,)),
                pltpu.SemaphoreType.DMA((2 * narrow_size - 2,)),
                pltpu.SemaphoreType.DMA((2 * narrow_size - 2,)),
                pltpu.SemaphoreType.DMA((3,)),
            ],
            out_shape=[
                struct(images, all_heads, slots, 256, dtype=BF16),
                struct(images, slots, width, dtype=BF16),
                struct(images, slots, width),
                struct(4, width, width, dtype=BF16),
                struct(narrow_size, 8, width),
                struct(images, slots, width, dtype=BF16),
                struct(images, 256, width, dtype=BF16),
                struct(images, 256, width, dtype=BF16),
                struct(narrow_size - 1, width, width),
                struct(narrow_size - 1, width, width),
            ],
            compiler_params=pltpu.CompilerParams(
                vmem_limit_bytes=VMEM_LIMIT, dimension_semantics=("arbitrary",), collective_id=0,
                has_side_effects=True,
            ),
            name="attention_forward",
        )(
            sid, grid_shape, tokens, row(first_gain), row(first_shift), row(proj_bias), own_a, slices, square, small,
        )

        vec = jnp.concatenate([row(v) for v in (attn_scale, second_gain, second_shift, mlp_scale, down_bias)])
        beyond = (wide_size // SLICES).bit_length() - 1
        rows = PAIR * slots
        pairs = images // PAIR
        last = narrow_size - 1

        def remote_params(at):
            return pltpu.CompilerParams(
                vmem_limit_bytes=VMEM_LIMIT, collective_id=at, has_side_effects=True,
            )

        ends = pl.BlockSpec((PAIR, slots, width), lambda s, i: (jnp.where((s > 0) & (s < last), pairs - 1, i), 0, 0))
        outs = pl.BlockSpec((PAIR, slots, width), lambda s, i: (jnp.where(s < last, 0, i), 0, 0))
        layer_out, middle_grad, grad_b, grad_c, sums, _ = pl.pallas_call(
            functools.partial(feed_forward, narrow=narrow_size, beyond=beyond),
            grid=(narrow_size, pairs),
            in_specs=[smem] + [ends] * 3 + [vmem] * 5 + [anyspace] * 2,
            out_specs=[outs] * 2 + [anyspace, vmem, vmem, anyspace],
            input_output_aliases={10: 5},
            scratch_shapes=[
                pltpu.VMEM((width, width), F32),
                pltpu.VMEM((2, width, width), F32),
                pltpu.VMEM((2, width, width), BF16),
                pltpu.VMEM((2, width, width), BF16),
                pltpu.VMEM((pairs, rows, width), BF16),
                pltpu.VMEM((pairs, rows, width), BF16),
                pltpu.VMEM((pairs, rows, width), F32),
                pltpu.VMEM((pairs, rows, width), F32),
                pltpu.VMEM((width, width), F32),
            ]
            + Reduce.scratch(width, width, beyond)
            + [
                pltpu.SemaphoreType.DMA((2,)),
                pltpu.SemaphoreType.DMA((6 + beyond,)),
                pltpu.SemaphoreType.DMA((6 + beyond,)),
                pltpu.SemaphoreType.DMA((copies,)),
                pltpu.SemaphoreType.DMA((copies,)),
            ],
            out_shape=[
                struct(images, slots, width, dtype=BF16),
                struct(images, slots, width),
                struct(width, width),
                struct(width, width),
                struct(7, 8, width),
                struct(narrow_size - 1, width, width),
            ],
            compiler_params=remote_params(1),
            name="feed_forward",
        )(grid_shape, tokens, branch, cotangent, vec, small, up_weight, down_weight, slices, gath_b, gath_c)

        def first_pass(*shape):
            return pl.BlockSpec((PAIR,) + shape, lambda i: (jnp.minimum(i, pairs - 1),) + (0,) * len(shape))

        def second_pass(*shape, at=0):
            return pl.BlockSpec((PAIR,) + shape, lambda i: (jnp.maximum(i - pairs, 0), at) + (0,) * (len(shape) - 1))

        both_passes = pl.BlockSpec((PAIR, slots, width), lambda i: (i % pairs, 0, 0))
        total_rows = width + SMALL_ROWS
        vec = jnp.concatenate([row(v) for v in (attn_scale, first_gain, first_shift)])
        tokens_grad, total, grad_c, late = pl.pallas_call(
            functools.partial(attention_backward, beyond=beyond),
            grid=(2 * pairs,),
            in_specs=[smem, smem, both_passes, both_passes]
            + [first_pass(slots, 256)] * 2
            + [first_pass(256, 256)] * 2
            + [first_pass(4, slots, 256)]
            + [second_pass(slots, width), second_pass(256, width), second_pass(256, width)]
            + [second_pass(4, slots, 256, at=1), second_pass(4, slots, 256, at=2)]
            + [vmem] * 4,
            out_specs=[second_pass(slots, width), anyspace, anyspace, vmem],
            scratch_shapes=[
                pltpu.VMEM((total_rows, width), F32),
                pltpu.VMEM((width, width), F32),
                pltpu.VMEM((total_rows, width), F32),
                pltpu.VMEM((pairs, rows, width), BF16),
                pltpu.VMEM((3, pairs, rows, 256), BF16),
                pltpu.VMEM((rows, width), BF16),
                pltpu.VMEM((rows, width), BF16),
                pltpu.VMEM((rows, width), BF16),
                pltpu.VMEM((len(GRIDS), 8, DIAG), F32),
                pltpu.VMEM((9, 8, 256), F32),
                pltpu.VMEM((2, 8, 256), F32),
                pltpu.VMEM((16, width), F32),
                pltpu.VMEM((SLICES - 1, 16, width), F32),
                pltpu.VMEM((2 * max(beyond, 1), 16, width), F32),
            ]
            + Reduce.scratch(width, width, beyond)
            + Reduce.scratch(total_rows, width, beyond)
            + [
                pltpu.SemaphoreType.DMA((2 * (6 + beyond),)),
                pltpu.SemaphoreType.DMA((2 * (6 + beyond),)),
                pltpu.SemaphoreType.DMA((SLICES - 1 + beyond,)),
                pltpu.SemaphoreType.DMA((SLICES - 1 + beyond,)),
                pltpu.SemaphoreType.DMA((2,)),
            ],
            out_shape=[
                struct(images, slots, width), struct(total_rows, width), struct(width, width), struct(16, width),
            ],
            compiler_params=remote_params(2),
            name="attention_backward",
        )(
            sid, grid_shape, tokens, middle_grad, attended, queries, keys, values, probs, queries, keys, values, probs,
            probs, vec, weights_a, sums, grad_c,
        )

        parts = len(GRIDS)

        def image_block():
            return pl.BlockSpec((images // parts, slots, width), lambda i: (i, 0, 0))

        def row_block(total_rows=width):
            return pl.BlockSpec((total_rows // parts, width), lambda i: (i, 0))

        tokens_grad, layer_out, grad_b, grad_c, qkv_grad, proj_grad, square_grad = pl.pallas_call(
            finish,
            grid=(parts,),
            in_specs=[image_block(), image_block(), row_block(), row_block(), vmem],
            out_specs=[image_block(), image_block(), row_block(), row_block(), row_block(3 * local), row_block(local), vmem],
            out_shape=[
                struct(images, slots, width), struct(images, slots, width, dtype=BF16), struct(width, width),
                struct(width, width), struct(3 * local, width), struct(local, width), struct(SPAN, 8, 128),
            ],
            compiler_params=params,
            name="finish",
        )(tokens_grad, layer_out, grad_b, grad_c, total)
        qkv_grad = jnp.transpose(qkv_grad.reshape(3, local, width), (0, 2, 1))
        square_grad = jnp.transpose(square_grad[:, :heads, :SPAN], (1, 0, 2))[:, ::-1, ::-1]
        edges = jnp.sum(total[width + 64 : width + 73, :256], axis=1).reshape(3, heads).T
        table_grad = jnp.concatenate([square_grad.reshape(heads, SPAN * SPAN), edges], axis=1)
        more = total[width + 80 : width + 82, :local]
        sums = total[width + 88 : width + 95]
        late = jnp.sum(late.reshape(2, 8, width), axis=1)
        return (
            layer_out,
            tokens_grad,
            late[0],
            late[1],
            qkv_grad,
            more[0],
            more[1],
            table_grad,
            proj_grad,
            sums[5] * attn_scale.astype(F32),
            sums[4],
            sums[2],
            sums[3],
            grad_b,
            sums[6],
            grad_c,
            sums[1] * mlp_scale.astype(F32),
            sums[0],
        )

    return body


def solution(mesh):
    rows = P("wide", None, None)
    return jax.shard_map(
        make_body(mesh.shape["wide"], mesh.shape["narrow"]),
        mesh=mesh,
        in_specs=(
            rows, P("wide", None), P(), P(), P(None, None, "narrow"), P("narrow"), P("narrow"), P("narrow", None),
            P("narrow", None), P(), P(), P(), P(), P(None, "narrow"), P("narrow"), P("narrow", None), P(), P(), rows,
        ),
        out_specs=(
            rows, rows, P(), P(), P(None, None, "narrow"), P("narrow"), P("narrow"), P("narrow", None),
            P("narrow", None), P(), P(), P(), P(), P(None, "narrow"), P("narrow"), P("narrow", None), P(), P(),
        ),
        check_vma=False,
    )
```

```python
import functools

import jax
import jax.numpy as jnp
from jax import lax
from jax.experimental import pallas as pl
from jax.experimental.pallas import tpu as pltpu
from jax.sharding import PartitionSpec as P

HD = 64
MAXG = 24
SPAN = 2 * MAXG - 1
EPSILON = 1e-06
MASKED = -1e30
INV_ROOT_TWO = 0.7071067811865476
INV_ROOT_TWO_PI = 0.3989422804014327
GRIDS = ((14, 14), (10, 20), (20, 10), (8, 24), (24, 8), (12, 16), (16, 12), (13, 15))
DIAG = 512
F32 = jnp.float32
BF16 = jnp.bfloat16
VMEM_LIMIT = 60 * 1024 * 1024


def dot_nn(a, b):
    return lax.dot_general(a, b, (((1,), (0,)), ((), ())), preferred_element_type=F32)


def dot_nt(a, b):
    return lax.dot_general(a, b, (((1,), (1,)), ((), ())), preferred_element_type=F32)


def dot_tn(a, b):
    return lax.dot_general(a, b, (((0,), (0,)), ((), ())), preferred_element_type=F32)


def row_mean(v):
    return jnp.sum(v, axis=-1, keepdims=True) * (1.0 / v.shape[-1])


def norm_stats(v):
    centred = v - row_mean(v)
    inv = lax.rsqrt(row_mean(centred * centred) + EPSILON)
    return centred * inv, inv


def norm_back(incoming, normed, inv, gain):
    scaled = incoming * gain
    return inv * (scaled - row_mean(scaled) - normed * row_mean(scaled * normed))


def fold_rows(v):
    rows = v.shape[0]
    return jnp.sum(v.reshape(rows // 8, 8, v.shape[1]), axis=0)


def windows(shape_at):
    high, wide = GRIDS[shape_at]
    centre = MAXG - 1
    for m in range(-high, high):
        at = 207 + m * wide
        if m > -high:
            yield 0, centre + m, centre, at, wide
        if m < high - 1:
            yield 1, centre + 1 + m, centre + 1 - wide, at + 1, wide - 1


def kind_of(grid_ref, image):
    high, wide = grid_ref[image, 0], grid_ref[image, 1]
    kind = jnp.int32(0)
    for at, (grid_high, grid_wide) in enumerate(GRIDS):
        kind = jnp.where((high == grid_high) & (wide == grid_wide), at, kind)
    return kind


def slot_masks(high, wide, reverse):
    rows = lax.broadcasted_iota(jnp.int32, (208, 1), 0)
    p = 207 - rows if reverse else rows
    s = lax.broadcasted_iota(jnp.int32, (1, 256), 1)
    limit = high * wide
    wide_f = wide.astype(F32)

    def column(slot):
        patch = (slot - 1).astype(F32)
        return patch - wide_f * jnp.floor((patch + 0.5) / wide_f)

    later = column(s) >= column(p)
    p_patch = (p >= 1) & (p <= limit)
    s_patch = (s >= 1) & (s <= limit)
    return p, s, limit, later, p_patch, s_patch


MESH = pl.DeviceIdType.MESH
SLICES = 8
SLICE_ROWS = 96
PART_ROWS = 24


def chunks_of(narrow):
    all_shards = tuple(range(1, narrow))
    rows = [(group, at, 24, all_shards) for group in range(2) for at in (0, 24, 48, 72)]
    return tuple(rows) + tuple((2, 0, SLICE_ROWS, (k,)) for k in all_shards)


ROW_CHUNKS = 8


class Neighbours:
    def __init__(self):
        self.wide = lax.axis_index("wide")
        self.me = self.wide % SLICES
        self.base = self.wide - self.me
        self.core = core = self.me % 2
        x_bit, y_bit = (self.me // 2) % 2, self.me // 4
        over_x, over_y = self.me + 2 - 4 * x_bit, self.me + 4 - 8 * y_bit
        self.first = over_x * (1 - core) + over_y * core
        self.second = over_y * (1 - core) + over_x * core
        self.first_bit = x_bit * (1 - core) + y_bit * core
        self.second_bit = y_bit * (1 - core) + x_bit * core
        self.third = over_x + over_y - self.me
        self.twin = self.me + 1 - 2 * core

    def beyond(self, step):
        size = SLICES << step
        return self.wide + size - 2 * size * ((self.wide // size) % 2)


class Gather(Neighbours):
    def __init__(self, narrow, slices, buffers, send, recv, done=()):
        super().__init__()
        self.done = done
        self.narrow, self.slices, self.buffers, self.send, self.recv = narrow, slices, buffers, send, recv
        self.z = lax.axis_index("narrow")
        self.chunks = chunks_of(narrow)
        self.per_chunk = narrow - 1 + 7
        self.started = []

    def copy(self, chunk, phase, piece):
        group, at, rows, shards = self.chunks[chunk]
        buffer = self.buffers[group]

        def part(owner):
            return buffer.at[
                pl.ds(shards[0] - 1, len(shards)), pl.ds(pl.multiple_of(owner * SLICE_ROWS + at, 8), rows), :
            ]

        place = chunk * self.per_chunk
        if phase == 0:
            place += piece - 1
            source = self.slices.at[group, pl.ds(at, rows), :]
            target = buffer.at[piece - 1, pl.ds(pl.multiple_of(self.me * SLICE_ROWS + at, 8), rows), :]
            device = {"narrow": (self.z + self.narrow - piece) % self.narrow}
        else:
            owners = (self.me, self.first, self.second, self.third)
            place += self.narrow - 1 + (0, 1, 3)[phase - 1] + piece
            source = target = part(owners[piece])
            device = {"wide": self.base + (self.first, self.second, self.twin)[phase - 1]}
        return pltpu.make_async_remote_copy(
            src_ref=source, dst_ref=target, send_sem=self.send.at[place], recv_sem=self.recv.at[place],
            device_id=device, device_id_type=MESH,
        )

    def pieces(self, chunk, phase):
        return (self.chunks[chunk][3], range(1), range(2), range(4))[phase]

    def start(self, chunk, phase):
        self.started.append((chunk, phase))
        for piece in self.pieces(chunk, phase):
            self.copy(chunk, phase, piece).start()

    def arrive(self, chunk, phase):
        for piece in self.pieces(chunk, phase):
            self.copy(chunk, phase, piece).wait_recv()

    def run(self, steps):
        for chunk, phase in steps:
            if phase > 0 and (chunk, phase - 1) not in self.done:
                self.arrive(chunk, phase - 1)
            self.start(chunk, phase)

    def drain(self):
        for chunk, phase in self.started:
            for piece in self.pieces(chunk, phase):
                self.copy(chunk, phase, piece).wait_send()

    def barrier(self):
        sem = pltpu.get_barrier_semaphore()
        for k in range(1, self.narrow):
            pl.semaphore_signal(
                sem, inc=1, device_id={"narrow": (self.z + k) % self.narrow}, device_id_type=MESH
            )
        for other in (self.first, self.second, self.twin):
            pl.semaphore_signal(sem, inc=1, device_id={"wide": self.base + other}, device_id_type=MESH)
        pl.semaphore_wait(sem, self.narrow - 1 + 3)


def tick(t):
    steps = ((t, 1), (t + 2, 0), (t - 1, 2), (t - 2, 3))
    return tuple((chunk, phase) for chunk, phase in steps if 0 <= chunk < ROW_CHUNKS + 3 * (phase == 0))


LATE = {7: 7, 16: 8}
LAST = (9,)


def attention_forward(
    grid_ref, tok_ref, gain_ref, shift_ref, pb_ref, own_ref, slices, table_ref, small_ref,
    prob_ref, att_ref, branch_ref, wa_ref, small_out, q_out, k_out, v_out, gath_b, gath_c,
    stage, first_in, queries, k_pad, v_pad, bias, lined, diag, far, smalls, send, recv, extra_send, extra_recv, local,
    narrow,
):
    image = pl.program_id(0)
    images = pl.num_programs(0)
    gather = Gather(narrow, slices, (stage, gath_b, gath_c), send, recv)

    def extra(which, k):
        source = diag if which else small_ref.at[k]
        target = far.at[k - 1] if which else smalls.at[k]
        place = which * (narrow - 1) + k - 1
        return pltpu.make_async_remote_copy(
            src_ref=source, dst_ref=target, send_sem=extra_send.at[place], recv_sem=extra_recv.at[place],
            device_id={"narrow": (gather.z + narrow - k) % narrow}, device_id_type=MESH,
        )

    def keep(which):
        source, target = ((queries, q_out), (k_pad, k_out), (v_pad, v_out))[which]
        return pltpu.make_async_copy(source, target, local.at[which])

    @pl.when(image == 0)
    def _():
        def bias_of(slot, at, table):
            p, s, limit, later, p_patch, s_patch = slot_masks(grid_ref[at, 0], grid_ref[at, 1], False)
            both = p_patch & s_patch
            open_key = s <= limit
            for h in range(3):
                row = h * 16 + kind_of(grid_ref, at) * 2
                toep = [
                    pltpu.roll(
                        jnp.broadcast_to(table(row + which), (208, DIAG)), DIAG - 207, 1, stride=1, stride_axis=0
                    )[:, :256]
                    for which in range(2)
                ]
                c0, c1, c2 = (smalls[slot, 3:4, h * 3 + c : h * 3 + c + 1] for c in range(3))
                outer = jnp.where((p == 0) & s_patch, c0, jnp.where(p_patch & (s == 0), c1, c2))
                value = jnp.where(both, jnp.where(later, toep[0], toep[1]), outer)
                bias[at, slot * 3 + h] = jnp.where(open_key, value, MASKED).astype(BF16)

        def far_bias(slot):
            @pl.loop(0, 8)
            def _(at):
                bias_of(slot, at, lambda row: far[slot - 1, pl.ds(row, 1), :])

        def weights_of(part):
            gather.arrive(part, 3)
            for slot in range(narrow - 1):
                for pair in range(4):
                    rows = [
                        stage[slot, pl.ds((2 * pair + i) * SLICE_ROWS + part * PART_ROWS, PART_ROWS), :]
                        for i in range(2)
                    ]
                    at = (slot + 1) * 192 + pair * 2 * PART_ROWS
                    wa_ref[part, at : at + 2 * PART_ROWS, :] = jnp.concatenate(rows, axis=0).astype(BF16)

        def project(part, target, finish):
            @pl.loop(0, 8)
            def _(at):
                target[at, 0:208, :] = finish(dot_nt(first_in[at], wa_ref[part])).astype(BF16)

            keep(part).start()

        lined[...] = jnp.zeros_like(lined)
        for shape_at in range(len(GRIDS)):
            for which, row, col, at, size in windows(shape_at):
                lined[shape_at * 2 + which, :, at : at + size] = table_ref[row, :, col : col + size]
        for h in range(3):
            for r in range(16):
                diag[h * 16 + r : h * 16 + r + 1, :] = lined[r, h : h + 1, :]
        gather.barrier()
        smalls[0] = small_ref[0]
        gather.run(((0, 0), (1, 0)))
        for k in range(1, narrow):
            extra(0, k).start()
            extra(1, k).start()
        k_pad[:, 208:256, :] = jnp.zeros((8, 48, 768), BF16)
        v_pad[:, 208:256, :] = jnp.zeros((8, 48, 768), BF16)
        for part in range(4):
            wa_ref[part, 0:192, :] = own_ref[part * 192 : (part + 1) * 192, :]

        @pl.loop(0, 8)
        def _(at):
            normed, _ = norm_stats(tok_ref[at].astype(F32))
            first_in[at] = (normed * gain_ref[...] + shift_ref[...]).astype(BF16)
            bias_of(0, at, lambda row: diag[pl.ds(row, 1), :])

        gather.run(tick(0))
        gather.run(tick(1))
        for k in range(1, narrow):
            extra(0, k).wait_recv()
            extra(1, k).wait_recv()
        far_bias(1)
        gather.run(tick(2))
        for k in range(2, narrow):
            far_bias(k)
        gather.run(tick(3))
        q_bias = sum(smalls[k, 0:1, :] for k in range(narrow))
        v_bias = sum(smalls[k, 1:2, :] for k in range(narrow))
        small_out[...] = smalls[...]
        weights_of(0)
        project(0, queries, lambda v: (v + q_bias) * (HD ** -0.5))
        gather.run(tick(4))
        weights_of(1)
        project(1, k_pad, lambda v: v)
        gather.run(tick(5))
        weights_of(2)
        project(2, v_pad, lambda v: v + v_bias)
        gather.run(tick(6))
        weights_of(3)

    head_of = lax.broadcasted_iota(jnp.int32, (1, 256), 1) // HD

    @pl.loop(0, 3)
    def _(group):
        for when, t in LATE.items():
            @pl.when(image * 3 + group == when)
            def _():
                gather.run(tick(t))

        lanes = pl.ds(pl.multiple_of(group * 256, 256), 256)
        q_group = queries[image, :, lanes]
        k_group = k_pad[image, :, lanes]
        v_group = v_pad[image, :, lanes]
        stacked = jnp.concatenate(
            [jnp.where(head_of == h, q_group, jnp.zeros_like(q_group)) for h in range(4)], axis=0
        )
        raw = dot_nt(stacked, k_group)
        probs = []
        for h in range(4):
            head = group * 4 + h
            scores = raw[h * 208 : (h + 1) * 208, :] + bias[image, head].astype(F32)
            top = jnp.max(scores, axis=-1, keepdims=True)
            raised = jnp.exp(scores - top)
            prob = (raised * (1.0 / jnp.sum(raised, axis=-1, keepdims=True))).astype(BF16)
            prob_ref[0, head] = prob
            probs.append(prob)
        mixed = dot_nn(jnp.concatenate(probs, axis=0), v_group)
        out = mixed[0:208]
        for h in range(1, 4):
            out = jnp.where(head_of == h, mixed[h * 208 : (h + 1) * 208], out)
        att_ref[0, :, lanes] = out.astype(BF16)

    branch_ref[0] = dot_nn(att_ref[0], wa_ref[3]) + pb_ref[...]

    @pl.when(image == images - 1)
    def _():
        for t in LAST:
            gather.run(tick(t))
        for chunk in range(4, ROW_CHUNKS):
            gather.arrive(chunk, 3)
        for chunk in range(ROW_CHUNKS, len(gather.chunks)):
            gather.arrive(chunk, 0)
        gather.drain()
        for k in range(1, narrow):
            extra(0, k).wait_send()
            extra(1, k).wait_send()
        for which in range(3):
            keep(which).wait()


class Reduce:
    STEPS = 7

    def __init__(self, near, beyond, source, half, quarter, eighth, between, total, send, recv, first_sem):
        self.near, self.beyond, self.source, self.total = near, beyond, source, total
        self.half, self.quarter, self.eighth, self.between = half, quarter, eighth, between
        self.send, self.recv, self.first_sem = send, recv, first_sem
        self.rows = eighth.shape[0]

    @staticmethod
    def scratch(rows, width, beyond):
        shapes = [(rows // 2, width), (rows // 4, width), (rows // 8, width), (2 * max(beyond, 1), rows // 8, width)]
        return [pltpu.VMEM(shape, F32) for shape in shapes]

    def span(self, ref, start, count):
        return ref.at[pl.ds(pl.multiple_of(start, 8), count), :]

    def value(self, ref, start, count):
        return ref[pl.ds(pl.multiple_of(start, 8), count), :]

    def copy(self, step):
        near, rows = self.near, self.rows
        half_at = near.core * 4 * rows
        quarter_at = half_at + near.first_bit * 2 * rows
        own_at = quarter_at + near.second_bit * rows
        if step == 0:
            source, target, to = self.span(self.source, (1 - near.core) * 4 * rows, 4 * rows), self.half, near.twin
        elif step == 1:
            source, target, to = (
                self.span(self.half, (1 - near.first_bit) * 2 * rows, 2 * rows), self.quarter, near.first
            )
        elif step == 2:
            source, target, to = self.span(self.quarter, (1 - near.second_bit) * rows, rows), self.eighth, near.second
        else:
            at, count, to = (
                (own_at, rows, near.second), (quarter_at, 2 * rows, near.first), (half_at, 4 * rows, near.twin)
            )[step - 3]
            source = target = self.span(self.total, at, count)
        return self.remote(source, target, step, near.base + to)

    def remote(self, source, target, place, to):
        place += self.first_sem
        return pltpu.make_async_remote_copy(
            src_ref=source, dst_ref=target, send_sem=self.send.at[place], recv_sem=self.recv.at[place],
            device_id={"wide": to}, device_id_type=MESH,
        )

    def run(self, step):
        near, rows = self.near, self.rows
        if step > 0:
            self.copy(step - 1).wait_recv()
        if step == 1:
            self.half[...] += self.value(self.source, near.core * 4 * rows, 4 * rows)
        if step == 2:
            self.quarter[...] += self.value(self.half, near.first_bit * 2 * rows, 2 * rows)
        if step == 3:
            summed = self.eighth[...] + self.value(self.quarter, near.second_bit * rows, rows)
            for i in range(self.beyond):
                self.between[2 * i] = summed
                copy = self.remote(self.between.at[2 * i], self.between.at[2 * i + 1], 6 + i, near.beyond(i))
                copy.start()
                copy.wait()
                summed = self.between[2 * i] + self.between[2 * i + 1]
            own_at = (near.core * 4 + near.first_bit * 2 + near.second_bit) * rows
            self.total[pl.ds(pl.multiple_of(own_at, 8), rows), :] = summed
        if step < 6:
            self.copy(step).start()

    def drain(self):
        for step in range(6):
            self.copy(step).wait_send()


def greet(near, beyond, narrow=1):
    sem = pltpu.get_barrier_semaphore()
    for k in range(1, narrow):
        pl.semaphore_signal(sem, inc=1, device_id={"narrow": (near.z + k) % narrow}, device_id_type=MESH)
    for k in range(1, SLICES):
        other = near.base + (near.me + k) % SLICES
        pl.semaphore_signal(sem, inc=1, device_id={"wide": other}, device_id_type=MESH)
    for i in range(beyond):
        pl.semaphore_signal(sem, inc=1, device_id={"wide": near.beyond(i)}, device_id_type=MESH)
    pl.semaphore_wait(sem, narrow - 1 + SLICES - 1 + beyond)


PAIR = 2
FF_GATHER = {0: ((8, 1),), 1: ((8, 2), (9, 1)), 2: ((10, 1),), 3: ((8, 3), (9, 2)), 5: ((9, 3), (10, 2)), 8: ((10, 3),)}

FF_SUM = {4: 0, 7: 1, 9: 2, 11: 3, 13: 4, 15: 5}


def feed_forward(
    grid_ref, tok_ref, branch_ref, cot_ref, vec_ref, small_ref, ownb_ref, ownc_ref, slices, gath_b, _,
    out_ref, mg_ref, out_b, grad_c, sums_ref, gath_c,
    total_b, stage, wb, wc, second_ins, branch_lows, mlp_acc, second_acc, grad_b, half, quarter, eighth, between,
    loads, send, recv, gather_send, gather_recv, narrow, beyond,
):
    slot, pair = pl.program_id(0), pl.program_id(1)
    slots, pairs = pl.num_programs(0), pl.num_programs(1)
    rows = PAIR * 208
    gather = Gather(narrow, slices, (None, None, gath_c), gather_send, gather_recv, done=tuple((ROW_CHUNKS + k, 0) for k in range(3)))
    reduction = Reduce(gather, beyond, grad_b, half, quarter, eighth, between, total_b, send, recv, 0)

    def load(which, at):
        return pltpu.make_async_copy((gath_b, gath_c)[which].at[at], stage.at[which], loads.at[which])

    @pl.when((slot == 0) & (pair == 0))
    def _():
        greet(gather, beyond, narrow)
        wb[0] = ownb_ref[...]
        wc[0] = ownc_ref[...]
        grad_b[...] = jnp.zeros_like(grad_b)
        grad_c[...] = jnp.zeros_like(grad_c)
        sums_ref[...] = jnp.zeros_like(sums_ref)

    for when, steps in FF_GATHER.items():
        @pl.when(slot * pairs + pair == when)
        def _():
            gather.run(steps)

    for when, step in FF_SUM.items():
        @pl.when(slot * pairs + pair == when)
        def _():
            reduction.run(step)

    for k in range(1, narrow):
        @pl.when((pair == pairs - 1) & (slot == k - 1))
        def _():
            load(0, k - 1).start()
            if k > 1:
                gather.arrive(ROW_CHUNKS + k - 1, 3)
                load(1, k - 1).start()

    attn_scale, second_gain, second_shift, mlp_scale, down_bias = (vec_ref[i : i + 1, :] for i in range(5))

    def residual():
        branch = branch_ref[...].reshape(rows, 768)
        return branch, tok_ref[...].reshape(rows, 768).astype(F32) + attn_scale * branch

    def masked_cotangent():
        at = lax.broadcasted_iota(jnp.int32, (rows, 1), 0)
        limit = jnp.zeros((rows, 1), jnp.int32)
        for i in range(PAIR):
            image = pair * PAIR + i
            inside = (at >= i * 208) & (at < (i + 1) * 208)
            limit = jnp.where(inside, grid_ref[image, 0] * grid_ref[image, 1] + i * 208, limit)
        return jnp.where(at <= limit, cot_ref[...].reshape(rows, 768).astype(F32), 0.0)

    @pl.when(slot == 0)
    def _():
        _, middle = residual()
        normed, _ = norm_stats(middle)
        second_ins[pair] = (normed * second_gain + second_shift).astype(BF16)
        branch_lows[pair] = (masked_cotangent() * mlp_scale).astype(BF16)
        mlp_acc[pair] = jnp.zeros((rows, 768), F32)
        second_acc[pair] = jnp.zeros((rows, 768), F32)

    second_in, branch_low = second_ins[pair], branch_lows[pair]
    up, down = wb[slot % 2], wc[slot % 2]
    up_pre = dot_nn(second_in, up) + small_ref[slot, 2:3, :]
    cdf = 0.5 * (1.0 + lax.erf(up_pre * INV_ROOT_TWO))
    hidden = (up_pre * cdf).astype(BF16)
    slope = cdf + up_pre * jnp.exp(-0.5 * up_pre * up_pre) * INV_ROOT_TWO_PI
    mlp_acc[pair] += dot_nn(hidden, down)
    pre_low = (dot_nt(branch_low, down) * slope).astype(BF16)
    second_acc[pair] += dot_nt(pre_low, up)

    @pl.when(slot == 0)
    def _():
        grad_c[...] += dot_tn(hidden, branch_low)
        grad_b[...] += dot_tn(second_in, pre_low)
        sums_ref[6] += fold_rows(pre_low.astype(F32))

    @pl.when((pair == pairs - 1) & (slot == 0))
    def _():
        gather.arrive(ROW_CHUNKS, 3)
        load(1, 0).start()

    @pl.when((pair == pairs - 1) & (slot < slots - 1))
    def _():
        for which, weights in enumerate((wb, wc)):
            load(which, slot).wait()
            weights[(slot + 1) % 2] = stage[which].astype(BF16)

    @pl.when(slot == slots - 1)
    def _():
        branch, middle = residual()
        normed, inv = norm_stats(middle)
        out_grad = masked_cotangent()
        mlp_branch = mlp_acc[pair] + down_bias
        out_ref[...] = (middle + mlp_scale * mlp_branch).astype(BF16).reshape(PAIR, 208, 768)
        second_grad = second_acc[pair]
        middle_grad = out_grad + norm_back(second_grad, normed, inv, second_gain)
        mg_ref[...] = middle_grad.reshape(PAIR, 208, 768)
        sums_ref[0] += fold_rows(out_grad * mlp_branch)
        sums_ref[1] += fold_rows(out_grad)
        sums_ref[2] += fold_rows(second_grad * normed)
        sums_ref[3] += fold_rows(second_grad)
        sums_ref[4] += fold_rows(middle_grad * branch)
        sums_ref[5] += fold_rows(middle_grad)

    @pl.when((slot == slots - 1) & (pair == pairs - 1))
    def _():
        reduction.run(6)
        copy = pltpu.make_async_copy(total_b, out_b, loads.at[0])
        copy.start()
        copy.wait()
        reduction.drain()
        gather.drain()


SMALL_ROWS = 128
AB_TICKS = {0: ((0, 0),), 1: ((0, 1),), 4: ((0, 2),), 6: ((0, 3),)}
AB_LATE = {0: ((1, 0), (0, 4)), 3: ((1, 1),), 7: ((0, 5),), 9: ((1, 2),), 12: ((1, 3),), 15: ((1, 4),)}
AB_LAST = ((0, 6), (1, 5), (1, 6))


def attention_backward(
    grid_ref, tok_ref, mg_ref, att_ref, q0_ref, k0_ref, v0_ref, p0_ref, q_ref, k_ref, v_ref, p1_ref, p2_ref,
    vec_ref, wa_ref, ff_sums_ref, grad_c,
    tg_ref, total_out, out_c, late_total,
    total, total_c, grads, attn_lows, kept, dq, dk, dv, lines, edges, sums, late, late_in, late_between,
    *rest, beyond,
):
    step = pl.program_id(0)
    half = pl.num_programs(0) // 2
    rows = PAIR * 208
    near = Neighbours()
    send, recv, late_send, late_recv, local = rest[8:]
    chains = (
        Reduce(near, beyond, grad_c, *rest[0:4], total_c, send, recv, 0),
        Reduce(near, beyond, grads, *rest[4:8], total, send, recv, 6 + beyond),
    )
    attn_scale, first_gain, first_shift = (vec_ref[i : i + 1, :] for i in range(3))
    head_of = lax.broadcasted_iota(jnp.int32, (1, 256), 1) // HD

    def advance(i):
        table = [(when % PAIR, when // PAIR, steps) for when, steps in AB_TICKS.items()]
        table += [(8 + when % 4, half + when // 4, steps) for when, steps in AB_LATE.items()]
        for part, when, steps in table:
            if part == i:
                @pl.when(step == when)
                def _():
                    for chain, at in steps:
                        chains[chain].run(at)

    def stack(group):
        return jnp.concatenate([jnp.where(head_of == h, group, jnp.zeros_like(group)) for h in range(4)], axis=0)

    def merge(mixed):
        out = mixed[0:208]
        for h in range(1, 4):
            out = jnp.where(head_of == h, mixed[h * 208 : (h + 1) * 208], out)
        return out

    def heads_back(q_group, k_group, v_group, g_group, prob_at, each):
        q_stack, g_stack = stack(q_group), stack(g_group)
        prob_grads = dot_nt(g_stack, v_group)
        lows = []
        for h in range(4):
            prob = prob_at(h).astype(F32)
            prob_grad = prob_grads[h * 208 : (h + 1) * 208]
            score_grad = prob * (prob_grad - jnp.sum(prob * prob_grad, axis=-1, keepdims=True))
            low = score_grad.astype(BF16)
            lows.append(low)
            each(h, score_grad, low)
        low_stack = jnp.concatenate(lows, axis=0)
        prob_stack = jnp.concatenate([prob_at(h) for h in range(4)], axis=0)
        return (
            merge(dot_nn(low_stack, k_group)).astype(BF16) * jnp.asarray(HD ** -0.5, BF16),
            dot_tn(low_stack, q_stack)[0:208].astype(BF16),
            dot_tn(prob_stack, g_stack)[0:208].astype(BF16),
        )

    @pl.when(step == 0)
    def _():
        greet(near, beyond)
        grads[...] = jnp.zeros_like(grads)
        sums[...] = jnp.zeros_like(sums)
        lines[...] = jnp.zeros_like(lines)
        edges[...] = jnp.zeros_like(edges)
        late[...] = jnp.zeros_like(late)

    normed, inv = norm_stats(tok_ref[...].reshape(rows, 768).astype(F32))
    middle_grad = mg_ref[...].reshape(rows, 768)

    @pl.when(step < half)
    def _():
        attn_low = (middle_grad * attn_scale).astype(BF16)
        attn_lows[step] = attn_low
        attended_grad = dot_nt(attn_low, wa_ref[3, 0:256, :]).astype(BF16)
        grads[576:768, :] += dot_tn(att_ref[...].reshape(rows, 256), attn_low)[0:192, :]
        flip = (
            lax.broadcasted_iota(jnp.int32, (208, 208), 0) + lax.broadcasted_iota(jnp.int32, (208, 208), 1) == 207
        ).astype(BF16)

        for i in range(PAIR):
            advance(i)
            image = step * PAIR + i
            p, s, limit, later, p_patch, s_patch = slot_masks(grid_ref[image, 0], grid_ref[image, 1], True)
            both = p_patch & s_patch
            kind = kind_of(grid_ref, image)

            def table_grad(h, score_grad, low):
                if h == 3:
                    return
                low_rest = (score_grad - low.astype(F32)).astype(BF16)
                turned = dot_nn(flip, low) + dot_nn(flip, low_rest)
                patches = jnp.where(both, turned, 0.0)
                edge = turned - patches
                for which, part in enumerate((jnp.where(later, patches, 0.0), jnp.where(later, 0.0, patches))):
                    wide = jnp.concatenate([part, jnp.zeros((208, 256), F32)], axis=1)
                    folded = jnp.sum(pltpu.roll(wide, 0, 1, stride=1, stride_axis=0), axis=0, keepdims=True)
                    row = which * 3 + h
                    for shape_at in range(len(GRIDS)):
                        lines[shape_at, row : row + 1, :] += jnp.where(kind == shape_at, folded, 0.0)
                class_query = jnp.where((p == 0) & s_patch, edge, 0.0)
                class_key = jnp.where(p_patch & (s == 0), edge, 0.0)
                for at, part in enumerate((class_query, class_key, edge - class_query - class_key)):
                    edges[at * 3 + h] += fold_rows(part)

            here = slice(i * 208, (i + 1) * 208)
            own = heads_back(
                q0_ref[i], k0_ref[i], v0_ref[i], attended_grad[here], lambda h: p0_ref[i, h], table_grad
            )
            for c, grad in enumerate(own):
                kept[c, step, here, :] = grad
            sums[0] += fold_rows(own[0].astype(F32))
            sums[1] += fold_rows(own[2].astype(F32))

        first_in = (normed * first_gain + first_shift).astype(BF16)
        for c in range(3):
            grads[c * 192 : (c + 1) * 192, :] += dot_tn(kept[c, step], first_in)[0:192, :]

    @pl.when(step == half)
    def _():
        grads[768 : 768 + SMALL_ROWS, :] = jnp.zeros((SMALL_ROWS, 768), F32)
        for shape_at in range(len(GRIDS)):
            grads[768 + shape_at * 8 : 776 + shape_at * 8, 0:DIAG] = lines[shape_at]
        for at in range(9):
            grads[832 + at : 833 + at, 0:256] = jnp.sum(edges[at], axis=0, keepdims=True)
        for at in range(2):
            grads[848 + at : 849 + at, 0:256] = jnp.sum(sums[at], axis=0, keepdims=True)
        for at in range(7):
            grads[856 + at : 857 + at, :] = jnp.sum(ff_sums_ref[at], axis=0, keepdims=True)

    @pl.when(step >= half)
    def _():
        at = step - half
        attended_grad = dot_nt(attn_lows[at], wa_ref[3, 256:768, :]).astype(BF16)
        for c, ref in enumerate((dq, dk, dv)):
            ref[:, 0:256] = kept[c, at]
        for i in range(PAIR):
            here = slice(i * 208, (i + 1) * 208)
            for group in (1, 2):
                advance(8 + i * 2 + group - 1)
                lanes = slice(group * 256, group * 256 + 256)
                probs = (p1_ref, p2_ref)[group - 1]
                parts = heads_back(
                    q_ref[i, :, lanes], k_ref[i, :, lanes], v_ref[i, :, lanes],
                    attended_grad[here, (group - 1) * 256 : group * 256], lambda h: probs[i, h], lambda *_: None,
                )
                for ref, part in zip((dq, dk, dv), parts):
                    ref[here, lanes] = part
        first_grad = dot_nn(dq[...], wa_ref[0]) + dot_nn(dk[...], wa_ref[1]) + dot_nn(dv[...], wa_ref[2])
        tg_ref[...] = (middle_grad + norm_back(first_grad, normed, inv, first_gain)).reshape(PAIR, 208, 768)
        late[0:8, :] += fold_rows(first_grad * normed)
        late[8:16, :] += fold_rows(first_grad)

    @pl.when(step == 2 * half - 1)
    def _():
        copies = [
            pltpu.make_async_remote_copy(
                src_ref=late, dst_ref=late_in.at[k - 1], send_sem=late_send.at[k - 1], recv_sem=late_recv.at[k - 1],
                device_id={"wide": near.base + (near.me + k) % SLICES}, device_id_type=MESH,
            )
            for k in range(1, SLICES)
        ]
        for copy in copies:
            copy.start()
        outs = [
            pltpu.make_async_copy(source, target, local.at[i])
            for i, (source, target) in enumerate(((total_c, out_c), (total, total_out)))
        ]
        for chain, at in AB_LAST:
            chains[chain].run(at)
        for copy in outs:
            copy.start()
        for copy in copies:
            copy.wait()
        summed = late[...]
        for k in range(SLICES - 1):
            summed = summed + late_in[k]
        for i in range(beyond):
            late_between[2 * i] = summed
            copy = pltpu.make_async_remote_copy(
                src_ref=late_between.at[2 * i], dst_ref=late_between.at[2 * i + 1],
                send_sem=late_send.at[SLICES - 1 + i], recv_sem=late_recv.at[SLICES - 1 + i],
                device_id={"wide": near.beyond(i)}, device_id_type=MESH,
            )
            copy.start()
            copy.wait()
            summed = late_between[2 * i] + late_between[2 * i + 1]
        late_total[...] = summed
        for copy in outs:
            copy.wait()
        for chain in chains:
            chain.drain()


def finish(tg_in, out_in, b_in, c_in, total_ref, tg_ref, out_ref, b_ref, c_ref, qkv_ref, proj_ref, table_ref):
    tg_ref[...] = tg_in[...]
    out_ref[...] = out_in[...]
    b_ref[...] = b_in[...]
    c_ref[...] = c_in[...]

    step, steps = pl.program_id(0), pl.num_programs(0)
    rows = qkv_ref.shape[0]
    qkv_ref[...] = total_ref[pl.ds(pl.multiple_of(step * rows, 8), rows), :]
    rows = proj_ref.shape[0]
    proj_ref[...] = total_ref[pl.ds(pl.multiple_of(576 + step * rows, 8), rows), :]

    @pl.when(step == 0)
    def _():
        table_ref[...] = jnp.zeros_like(table_ref)

    for shape_at in range(len(GRIDS)):
        @pl.when(step == shape_at)
        def _():
            for which, row, col, at, size in windows(shape_at):
                first = 768 + shape_at * 8 + which * 3
                table_ref[row, 0:3, col : col + size] += total_ref[first : first + 3, at : at + size]


def make_body(wide_size, narrow_size):
    def body(
        tokens, grid_shape, first_gain, first_shift, qkv_weight, query_bias, value_bias, rel_table, proj_weight,
        proj_bias, attn_scale, second_gain, second_shift, up_weight, up_bias, down_weight, down_bias, mlp_scale,
        cotangent,
    ):
        images, slots, width = tokens.shape
        heads, table_size = rel_table.shape
        local = heads * HD
        own_a = jnp.concatenate(
            [jnp.transpose(qkv_weight, (0, 2, 1)).reshape(3 * local, width), proj_weight], axis=0
        )
        table = rel_table.astype(F32)
        square = table[:, : SPAN * SPAN].reshape(heads, SPAN, SPAN)[:, ::-1, ::-1]
        square = jnp.pad(jnp.transpose(square, (1, 0, 2)), ((0, 0), (0, 8 - heads), (0, 128 - SPAN)))

        def small_for(k):
            def at(v, start):
                return jnp.pad(v.astype(F32).reshape(1, -1), ((0, 0), (start, width - start - v.size)))

            return jnp.concatenate(
                [
                    at(query_bias, k * local), at(value_bias, k * local), at(up_bias, 0),
                    at(table[:, SPAN * SPAN :].reshape(-1), 0), jnp.zeros((4, width), F32),
                ]
            )

        small = jnp.stack([small_for(k) for k in range(narrow_size)])
        all_heads = narrow_size * heads

        def row(v):
            return v.astype(F32).reshape(1, -1)

        smem = pl.BlockSpec(memory_space=pltpu.SMEM)
        anyspace = pl.BlockSpec(memory_space=pl.ANY)
        vmem = pl.BlockSpec(memory_space=pltpu.VMEM)

        def whole(*shape):
            return pl.BlockSpec(shape, lambda i, *_: (0,) * len(shape))

        def per_image(*shape):
            return pl.BlockSpec((1,) + shape, lambda i, *_: (i,) + (0,) * len(shape))

        def struct(*shape, dtype=F32):
            return jax.ShapeDtypeStruct(shape, dtype)

        params = pltpu.CompilerParams(vmem_limit_bytes=VMEM_LIMIT, dimension_semantics=("arbitrary",))
        copies = len(chunks_of(narrow_size)) * (narrow_size - 1 + 7)
        copies = len(chunks_of(narrow_size)) * (narrow_size - 1 + 7)
        me = lax.axis_index("wide") % SLICES
        slices = jnp.stack(
            [lax.dynamic_slice_in_dim(own_a.reshape(4, local, width), me * PART_ROWS, PART_ROWS, 1).reshape(-1, width)]
            + [lax.dynamic_slice_in_dim(w, me * SLICE_ROWS, SLICE_ROWS, 0) for w in (up_weight, down_weight)]
        ).astype(F32)
        probs, attended, branch, weights_a, small, queries, keys, values, gath_b, gath_c = pl.pallas_call(
            functools.partial(attention_forward, narrow=narrow_size),
            grid=(images,),
            in_specs=[smem, vmem] + [whole(1, width)] * 3 + [vmem] * 4,
            out_specs=[per_image(all_heads, slots, 256), per_image(slots, width), per_image(slots, width)]
            + [vmem, vmem] + [anyspace] * 5,
            scratch_shapes=[
                pltpu.VMEM((narrow_size - 1, width, width), F32),
                pltpu.VMEM((images, slots, width), BF16),
                pltpu.VMEM((images, slots, width), BF16),
                pltpu.VMEM((images, 256, width), BF16),
                pltpu.VMEM((images, 256, width), BF16),
                pltpu.VMEM((images, all_heads, slots, 256), BF16),
                pltpu.VMEM((16, 8, DIAG), F32),
                pltpu.VMEM((48, DIAG), F32),
                pltpu.VMEM((narrow_size - 1, 48, DIAG), F32),
                pltpu.VMEM((narrow_size, 8, width), F32),
                pltpu.SemaphoreType.DMA((copies,)),
                pltpu.SemaphoreType.DMA((copies,)),
                pltpu.SemaphoreType.DMA((2 * narrow_size - 2,)),
                pltpu.SemaphoreType.DMA((2 * narrow_size - 2,)),
                pltpu.SemaphoreType.DMA((3,)),
            ],
            out_shape=[
                struct(images, all_heads, slots, 256, dtype=BF16),
                struct(images, slots, width, dtype=BF16),
                struct(images, slots, width),
                struct(4, width, width, dtype=BF16),
                struct(narrow_size, 8, width),
                struct(images, slots, width, dtype=BF16),
                struct(images, 256, width, dtype=BF16),
                struct(images, 256, width, dtype=BF16),
                struct(narrow_size - 1, width, width),
                struct(narrow_size - 1, width, width),
            ],
            compiler_params=pltpu.CompilerParams(
                vmem_limit_bytes=VMEM_LIMIT, dimension_semantics=("arbitrary",), collective_id=0,
                has_side_effects=True,
            ),
            name="attention_forward",
        )(
            grid_shape, tokens, row(first_gain), row(first_shift), row(proj_bias), own_a, slices, square, small,
        )

        vec = jnp.concatenate([row(v) for v in (attn_scale, second_gain, second_shift, mlp_scale, down_bias)])
        beyond = (wide_size // SLICES).bit_length() - 1
        rows = PAIR * slots
        pairs = images // PAIR
        last = narrow_size - 1

        def remote_params(at):
            return pltpu.CompilerParams(
                vmem_limit_bytes=VMEM_LIMIT, collective_id=at, has_side_effects=True,
            )

        ends = pl.BlockSpec((PAIR, slots, width), lambda s, i: (jnp.where((s > 0) & (s < last), pairs - 1, i), 0, 0))
        outs = pl.BlockSpec((PAIR, slots, width), lambda s, i: (jnp.where(s < last, 0, i), 0, 0))
        layer_out, middle_grad, grad_b, grad_c, sums, _ = pl.pallas_call(
            functools.partial(feed_forward, narrow=narrow_size, beyond=beyond),
            grid=(narrow_size, pairs),
            in_specs=[smem] + [ends] * 3 + [vmem] * 5 + [anyspace] * 2,
            out_specs=[outs] * 2 + [anyspace, vmem, vmem, anyspace],
            input_output_aliases={10: 5},
            scratch_shapes=[
                pltpu.VMEM((width, width), F32),
                pltpu.VMEM((2, width, width), F32),
                pltpu.VMEM((2, width, width), BF16),
                pltpu.VMEM((2, width, width), BF16),
                pltpu.VMEM((pairs, rows, width), BF16),
                pltpu.VMEM((pairs, rows, width), BF16),
                pltpu.VMEM((pairs, rows, width), F32),
                pltpu.VMEM((pairs, rows, width), F32),
                pltpu.VMEM((width, width), F32),
            ]
            + Reduce.scratch(width, width, beyond)
            + [
                pltpu.SemaphoreType.DMA((2,)),
                pltpu.SemaphoreType.DMA((6 + beyond,)),
                pltpu.SemaphoreType.DMA((6 + beyond,)),
                pltpu.SemaphoreType.DMA((copies,)),
                pltpu.SemaphoreType.DMA((copies,)),
            ],
            out_shape=[
                struct(images, slots, width, dtype=BF16),
                struct(images, slots, width),
                struct(width, width),
                struct(width, width),
                struct(7, 8, width),
                struct(narrow_size - 1, width, width),
            ],
            compiler_params=remote_params(1),
            name="feed_forward",
        )(grid_shape, tokens, branch, cotangent, vec, small, up_weight, down_weight, slices, gath_b, gath_c)

        def first_pass(*shape):
            return pl.BlockSpec((PAIR,) + shape, lambda i: (jnp.minimum(i, pairs - 1),) + (0,) * len(shape))

        def second_pass(*shape, at=0):
            return pl.BlockSpec((PAIR,) + shape, lambda i: (jnp.maximum(i - pairs, 0), at) + (0,) * (len(shape) - 1))

        both_passes = pl.BlockSpec((PAIR, slots, width), lambda i: (i % pairs, 0, 0))
        total_rows = width + SMALL_ROWS
        vec = jnp.concatenate([row(v) for v in (attn_scale, first_gain, first_shift)])
        tokens_grad, total, grad_c, late = pl.pallas_call(
            functools.partial(attention_backward, beyond=beyond),
            grid=(2 * pairs,),
            in_specs=[smem, both_passes, both_passes]
            + [first_pass(slots, 256)] * 2
            + [first_pass(256, 256)] * 2
            + [first_pass(4, slots, 256)]
            + [second_pass(slots, width), second_pass(256, width), second_pass(256, width)]
            + [second_pass(4, slots, 256, at=1), second_pass(4, slots, 256, at=2)]
            + [vmem] * 4,
            out_specs=[second_pass(slots, width), anyspace, anyspace, vmem],
            scratch_shapes=[
                pltpu.VMEM((total_rows, width), F32),
                pltpu.VMEM((width, width), F32),
                pltpu.VMEM((total_rows, width), F32),
                pltpu.VMEM((pairs, rows, width), BF16),
                pltpu.VMEM((3, pairs, rows, 256), BF16),
                pltpu.VMEM((rows, width), BF16),
                pltpu.VMEM((rows, width), BF16),
                pltpu.VMEM((rows, width), BF16),
                pltpu.VMEM((len(GRIDS), 8, DIAG), F32),
                pltpu.VMEM((9, 8, 256), F32),
                pltpu.VMEM((2, 8, 256), F32),
                pltpu.VMEM((16, width), F32),
                pltpu.VMEM((SLICES - 1, 16, width), F32),
                pltpu.VMEM((2 * max(beyond, 1), 16, width), F32),
            ]
            + Reduce.scratch(width, width, beyond)
            + Reduce.scratch(total_rows, width, beyond)
            + [
                pltpu.SemaphoreType.DMA((2 * (6 + beyond),)),
                pltpu.SemaphoreType.DMA((2 * (6 + beyond),)),
                pltpu.SemaphoreType.DMA((SLICES - 1 + beyond,)),
                pltpu.SemaphoreType.DMA((SLICES - 1 + beyond,)),
                pltpu.SemaphoreType.DMA((2,)),
            ],
            out_shape=[
                struct(images, slots, width), struct(total_rows, width), struct(width, width), struct(16, width),
            ],
            compiler_params=remote_params(2),
            name="attention_backward",
        )(
            grid_shape, tokens, middle_grad, attended, queries, keys, values, probs, queries, keys, values, probs,
            probs, vec, weights_a, sums, grad_c,
        )

        parts = len(GRIDS)

        def image_block():
            return pl.BlockSpec((images // parts, slots, width), lambda i: (i, 0, 0))

        def row_block(total_rows=width):
            return pl.BlockSpec((total_rows // parts, width), lambda i: (i, 0))

        tokens_grad, layer_out, grad_b, grad_c, qkv_grad, proj_grad, square_grad = pl.pallas_call(
            finish,
            grid=(parts,),
            in_specs=[image_block(), image_block(), row_block(), row_block(), vmem],
            out_specs=[image_block(), image_block(), row_block(), row_block(), row_block(3 * local), row_block(local), vmem],
            out_shape=[
                struct(images, slots, width), struct(images, slots, width, dtype=BF16), struct(width, width),
                struct(width, width), struct(3 * local, width), struct(local, width), struct(SPAN, 8, 128),
            ],
            compiler_params=params,
            name="finish",
        )(tokens_grad, layer_out, grad_b, grad_c, total)
        qkv_grad = jnp.transpose(qkv_grad.reshape(3, local, width), (0, 2, 1))
        square_grad = jnp.transpose(square_grad[:, :heads, :SPAN], (1, 0, 2))[:, ::-1, ::-1]
        edges = jnp.sum(total[width + 64 : width + 73, :256], axis=1).reshape(3, heads).T
        table_grad = jnp.concatenate([square_grad.reshape(heads, SPAN * SPAN), edges], axis=1)
        more = total[width + 80 : width + 82, :local]
        sums = total[width + 88 : width + 95]
        late = jnp.sum(late.reshape(2, 8, width), axis=1)
        return (
            layer_out,
            tokens_grad,
            late[0],
            late[1],
            qkv_grad,
            more[0],
            more[1],
            table_grad,
            proj_grad,
            sums[5] * attn_scale.astype(F32),
            sums[4],
            sums[2],
            sums[3],
            grad_b,
            sums[6],
            grad_c,
            sums[1] * mlp_scale.astype(F32),
            sums[0],
        )

    return body


def solution(mesh):
    rows = P("wide", None, None)
    return jax.shard_map(
        make_body(mesh.shape["wide"], mesh.shape["narrow"]),
        mesh=mesh,
        in_specs=(
            rows, P("wide", None), P(), P(), P(None, None, "narrow"), P("narrow"), P("narrow"), P("narrow", None),
            P("narrow", None), P(), P(), P(), P(), P(None, "narrow"), P("narrow"), P("narrow", None), P(), P(), rows,
        ),
        out_specs=(
            rows, rows, P(), P(), P(None, None, "narrow"), P("narrow"), P("narrow"), P("narrow", None),
            P("narrow", None), P(), P(), P(), P(), P(None, "narrow"), P("narrow"), P("narrow", None), P(), P(),
        ),
        check_vma=False,
    )
```

```python
import functools

import jax
import jax.numpy as jnp
from jax import lax
from jax.experimental import pallas as pl
from jax.experimental.pallas import tpu as pltpu
from jax.sharding import PartitionSpec as P

HD = 64
MAXG = 24
SPAN = 2 * MAXG - 1
EPSILON = 1e-06
MASKED = -1e30
INV_ROOT_TWO = 0.7071067811865476
INV_ROOT_TWO_PI = 0.3989422804014327
GRIDS = ((14, 14), (10, 20), (20, 10), (8, 24), (24, 8), (12, 16), (16, 12), (13, 15))
DIAG = 512
F32 = jnp.float32
BF16 = jnp.bfloat16
VMEM_LIMIT = 60 * 1024 * 1024


def dot_nn(a, b):
    return lax.dot_general(a, b, (((1,), (0,)), ((), ())), preferred_element_type=F32)


def dot_nt(a, b):
    return lax.dot_general(a, b, (((1,), (1,)), ((), ())), preferred_element_type=F32)


def dot_tn(a, b):
    return lax.dot_general(a, b, (((0,), (0,)), ((), ())), preferred_element_type=F32)


def row_mean(v):
    return jnp.sum(v, axis=-1, keepdims=True) * (1.0 / v.shape[-1])


def norm_stats(v):
    centred = v - row_mean(v)
    inv = lax.rsqrt(row_mean(centred * centred) + EPSILON)
    return centred * inv, inv


def norm_back(incoming, normed, inv, gain):
    scaled = incoming * gain
    return inv * (scaled - row_mean(scaled) - normed * row_mean(scaled * normed))


def fold_rows(v):
    rows = v.shape[0]
    return jnp.sum(v.reshape(rows // 8, 8, v.shape[1]), axis=0)


def windows(shape_at):
    high, wide = GRIDS[shape_at]
    centre = MAXG - 1
    for m in range(-high, high):
        at = 207 + m * wide
        if m > -high:
            yield 0, centre + m, centre, at, wide
        if m < high - 1:
            yield 1, centre + 1 + m, centre + 1 - wide, at + 1, wide - 1


def kind_of(grid_ref, image):
    high, wide = grid_ref[image, 0], grid_ref[image, 1]
    kind = jnp.int32(0)
    for at, (grid_high, grid_wide) in enumerate(GRIDS):
        kind = jnp.where((high == grid_high) & (wide == grid_wide), at, kind)
    return kind


def slot_masks(high, wide, reverse):
    rows = lax.broadcasted_iota(jnp.int32, (208, 1), 0)
    p = 207 - rows if reverse else rows
    s = lax.broadcasted_iota(jnp.int32, (1, 256), 1)
    limit = high * wide
    wide_f = wide.astype(F32)

    def column(slot):
        patch = (slot - 1).astype(F32)
        return patch - wide_f * jnp.floor((patch + 0.5) / wide_f)

    later = column(s) >= column(p)
    p_patch = (p >= 1) & (p <= limit)
    s_patch = (s >= 1) & (s <= limit)
    return p, s, limit, later, p_patch, s_patch


MESH = pl.DeviceIdType.MESH
SLICES = 8
SLICE_ROWS = 96
PART_ROWS = 24


def chunks_of(narrow):
    all_shards = tuple(range(1, narrow))
    rows = [(group, at, 24, all_shards) for group in range(2) for at in (0, 24, 48, 72)]
    return tuple(rows) + tuple((2, 0, SLICE_ROWS, (k,)) for k in all_shards)


ROW_CHUNKS = 8


class Neighbours:
    def __init__(self):
        self.wide = lax.axis_index("wide")
        self.me = self.wide % SLICES
        self.base = self.wide - self.me
        self.core = core = self.me % 2
        x_bit, y_bit = (self.me // 2) % 2, self.me // 4
        over_x, over_y = self.me + 2 - 4 * x_bit, self.me + 4 - 8 * y_bit
        self.first = over_x * (1 - core) + over_y * core
        self.second = over_y * (1 - core) + over_x * core
        self.first_bit = x_bit * (1 - core) + y_bit * core
        self.second_bit = y_bit * (1 - core) + x_bit * core
        self.third = over_x + over_y - self.me
        self.twin = self.me + 1 - 2 * core

    def beyond(self, step):
        size = SLICES << step
        return self.wide + size - 2 * size * ((self.wide // size) % 2)


class Gather(Neighbours):
    def __init__(self, narrow, slices, buffers, send, recv, done=()):
        super().__init__()
        self.done = done
        self.narrow, self.slices, self.buffers, self.send, self.recv = narrow, slices, buffers, send, recv
        self.z = lax.axis_index("narrow")
        self.chunks = chunks_of(narrow)
        self.per_chunk = narrow - 1 + 7
        self.started = []

    def copy(self, chunk, phase, piece):
        group, at, rows, shards = self.chunks[chunk]
        buffer = self.buffers[group]

        def part(owner):
            return buffer.at[
                pl.ds(shards[0] - 1, len(shards)), pl.ds(pl.multiple_of(owner * SLICE_ROWS + at, 8), rows), :
            ]

        place = chunk * self.per_chunk
        if phase == 0:
            place += piece - 1
            source = self.slices.at[group, pl.ds(at, rows), :]
            target = buffer.at[piece - 1, pl.ds(pl.multiple_of(self.me * SLICE_ROWS + at, 8), rows), :]
            device = {"narrow": (self.z + self.narrow - piece) % self.narrow}
        else:
            owners = (self.me, self.first, self.second, self.third)
            place += self.narrow - 1 + (0, 1, 3)[phase - 1] + piece
            source = target = part(owners[piece])
            device = {"wide": self.base + (self.first, self.second, self.twin)[phase - 1]}
        return pltpu.make_async_remote_copy(
            src_ref=source, dst_ref=target, send_sem=self.send.at[place], recv_sem=self.recv.at[place],
            device_id=device, device_id_type=MESH,
        )

    def pieces(self, chunk, phase):
        return (self.chunks[chunk][3], range(1), range(2), range(4))[phase]

    def start(self, chunk, phase):
        self.started.append((chunk, phase))
        for piece in self.pieces(chunk, phase):
            self.copy(chunk, phase, piece).start()

    def arrive(self, chunk, phase):
        for piece in self.pieces(chunk, phase):
            self.copy(chunk, phase, piece).wait_recv()

    def run(self, steps):
        for chunk, phase in steps:
            if phase > 0 and (chunk, phase - 1) not in self.done:
                self.arrive(chunk, phase - 1)
            self.start(chunk, phase)

    def drain(self):
        for chunk, phase in self.started:
            for piece in self.pieces(chunk, phase):
                self.copy(chunk, phase, piece).wait_send()

    def barrier(self):
        sem = pltpu.get_barrier_semaphore()
        for k in range(1, self.narrow):
            pl.semaphore_signal(
                sem, inc=1, device_id={"narrow": (self.z + k) % self.narrow}, device_id_type=MESH
            )
        for other in (self.first, self.second, self.twin):
            pl.semaphore_signal(sem, inc=1, device_id={"wide": self.base + other}, device_id_type=MESH)
        pl.semaphore_wait(sem, self.narrow - 1 + 3)


def tick(t):
    steps = ((t, 1), (t + 2, 0), (t - 1, 2), (t - 2, 3))
    return tuple((chunk, phase) for chunk, phase in steps if 0 <= chunk < ROW_CHUNKS + 3 * (phase == 0))


LATE = {8: 7, 15: 8}
LAST = (9,)


def attention_forward(
    grid_ref, tok_ref, gain_ref, shift_ref, pb_ref, own_ref, slices, table_ref, small_ref,
    prob_ref, att_ref, branch_ref, wa_ref, small_out, q_out, k_out, v_out, gath_b, gath_c,
    stage, first_in, queries, k_pad, v_pad, bias, lined, diag, far, smalls, send, recv, extra_send, extra_recv, local,
    narrow,
):
    image = pl.program_id(0)
    images = pl.num_programs(0)
    gather = Gather(narrow, slices, (stage, gath_b, gath_c), send, recv)

    def extra(which, k):
        source = diag if which else small_ref.at[k]
        target = far.at[k - 1] if which else smalls.at[k]
        place = which * (narrow - 1) + k - 1
        return pltpu.make_async_remote_copy(
            src_ref=source, dst_ref=target, send_sem=extra_send.at[place], recv_sem=extra_recv.at[place],
            device_id={"narrow": (gather.z + narrow - k) % narrow}, device_id_type=MESH,
        )

    def keep(which):
        source, target = ((queries, q_out), (k_pad, k_out), (v_pad, v_out))[which]
        return pltpu.make_async_copy(source, target, local.at[which])

    @pl.when(image == 0)
    def _():
        def bias_of(slot, at, table):
            p, s, limit, later, p_patch, s_patch = slot_masks(grid_ref[at, 0], grid_ref[at, 1], False)
            both = p_patch & s_patch
            open_key = s <= limit
            for h in range(3):
                row = h * 16 + kind_of(grid_ref, at) * 2
                toep = [
                    pltpu.roll(
                        jnp.broadcast_to(table(row + which), (208, DIAG)), DIAG - 207, 1, stride=1, stride_axis=0
                    )[:, :256]
                    for which in range(2)
                ]
                c0, c1, c2 = (smalls[slot, 3:4, h * 3 + c : h * 3 + c + 1] for c in range(3))
                outer = jnp.where((p == 0) & s_patch, c0, jnp.where(p_patch & (s == 0), c1, c2))
                value = jnp.where(both, jnp.where(later, toep[0], toep[1]), outer)
                bias[at, slot * 3 + h] = jnp.where(open_key, value, MASKED).astype(BF16)

        def far_bias(slot):
            @pl.loop(0, 8)
            def _(at):
                bias_of(slot, at, lambda row: far[slot - 1, pl.ds(row, 1), :])

        def weights_of(part):
            gather.arrive(part, 3)
            for slot in range(narrow - 1):
                for pair in range(4):
                    rows = [
                        stage[slot, pl.ds((2 * pair + i) * SLICE_ROWS + part * PART_ROWS, PART_ROWS), :]
                        for i in range(2)
                    ]
                    at = (slot + 1) * 192 + pair * 2 * PART_ROWS
                    wa_ref[part, at : at + 2 * PART_ROWS, :] = jnp.concatenate(rows, axis=0).astype(BF16)

        def project(part, target, finish):
            @pl.loop(0, 8)
            def _(at):
                target[at, 0:208, :] = finish(dot_nt(first_in[at], wa_ref[part])).astype(BF16)

            keep(part).start()

        lined[...] = jnp.zeros_like(lined)
        for shape_at in range(len(GRIDS)):
            for which, row, col, at, size in windows(shape_at):
                lined[shape_at * 2 + which, :, at : at + size] = table_ref[row, :, col : col + size]
        for h in range(3):
            for r in range(16):
                diag[h * 16 + r : h * 16 + r + 1, :] = lined[r, h : h + 1, :]
        gather.barrier()
        smalls[0] = small_ref[0]
        gather.run(((0, 0), (1, 0)))
        for k in range(1, narrow):
            extra(0, k).start()
            extra(1, k).start()
        k_pad[:, 208:256, :] = jnp.zeros((8, 48, 768), BF16)
        v_pad[:, 208:256, :] = jnp.zeros((8, 48, 768), BF16)
        for part in range(4):
            wa_ref[part, 0:192, :] = own_ref[part * 192 : (part + 1) * 192, :]

        @pl.loop(0, 8)
        def _(at):
            normed, _ = norm_stats(tok_ref[at].astype(F32))
            first_in[at] = (normed * gain_ref[...] + shift_ref[...]).astype(BF16)
            bias_of(0, at, lambda row: diag[pl.ds(row, 1), :])

        gather.run(tick(0))
        gather.run(tick(1))
        for k in range(1, narrow):
            extra(0, k).wait_recv()
            extra(1, k).wait_recv()
        far_bias(1)
        gather.run(tick(2))
        for k in range(2, narrow):
            far_bias(k)
        gather.run(tick(3))
        q_bias = sum(smalls[k, 0:1, :] for k in range(narrow))
        v_bias = sum(smalls[k, 1:2, :] for k in range(narrow))
        small_out[...] = smalls[...]
        weights_of(0)
        project(0, queries, lambda v: (v + q_bias) * (HD ** -0.5))
        gather.run(tick(4))
        weights_of(1)
        project(1, k_pad, lambda v: v)
        gather.run(tick(5))
        weights_of(2)
        project(2, v_pad, lambda v: v + v_bias)
        gather.run(tick(6))
        weights_of(3)

    head_of = lax.broadcasted_iota(jnp.int32, (1, 256), 1) // HD

    @pl.loop(0, 3)
    def _(group):
        for when, t in LATE.items():
            @pl.when(image * 3 + group == when)
            def _():
                gather.run(tick(t))

        lanes = pl.ds(pl.multiple_of(group * 256, 256), 256)
        q_group = queries[image, :, lanes]
        k_group = k_pad[image, :, lanes]
        v_group = v_pad[image, :, lanes]
        stacked = jnp.concatenate(
            [jnp.where(head_of == h, q_group, jnp.zeros_like(q_group)) for h in range(4)], axis=0
        )
        raw = dot_nt(stacked, k_group)
        probs = []
        for h in range(4):
            head = group * 4 + h
            scores = raw[h * 208 : (h + 1) * 208, :] + bias[image, head].astype(F32)
            top = jnp.max(scores, axis=-1, keepdims=True)
            raised = jnp.exp(scores - top)
            prob = (raised * (1.0 / jnp.sum(raised, axis=-1, keepdims=True))).astype(BF16)
            prob_ref[0, head] = prob
            probs.append(prob)
        mixed = dot_nn(jnp.concatenate(probs, axis=0), v_group)
        out = mixed[0:208]
        for h in range(1, 4):
            out = jnp.where(head_of == h, mixed[h * 208 : (h + 1) * 208], out)
        att_ref[0, :, lanes] = out.astype(BF16)

    branch_ref[0] = dot_nn(att_ref[0], wa_ref[3]) + pb_ref[...]

    @pl.when(image == images - 1)
    def _():
        for t in LAST:
            gather.run(tick(t))
        for chunk in range(4, ROW_CHUNKS):
            gather.arrive(chunk, 3)
        for chunk in range(ROW_CHUNKS, len(gather.chunks)):
            gather.arrive(chunk, 0)
        gather.drain()
        for k in range(1, narrow):
            extra(0, k).wait_send()
            extra(1, k).wait_send()
        for which in range(3):
            keep(which).wait()


class Reduce:
    STEPS = 7

    def __init__(self, near, beyond, source, half, quarter, eighth, between, total, send, recv, first_sem):
        self.near, self.beyond, self.source, self.total = near, beyond, source, total
        self.half, self.quarter, self.eighth, self.between = half, quarter, eighth, between
        self.send, self.recv, self.first_sem = send, recv, first_sem
        self.rows = eighth.shape[0]

    @staticmethod
    def scratch(rows, width, beyond):
        shapes = [(rows // 2, width), (rows // 4, width), (rows // 8, width), (2 * max(beyond, 1), rows // 8, width)]
        return [pltpu.VMEM(shape, F32) for shape in shapes]

    def span(self, ref, start, count):
        return ref.at[pl.ds(pl.multiple_of(start, 8), count), :]

    def value(self, ref, start, count):
        return ref[pl.ds(pl.multiple_of(start, 8), count), :]

    def copy(self, step):
        near, rows = self.near, self.rows
        half_at = near.core * 4 * rows
        quarter_at = half_at + near.first_bit * 2 * rows
        own_at = quarter_at + near.second_bit * rows
        if step == 0:
            source, target, to = self.span(self.source, (1 - near.core) * 4 * rows, 4 * rows), self.half, near.twin
        elif step == 1:
            source, target, to = (
                self.span(self.half, (1 - near.first_bit) * 2 * rows, 2 * rows), self.quarter, near.first
            )
        elif step == 2:
            source, target, to = self.span(self.quarter, (1 - near.second_bit) * rows, rows), self.eighth, near.second
        else:
            at, count, to = (
                (own_at, rows, near.second), (quarter_at, 2 * rows, near.first), (half_at, 4 * rows, near.twin)
            )[step - 3]
            source = target = self.span(self.total, at, count)
        return self.remote(source, target, step, near.base + to)

    def remote(self, source, target, place, to):
        place += self.first_sem
        return pltpu.make_async_remote_copy(
            src_ref=source, dst_ref=target, send_sem=self.send.at[place], recv_sem=self.recv.at[place],
            device_id={"wide": to}, device_id_type=MESH,
        )

    def run(self, step):
        near, rows = self.near, self.rows
        if step > 0:
            self.copy(step - 1).wait_recv()
        if step == 1:
            self.half[...] += self.value(self.source, near.core * 4 * rows, 4 * rows)
        if step == 2:
            self.quarter[...] += self.value(self.half, near.first_bit * 2 * rows, 2 * rows)
        if step == 3:
            summed = self.eighth[...] + self.value(self.quarter, near.second_bit * rows, rows)
            for i in range(self.beyond):
                self.between[2 * i] = summed
                copy = self.remote(self.between.at[2 * i], self.between.at[2 * i + 1], 6 + i, near.beyond(i))
                copy.start()
                copy.wait()
                summed = self.between[2 * i] + self.between[2 * i + 1]
            own_at = (near.core * 4 + near.first_bit * 2 + near.second_bit) * rows
            self.total[pl.ds(pl.multiple_of(own_at, 8), rows), :] = summed
        if step < 6:
            self.copy(step).start()

    def drain(self):
        for step in range(6):
            self.copy(step).wait_send()


def greet(near, beyond, narrow=1):
    sem = pltpu.get_barrier_semaphore()
    for k in range(1, narrow):
        pl.semaphore_signal(sem, inc=1, device_id={"narrow": (near.z + k) % narrow}, device_id_type=MESH)
    for k in range(1, SLICES):
        other = near.base + (near.me + k) % SLICES
        pl.semaphore_signal(sem, inc=1, device_id={"wide": other}, device_id_type=MESH)
    for i in range(beyond):
        pl.semaphore_signal(sem, inc=1, device_id={"wide": near.beyond(i)}, device_id_type=MESH)
    pl.semaphore_wait(sem, narrow - 1 + SLICES - 1 + beyond)


PAIR = 2
FF_GATHER = {0: ((8, 1),), 1: ((8, 2), (9, 1)), 2: ((10, 1),), 3: ((8, 3), (9, 2)), 5: ((9, 3), (10, 2)), 8: ((10, 3),)}

FF_SUM = {4: 0, 7: 1, 9: 2, 11: 3, 13: 4, 15: 5}


def feed_forward(
    grid_ref, tok_ref, branch_ref, cot_ref, vec_ref, small_ref, ownb_ref, ownc_ref, slices, gath_b, _,
    out_ref, mg_ref, out_b, grad_c, sums_ref, gath_c,
    total_b, stage, wb, wc, second_ins, branch_lows, mlp_acc, second_acc, grad_b, half, quarter, eighth, between,
    loads, send, recv, gather_send, gather_recv, narrow, beyond,
):
    slot, pair = pl.program_id(0), pl.program_id(1)
    slots, pairs = pl.num_programs(0), pl.num_programs(1)
    rows = PAIR * 208
    gather = Gather(narrow, slices, (None, None, gath_c), gather_send, gather_recv, done=tuple((ROW_CHUNKS + k, 0) for k in range(3)))
    reduction = Reduce(gather, beyond, grad_b, half, quarter, eighth, between, total_b, send, recv, 0)

    def load(which, at):
        return pltpu.make_async_copy((gath_b, gath_c)[which].at[at], stage.at[which], loads.at[which])

    @pl.when((slot == 0) & (pair == 0))
    def _():
        greet(gather, beyond, narrow)
        wb[0] = ownb_ref[...]
        wc[0] = ownc_ref[...]
        grad_b[...] = jnp.zeros_like(grad_b)
        grad_c[...] = jnp.zeros_like(grad_c)
        sums_ref[...] = jnp.zeros_like(sums_ref)

    for when, steps in FF_GATHER.items():
        @pl.when(slot * pairs + pair == when)
        def _():
            gather.run(steps)

    for when, step in FF_SUM.items():
        @pl.when(slot * pairs + pair == when)
        def _():
            reduction.run(step)

    for k in range(1, narrow):
        @pl.when((pair == pairs - 1) & (slot == k - 1))
        def _():
            load(0, k - 1).start()
            if k > 1:
                gather.arrive(ROW_CHUNKS + k - 1, 3)
                load(1, k - 1).start()

    attn_scale, second_gain, second_shift, mlp_scale, down_bias = (vec_ref[i : i + 1, :] for i in range(5))

    def residual():
        branch = branch_ref[...].reshape(rows, 768)
        return branch, tok_ref[...].reshape(rows, 768).astype(F32) + attn_scale * branch

    def masked_cotangent():
        at = lax.broadcasted_iota(jnp.int32, (rows, 1), 0)
        limit = jnp.zeros((rows, 1), jnp.int32)
        for i in range(PAIR):
            image = pair * PAIR + i
            inside = (at >= i * 208) & (at < (i + 1) * 208)
            limit = jnp.where(inside, grid_ref[image, 0] * grid_ref[image, 1] + i * 208, limit)
        return jnp.where(at <= limit, cot_ref[...].reshape(rows, 768).astype(F32), 0.0)

    @pl.when(slot == 0)
    def _():
        _, middle = residual()
        normed, _ = norm_stats(middle)
        second_ins[pair] = (normed * second_gain + second_shift).astype(BF16)
        branch_lows[pair] = (masked_cotangent() * mlp_scale).astype(BF16)
        mlp_acc[pair] = jnp.zeros((rows, 768), F32)
        second_acc[pair] = jnp.zeros((rows, 768), F32)

    second_in, branch_low = second_ins[pair], branch_lows[pair]
    up, down = wb[slot % 2], wc[slot % 2]
    up_pre = dot_nn(second_in, up) + small_ref[slot, 2:3, :]
    cdf = 0.5 * (1.0 + lax.erf(up_pre * INV_ROOT_TWO))
    hidden = (up_pre * cdf).astype(BF16)
    slope = cdf + up_pre * jnp.exp(-0.5 * up_pre * up_pre) * INV_ROOT_TWO_PI
    mlp_acc[pair] += dot_nn(hidden, down)
    pre_low = (dot_nt(branch_low, down) * slope).astype(BF16)
    second_acc[pair] += dot_nt(pre_low, up)

    @pl.when(slot == 0)
    def _():
        grad_c[...] += dot_tn(hidden, branch_low)
        grad_b[...] += dot_tn(second_in, pre_low)
        sums_ref[6] += fold_rows(pre_low.astype(F32))

    @pl.when((pair == pairs - 1) & (slot == 0))
    def _():
        gather.arrive(ROW_CHUNKS, 3)
        load(1, 0).start()

    @pl.when((pair == pairs - 1) & (slot < slots - 1))
    def _():
        for which, weights in enumerate((wb, wc)):
            load(which, slot).wait()
            weights[(slot + 1) % 2] = stage[which].astype(BF16)

    @pl.when(slot == slots - 1)
    def _():
        branch, middle = residual()
        normed, inv = norm_stats(middle)
        out_grad = masked_cotangent()
        mlp_branch = mlp_acc[pair] + down_bias
        out_ref[...] = (middle + mlp_scale * mlp_branch).astype(BF16).reshape(PAIR, 208, 768)
        second_grad = second_acc[pair]
        middle_grad = out_grad + norm_back(second_grad, normed, inv, second_gain)
        mg_ref[...] = middle_grad.reshape(PAIR, 208, 768)
        sums_ref[0] += fold_rows(out_grad * mlp_branch)
        sums_ref[1] += fold_rows(out_grad)
        sums_ref[2] += fold_rows(second_grad * normed)
        sums_ref[3] += fold_rows(second_grad)
        sums_ref[4] += fold_rows(middle_grad * branch)
        sums_ref[5] += fold_rows(middle_grad)

    @pl.when((slot == slots - 1) & (pair == pairs - 1))
    def _():
        reduction.run(6)
        copy = pltpu.make_async_copy(total_b, out_b, loads.at[0])
        copy.start()
        copy.wait()
        reduction.drain()
        gather.drain()


SMALL_ROWS = 128
AB_TICKS = {0: ((0, 0),), 1: ((0, 1),), 4: ((0, 2),), 6: ((0, 3),)}
AB_LATE = {0: ((1, 0), (0, 4)), 3: ((1, 1),), 7: ((0, 5),), 9: ((1, 2),), 12: ((1, 3),), 15: ((1, 4),)}
AB_LAST = ((1, 5), (0, 6), (1, 6))


def attention_backward(
    grid_ref, tok_ref, mg_ref, att_ref, q0_ref, k0_ref, v0_ref, p0_ref, q_ref, k_ref, v_ref, p1_ref, p2_ref,
    vec_ref, wa_ref, ff_sums_ref, grad_c,
    tg_ref, total_out, out_c, late_total,
    total, total_c, grads, attn_lows, kept, dq, dk, dv, lines, edges, sums, late, late_in, late_between,
    *rest, beyond,
):
    step = pl.program_id(0)
    half = pl.num_programs(0) // 2
    rows = PAIR * 208
    near = Neighbours()
    send, recv, late_send, late_recv, local = rest[8:]
    chains = (
        Reduce(near, beyond, grad_c, *rest[0:4], total_c, send, recv, 0),
        Reduce(near, beyond, grads, *rest[4:8], total, send, recv, 6 + beyond),
    )
    attn_scale, first_gain, first_shift = (vec_ref[i : i + 1, :] for i in range(3))
    head_of = lax.broadcasted_iota(jnp.int32, (1, 256), 1) // HD

    def advance(i):
        table = [(when % PAIR, when // PAIR, steps) for when, steps in AB_TICKS.items()]
        table += [(8 + when % 4, half + when // 4, steps) for when, steps in AB_LATE.items()]
        for part, when, steps in table:
            if part == i:
                @pl.when(step == when)
                def _():
                    for chain, at in steps:
                        chains[chain].run(at)

    def stack(group):
        return jnp.concatenate([jnp.where(head_of == h, group, jnp.zeros_like(group)) for h in range(4)], axis=0)

    def merge(mixed):
        out = mixed[0:208]
        for h in range(1, 4):
            out = jnp.where(head_of == h, mixed[h * 208 : (h + 1) * 208], out)
        return out

    def heads_back(q_group, k_group, v_group, g_group, prob_at, each):
        q_stack, g_stack = stack(q_group), stack(g_group)
        prob_grads = dot_nt(g_stack, v_group)
        lows = []
        for h in range(4):
            prob = prob_at(h).astype(F32)
            prob_grad = prob_grads[h * 208 : (h + 1) * 208]
            score_grad = prob * (prob_grad - jnp.sum(prob * prob_grad, axis=-1, keepdims=True))
            low = score_grad.astype(BF16)
            lows.append(low)
            each(h, score_grad, low)
        low_stack = jnp.concatenate(lows, axis=0)
        prob_stack = jnp.concatenate([prob_at(h) for h in range(4)], axis=0)
        return (
            merge(dot_nn(low_stack, k_group)).astype(BF16) * jnp.asarray(HD ** -0.5, BF16),
            dot_tn(low_stack, q_stack)[0:208].astype(BF16),
            dot_tn(prob_stack, g_stack)[0:208].astype(BF16),
        )

    @pl.when(step == 0)
    def _():
        greet(near, beyond)
        grads[...] = jnp.zeros_like(grads)
        sums[...] = jnp.zeros_like(sums)
        lines[...] = jnp.zeros_like(lines)
        edges[...] = jnp.zeros_like(edges)
        late[...] = jnp.zeros_like(late)

    normed, inv = norm_stats(tok_ref[...].reshape(rows, 768).astype(F32))
    middle_grad = mg_ref[...].reshape(rows, 768)

    @pl.when(step < half)
    def _():
        attn_low = (middle_grad * attn_scale).astype(BF16)
        attn_lows[step] = attn_low
        attended_grad = dot_nt(attn_low, wa_ref[3, 0:256, :]).astype(BF16)
        grads[576:768, :] += dot_tn(att_ref[...].reshape(rows, 256), attn_low)[0:192, :]
        flip = (
            lax.broadcasted_iota(jnp.int32, (208, 208), 0) + lax.broadcasted_iota(jnp.int32, (208, 208), 1) == 207
        ).astype(BF16)

        for i in range(PAIR):
            advance(i)
            image = step * PAIR + i
            p, s, limit, later, p_patch, s_patch = slot_masks(grid_ref[image, 0], grid_ref[image, 1], True)
            both = p_patch & s_patch
            kind = kind_of(grid_ref, image)

            def table_grad(h, score_grad, low):
                if h == 3:
                    return
                low_rest = (score_grad - low.astype(F32)).astype(BF16)
                turned = dot_nn(flip, low) + dot_nn(flip, low_rest)
                patches = jnp.where(both, turned, 0.0)
                edge = turned - patches
                for which, part in enumerate((jnp.where(later, patches, 0.0), jnp.where(later, 0.0, patches))):
                    wide = jnp.concatenate([part, jnp.zeros((208, 256), F32)], axis=1)
                    folded = jnp.sum(pltpu.roll(wide, 0, 1, stride=1, stride_axis=0), axis=0, keepdims=True)
                    row = which * 3 + h
                    for shape_at in range(len(GRIDS)):
                        lines[shape_at, row : row + 1, :] += jnp.where(kind == shape_at, folded, 0.0)
                class_query = jnp.where((p == 0) & s_patch, edge, 0.0)
                class_key = jnp.where(p_patch & (s == 0), edge, 0.0)
                for at, part in enumerate((class_query, class_key, edge - class_query - class_key)):
                    edges[at * 3 + h] += fold_rows(part)

            here = slice(i * 208, (i + 1) * 208)
            own = heads_back(
                q0_ref[i], k0_ref[i], v0_ref[i], attended_grad[here], lambda h: p0_ref[i, h], table_grad
            )
            for c, grad in enumerate(own):
                kept[c, step, here, :] = grad
            sums[0] += fold_rows(own[0].astype(F32))
            sums[1] += fold_rows(own[2].astype(F32))

        first_in = (normed * first_gain + first_shift).astype(BF16)
        for c in range(3):
            grads[c * 192 : (c + 1) * 192, :] += dot_tn(kept[c, step], first_in)[0:192, :]

    @pl.when(step == half)
    def _():
        grads[768 : 768 + SMALL_ROWS, :] = jnp.zeros((SMALL_ROWS, 768), F32)
        for shape_at in range(len(GRIDS)):
            grads[768 + shape_at * 8 : 776 + shape_at * 8, 0:DIAG] = lines[shape_at]
        for at in range(9):
            grads[832 + at : 833 + at, 0:256] = jnp.sum(edges[at], axis=0, keepdims=True)
        for at in range(2):
            grads[848 + at : 849 + at, 0:256] = jnp.sum(sums[at], axis=0, keepdims=True)
        for at in range(7):
            grads[856 + at : 857 + at, :] = jnp.sum(ff_sums_ref[at], axis=0, keepdims=True)

    @pl.when(step >= half)
    def _():
        at = step - half
        attended_grad = dot_nt(attn_lows[at], wa_ref[3, 256:768, :]).astype(BF16)
        for c, ref in enumerate((dq, dk, dv)):
            ref[:, 0:256] = kept[c, at]
        for i in range(PAIR):
            here = slice(i * 208, (i + 1) * 208)
            for group in (1, 2):
                advance(8 + i * 2 + group - 1)
                lanes = slice(group * 256, group * 256 + 256)
                probs = (p1_ref, p2_ref)[group - 1]
                parts = heads_back(
                    q_ref[i, :, lanes], k_ref[i, :, lanes], v_ref[i, :, lanes],
                    attended_grad[here, (group - 1) * 256 : group * 256], lambda h: probs[i, h], lambda *_: None,
                )
                for ref, part in zip((dq, dk, dv), parts):
                    ref[here, lanes] = part
        first_grad = dot_nn(dq[...], wa_ref[0]) + dot_nn(dk[...], wa_ref[1]) + dot_nn(dv[...], wa_ref[2])
        tg_ref[...] = (middle_grad + norm_back(first_grad, normed, inv, first_gain)).reshape(PAIR, 208, 768)
        late[0:8, :] += fold_rows(first_grad * normed)
        late[8:16, :] += fold_rows(first_grad)

    @pl.when(step == 2 * half - 1)
    def _():
        copies = [
            pltpu.make_async_remote_copy(
                src_ref=late, dst_ref=late_in.at[k - 1], send_sem=late_send.at[k - 1], recv_sem=late_recv.at[k - 1],
                device_id={"wide": near.base + (near.me + k) % SLICES}, device_id_type=MESH,
            )
            for k in range(1, SLICES)
        ]
        for copy in copies:
            copy.start()
        outs = [
            pltpu.make_async_copy(source, target, local.at[i])
            for i, (source, target) in enumerate(((total_c, out_c), (total, total_out)))
        ]
        for chain, at in AB_LAST:
            chains[chain].run(at)
        for copy in outs:
            copy.start()
        for copy in copies:
            copy.wait()
        summed = late[...]
        for k in range(SLICES - 1):
            summed = summed + late_in[k]
        for i in range(beyond):
            late_between[2 * i] = summed
            copy = pltpu.make_async_remote_copy(
                src_ref=late_between.at[2 * i], dst_ref=late_between.at[2 * i + 1],
                send_sem=late_send.at[SLICES - 1 + i], recv_sem=late_recv.at[SLICES - 1 + i],
                device_id={"wide": near.beyond(i)}, device_id_type=MESH,
            )
            copy.start()
            copy.wait()
            summed = late_between[2 * i] + late_between[2 * i + 1]
        late_total[...] = summed
        for copy in outs:
            copy.wait()
        for chain in chains:
            chain.drain()


def finish(tg_in, out_in, b_in, c_in, qkv_in, proj_in, lines_ref, tg_ref, out_ref, b_ref, c_ref, qkv_ref, proj_ref, table_ref):
    tg_ref[...] = tg_in[...]
    out_ref[...] = out_in[...]
    b_ref[...] = b_in[...]
    c_ref[...] = c_in[...]

    step = pl.program_id(0)
    qkv_ref[...] = qkv_in[...]
    proj_ref[...] = proj_in[...]

    @pl.when(step == 0)
    def _():
        table_ref[...] = jnp.zeros_like(table_ref)

    for shape_at in range(len(GRIDS)):
        @pl.when(step == shape_at)
        def _():
            for which, row, col, at, size in windows(shape_at):
                first = shape_at * 8 + which * 3
                table_ref[row, 0:3, col : col + size] += lines_ref[first : first + 3, at : at + size]


def make_body(wide_size, narrow_size):
    def body(
        tokens, grid_shape, first_gain, first_shift, qkv_weight, query_bias, value_bias, rel_table, proj_weight,
        proj_bias, attn_scale, second_gain, second_shift, up_weight, up_bias, down_weight, down_bias, mlp_scale,
        cotangent,
    ):
        images, slots, width = tokens.shape
        heads, table_size = rel_table.shape
        local = heads * HD
        own_a = jnp.concatenate(
            [jnp.transpose(qkv_weight, (0, 2, 1)).reshape(3 * local, width), proj_weight], axis=0
        )
        table = rel_table.astype(F32)
        square = table[:, : SPAN * SPAN].reshape(heads, SPAN, SPAN)[:, ::-1, ::-1]
        square = jnp.pad(jnp.transpose(square, (1, 0, 2)), ((0, 0), (0, 8 - heads), (0, 128 - SPAN)))

        def small_for(k):
            def at(v, start):
                return jnp.pad(v.astype(F32).reshape(1, -1), ((0, 0), (start, width - start - v.size)))

            return jnp.concatenate(
                [
                    at(query_bias, k * local), at(value_bias, k * local), at(up_bias, 0),
                    at(table[:, SPAN * SPAN :].reshape(-1), 0), jnp.zeros((4, width), F32),
                ]
            )

        small = jnp.stack([small_for(k) for k in range(narrow_size)])
        all_heads = narrow_size * heads

        def row(v):
            return v.astype(F32).reshape(1, -1)

        smem = pl.BlockSpec(memory_space=pltpu.SMEM)
        anyspace = pl.BlockSpec(memory_space=pl.ANY)
        vmem = pl.BlockSpec(memory_space=pltpu.VMEM)

        def whole(*shape):
            return pl.BlockSpec(shape, lambda i, *_: (0,) * len(shape))

        def per_image(*shape):
            return pl.BlockSpec((1,) + shape, lambda i, *_: (i,) + (0,) * len(shape))

        def struct(*shape, dtype=F32):
            return jax.ShapeDtypeStruct(shape, dtype)

        params = pltpu.CompilerParams(vmem_limit_bytes=VMEM_LIMIT, dimension_semantics=("arbitrary",))
        copies = len(chunks_of(narrow_size)) * (narrow_size - 1 + 7)
        copies = len(chunks_of(narrow_size)) * (narrow_size - 1 + 7)
        me = lax.axis_index("wide") % SLICES
        slices = jnp.stack(
            [lax.dynamic_slice_in_dim(own_a.reshape(4, local, width), me * PART_ROWS, PART_ROWS, 1).reshape(-1, width)]
            + [lax.dynamic_slice_in_dim(w, me * SLICE_ROWS, SLICE_ROWS, 0) for w in (up_weight, down_weight)]
        ).astype(F32)
        probs, attended, branch, weights_a, small, queries, keys, values, gath_b, gath_c = pl.pallas_call(
            functools.partial(attention_forward, narrow=narrow_size),
            grid=(images,),
            in_specs=[smem, vmem] + [whole(1, width)] * 3 + [vmem] * 4,
            out_specs=[per_image(all_heads, slots, 256), per_image(slots, width), per_image(slots, width)]
            + [vmem, vmem] + [anyspace] * 5,
            scratch_shapes=[
                pltpu.VMEM((narrow_size - 1, width, width), F32),
                pltpu.VMEM((images, slots, width), BF16),
                pltpu.VMEM((images, slots, width), BF16),
                pltpu.VMEM((images, 256, width), BF16),
                pltpu.VMEM((images, 256, width), BF16),
                pltpu.VMEM((images, all_heads, slots, 256), BF16),
                pltpu.VMEM((16, 8, DIAG), F32),
                pltpu.VMEM((48, DIAG), F32),
                pltpu.VMEM((narrow_size - 1, 48, DIAG), F32),
                pltpu.VMEM((narrow_size, 8, width), F32),
                pltpu.SemaphoreType.DMA((copies,)),
                pltpu.SemaphoreType.DMA((copies,)),
                pltpu.SemaphoreType.DMA((2 * narrow_size - 2,)),
                pltpu.SemaphoreType.DMA((2 * narrow_size - 2,)),
                pltpu.SemaphoreType.DMA((3,)),
            ],
            out_shape=[
                struct(images, all_heads, slots, 256, dtype=BF16),
                struct(images, slots, width, dtype=BF16),
                struct(images, slots, width),
                struct(4, width, width, dtype=BF16),
                struct(narrow_size, 8, width),
                struct(images, slots, width, dtype=BF16),
                struct(images, 256, width, dtype=BF16),
                struct(images, 256, width, dtype=BF16),
                struct(narrow_size - 1, width, width),
                struct(narrow_size - 1, width, width),
            ],
            compiler_params=pltpu.CompilerParams(
                vmem_limit_bytes=VMEM_LIMIT, dimension_semantics=("arbitrary",), collective_id=0,
                has_side_effects=True,
            ),
            name="attention_forward",
        )(
            grid_shape, tokens, row(first_gain), row(first_shift), row(proj_bias), own_a, slices, square, small,
        )

        vec = jnp.concatenate([row(v) for v in (attn_scale, second_gain, second_shift, mlp_scale, down_bias)])
        beyond = (wide_size // SLICES).bit_length() - 1
        rows = PAIR * slots
        pairs = images // PAIR
        last = narrow_size - 1

        def remote_params(at):
            return pltpu.CompilerParams(
                vmem_limit_bytes=VMEM_LIMIT, collective_id=at, has_side_effects=True,
            )

        ends = pl.BlockSpec((PAIR, slots, width), lambda s, i: (jnp.where((s > 0) & (s < last), pairs - 1, i), 0, 0))
        outs = pl.BlockSpec((PAIR, slots, width), lambda s, i: (jnp.where(s < last, 0, i), 0, 0))
        layer_out, middle_grad, grad_b, grad_c, sums, _ = pl.pallas_call(
            functools.partial(feed_forward, narrow=narrow_size, beyond=beyond),
            grid=(narrow_size, pairs),
            in_specs=[smem] + [ends] * 3 + [vmem] * 5 + [anyspace] * 2,
            out_specs=[outs] * 2 + [anyspace, vmem, vmem, anyspace],
            input_output_aliases={10: 5},
            scratch_shapes=[
                pltpu.VMEM((width, width), F32),
                pltpu.VMEM((2, width, width), F32),
                pltpu.VMEM((2, width, width), BF16),
                pltpu.VMEM((2, width, width), BF16),
                pltpu.VMEM((pairs, rows, width), BF16),
                pltpu.VMEM((pairs, rows, width), BF16),
                pltpu.VMEM((pairs, rows, width), F32),
                pltpu.VMEM((pairs, rows, width), F32),
                pltpu.VMEM((width, width), F32),
            ]
            + Reduce.scratch(width, width, beyond)
            + [
                pltpu.SemaphoreType.DMA((2,)),
                pltpu.SemaphoreType.DMA((6 + beyond,)),
                pltpu.SemaphoreType.DMA((6 + beyond,)),
                pltpu.SemaphoreType.DMA((copies,)),
                pltpu.SemaphoreType.DMA((copies,)),
            ],
            out_shape=[
                struct(images, slots, width, dtype=BF16),
                struct(images, slots, width),
                struct(width, width),
                struct(width, width),
                struct(7, 8, width),
                struct(narrow_size - 1, width, width),
            ],
            compiler_params=remote_params(1),
            name="feed_forward",
        )(grid_shape, tokens, branch, cotangent, vec, small, up_weight, down_weight, slices, gath_b, gath_c)

        def first_pass(*shape):
            return pl.BlockSpec((PAIR,) + shape, lambda i: (jnp.minimum(i, pairs - 1),) + (0,) * len(shape))

        def second_pass(*shape, at=0):
            return pl.BlockSpec((PAIR,) + shape, lambda i: (jnp.maximum(i - pairs, 0), at) + (0,) * (len(shape) - 1))

        both_passes = pl.BlockSpec((PAIR, slots, width), lambda i: (i % pairs, 0, 0))
        total_rows = width + SMALL_ROWS
        vec = jnp.concatenate([row(v) for v in (attn_scale, first_gain, first_shift)])
        tokens_grad, total, grad_c, late = pl.pallas_call(
            functools.partial(attention_backward, beyond=beyond),
            grid=(2 * pairs,),
            in_specs=[smem, both_passes, both_passes]
            + [first_pass(slots, 256)] * 2
            + [first_pass(256, 256)] * 2
            + [first_pass(4, slots, 256)]
            + [second_pass(slots, width), second_pass(256, width), second_pass(256, width)]
            + [second_pass(4, slots, 256, at=1), second_pass(4, slots, 256, at=2)]
            + [vmem] * 4,
            out_specs=[second_pass(slots, width), anyspace, anyspace, vmem],
            scratch_shapes=[
                pltpu.VMEM((total_rows, width), F32),
                pltpu.VMEM((width, width), F32),
                pltpu.VMEM((total_rows, width), F32),
                pltpu.VMEM((pairs, rows, width), BF16),
                pltpu.VMEM((3, pairs, rows, 256), BF16),
                pltpu.VMEM((rows, width), BF16),
                pltpu.VMEM((rows, width), BF16),
                pltpu.VMEM((rows, width), BF16),
                pltpu.VMEM((len(GRIDS), 8, DIAG), F32),
                pltpu.VMEM((9, 8, 256), F32),
                pltpu.VMEM((2, 8, 256), F32),
                pltpu.VMEM((16, width), F32),
                pltpu.VMEM((SLICES - 1, 16, width), F32),
                pltpu.VMEM((2 * max(beyond, 1), 16, width), F32),
            ]
            + Reduce.scratch(width, width, beyond)
            + Reduce.scratch(total_rows, width, beyond)
            + [
                pltpu.SemaphoreType.DMA((2 * (6 + beyond),)),
                pltpu.SemaphoreType.DMA((2 * (6 + beyond),)),
                pltpu.SemaphoreType.DMA((SLICES - 1 + beyond,)),
                pltpu.SemaphoreType.DMA((SLICES - 1 + beyond,)),
                pltpu.SemaphoreType.DMA((2,)),
            ],
            out_shape=[
                struct(images, slots, width), struct(total_rows, width), struct(width, width), struct(16, width),
            ],
            compiler_params=remote_params(2),
            name="attention_backward",
        )(
            grid_shape, tokens, middle_grad, attended, queries, keys, values, probs, queries, keys, values, probs,
            probs, vec, weights_a, sums, grad_c,
        )

        parts = len(GRIDS)

        def image_block():
            return pl.BlockSpec((images // parts, slots, width), lambda i: (i, 0, 0))

        def row_block(total_rows=width):
            return pl.BlockSpec((total_rows // parts, width), lambda i: (i, 0))

        tokens_grad, layer_out, grad_b, grad_c, qkv_grad, proj_grad, square_grad = pl.pallas_call(
            finish,
            grid=(parts,),
            in_specs=[image_block(), image_block(), row_block(), row_block(), row_block(3 * local)]
            + [
                pl.BlockSpec((local // parts, width), lambda i: (3 * parts + i, 0)),
                pl.BlockSpec((SMALL_ROWS, width), lambda i: (width // SMALL_ROWS, 0)),
            ],
            out_specs=[image_block(), image_block(), row_block(), row_block(), row_block(3 * local), row_block(local), vmem],
            out_shape=[
                struct(images, slots, width), struct(images, slots, width, dtype=BF16), struct(width, width),
                struct(width, width), struct(3 * local, width), struct(local, width), struct(SPAN, 8, 128),
            ],
            compiler_params=params,
            name="finish",
        )(tokens_grad, layer_out, grad_b, grad_c, total, total, total)
        qkv_grad = jnp.transpose(qkv_grad.reshape(3, local, width), (0, 2, 1))
        square_grad = jnp.transpose(square_grad[:, :heads, :SPAN], (1, 0, 2))[:, ::-1, ::-1]
        edges = jnp.sum(total[width + 64 : width + 73, :256], axis=1).reshape(3, heads).T
        table_grad = jnp.concatenate([square_grad.reshape(heads, SPAN * SPAN), edges], axis=1)
        more = total[width + 80 : width + 82, :local]
        sums = total[width + 88 : width + 95]
        late = jnp.sum(late.reshape(2, 8, width), axis=1)
        return (
            layer_out,
            tokens_grad,
            late[0],
            late[1],
            qkv_grad,
            more[0],
            more[1],
            table_grad,
            proj_grad,
            sums[5] * attn_scale.astype(F32),
            sums[4],
            sums[2],
            sums[3],
            grad_b,
            sums[6],
            grad_c,
            sums[1] * mlp_scale.astype(F32),
            sums[0],
        )

    return body


def solution(mesh):
    rows = P("wide", None, None)
    return jax.shard_map(
        make_body(mesh.shape["wide"], mesh.shape["narrow"]),
        mesh=mesh,
        in_specs=(
            rows, P("wide", None), P(), P(), P(None, None, "narrow"), P("narrow"), P("narrow"), P("narrow", None),
            P("narrow", None), P(), P(), P(), P(), P(None, "narrow"), P("narrow"), P("narrow", None), P(), P(), rows,
        ),
        out_specs=(
            rows, rows, P(), P(), P(None, None, "narrow"), P("narrow"), P("narrow"), P("narrow", None),
            P("narrow", None), P(), P(), P(), P(), P(None, "narrow"), P("narrow"), P("narrow", None), P(), P(),
        ),
        check_vma=False,
    )
```
